512 devices in a mesh: dp: 64 (over y_lo, z, core), blk: 8 (over y_hi, x).
Axes of the slice: x: 4, y: 4 (y_hi: 2, y_lo: 2; y = y_hi * 2 + y_lo), z: 16, core: 2. Of those that a mesh axis runs over, the one named last changes fastest.
Arguments:
- resid: bfloat16 [2048, 2048], P('dp'), may hold values from -40 to 40
- queries: bfloat16 [2048, 16, 128], P('dp', 'blk'), may hold values from -60 to 60
- new_kv: bfloat16 [2048, 2, 8, 128], P('dp', None, 'blk'), may hold values from -6 to 6
- prefix_pool: bfloat16 [2048, 128, 2, 8, 128], P('dp', None, None, 'blk'), may hold values from -6 to 6
- page_table: int32 [64, 32], P('dp'), may hold values from 0 to 31, each once within a row
- prompt_len: int32 [64], P('dp'), may hold values from 1 to 4096, 131072 in all
- tail_pool: bfloat16 [1024, 128, 2, 8, 128], P('dp', None, None, 'blk'), may hold values from -6 to 6
- tail_len: int32 [64, 16], P('dp'), may hold values from 1 to 128, 1024 in all within a row
- migration: int32 [1024], replicated, may hold values from 0 to 1023, each once
- out_w: bfloat16 [2048, 2048], P('blk'), may hold values from -0.125 to 0.125
- mlp_gain: bfloat16 [2048], replicated, may hold values from 0.099609375 to 1.8984375
- gate_w: bfloat16 [2048, 6144], P('blk', 'dp'), may hold values from -0.125 to 0.125
- up_w: bfloat16 [2048, 6144], P('blk', 'dp'), may hold values from -0.125 to 0.125
- down_w: bfloat16 [6144, 2048], P('dp', 'blk'), may hold values from -0.078125 to 0.078125
- final_gain: bfloat16 [2048], P('blk'), may hold values from 0.099609375 to 1.8984375
- score_w: bfloat16 [2048], P('blk'), may hold values from -0.125 to 0.125
Outputs:
- hidden_out: bfloat16 [2048, 2048], P('dp', 'blk')
- score: float32 [2048], P('dp')
The draws below stay inside these ranges and needn't reach their ends.
Inputs may be any that keep to these rules, and one draw needn't show every extreme that they name: `page_table`: each row lists every page of the device's pool once. `migration`: names every continuation once.
All inputs are finite; a program needn't handle non-finite values. No bound on the sum of `prompt_len` on one device may be relied on, other than what follows from the above.
Results may differ from the reference program's by a relative error of at most 0.012.
Values may be sent and summed in bfloat16 or wider, within the bound.
A program may use at most 64 MiB of HBM per device.

```python
import math
import jax
import jax.numpy as jnp
import numpy as np
from jax import lax

D = 2048
HQ = 16
KVH = 8
HD = 128
FF = 6144
CONT = 16
NEW = 2
PAGE = 128
PAGES = 32
TAIL = 128
CONTS = 1024
TOKENS = 2048
N_DP = 64


def fresh_pairs(key):
    raw = jax.random.normal(jax.random.fold_in(key, 11), (CONTS, NEW, 2, KVH, HD), jnp.float32)
    return jnp.clip(raw, -6.0, 6.0)


def draw_new_kv(key, part):
    return fresh_pairs(key).reshape(TOKENS, 2, KVH, HD).astype(jnp.bfloat16)


def draw_queries(key, part):
    base = 2.0 * jax.random.normal(jax.random.fold_in(key, 21), (CONTS, NEW, KVH, HQ // KVH, HD), jnp.float32)
    return jnp.clip(base, -60.0, 60.0).reshape(TOKENS, HQ, HD).astype(jnp.bfloat16)


def draw_resid(key, part):
    place = jnp.arange(D).astype(jnp.float32) / D
    columns = jnp.exp(jax.random.uniform(jax.random.fold_in(key, 31), (D,), jnp.float32, math.log(0.5), math.log(1.5))) * (1.0 + 2.0 * place)
    scales = jnp.exp(jax.random.uniform(jax.random.fold_in(key, 32), (TOKENS, 1), jnp.float32, math.log(0.5), math.log(2.0)))
    raw = jax.random.normal(jax.random.fold_in(key, 33), (TOKENS, D), jnp.float32)
    return jnp.clip(raw * columns * scales, -40.0, 40.0).astype(jnp.bfloat16)


def level_of(key, shape, cuts, least, top_value):
    def one(dim, parts):
        heights = jax.random.uniform(jax.random.fold_in(jax.random.fold_in(key, 6), dim), (parts,), jnp.float32, least / len(cuts), top_value / len(cuts))
        return jnp.repeat(jnp.exp(heights), shape[dim] // parts).reshape((-1,) + (1,) * (len(shape) - dim - 1))

    level = one(*cuts[0])
    for cut in cuts[1:]:
        level = level * one(*cut)
    return level


def length_profile(count, total, reach, slope):
    weights = [(1 << 20) // math.isqrt(standing ** slope) + 1 for standing in range(2, count + 1)]
    surplus, holding = total - reach - (count - 1), [1] * (count - 1)
    while surplus > 0:
        free = [i for i in range(count - 1) if holding[i] < reach]
        whole, budget = sum([weights[i] for i in free]), surplus
        for i in free:
            addition = min(reach - holding[i], max(1, budget * weights[i] // whole), surplus)
            holding[i] = holding[i] + addition
            surplus = surplus - addition
    return np.array([reach] + holding)


def uneven(key, count, total, most, lean):
    if count == 2:
        one = jax.random.randint(key, (), max(1, total - most), min(most, total - 1) + 1)
        return jnp.stack([one, total - one])
    sizes = jnp.asarray(length_profile(count, total, most, lean), jnp.int32)
    couples = (count - 1) // 2
    giver, sink = sizes[1:1 + 2 * couples:2], sizes[2:2 + 2 * couples:2]
    slack = jnp.minimum(giver - 1, most - sink)
    shifted = jax.random.randint(jax.random.fold_in(key, 1), (couples,), 0, 1 << 20) % (slack + 1)
    sizes = sizes.at[1:1 + 2 * couples:2].set(giver - shifted).at[2:2 + 2 * couples:2].set(sink + shifted)
    return sizes[jax.random.permutation(jax.random.fold_in(key, 2), count)]


def gaussian(key, shape, scale, bound, split=(), kind=jnp.bfloat16):
    factor_of = level_of(key, shape, split, -0.22, 0.18) if split else 1.0
    entries = jax.random.normal(key, shape, jnp.float32) * scale * factor_of
    return jnp.minimum(jnp.maximum(entries, -bound), bound).astype(kind)


def setup_inputs(seed: int = 0) -> dict:
    arg_keys = jax.random.split(jax.random.key(seed), 17)
    return {
        "resid": draw_resid(jax.random.fold_in(arg_keys[16], 71), 0),
        "queries": draw_queries(jax.random.fold_in(arg_keys[16], 71), 0),
        "new_kv": draw_new_kv(jax.random.fold_in(arg_keys[16], 71), 0),
        "prefix_pool": gaussian(arg_keys[3], (N_DP * PAGES, PAGE, 2, KVH, HD), 1.0, 6.0, ((0, 64), (3, 8))),
        "page_table": jax.vmap(lambda own: jax.random.permutation(own, PAGES))(jax.random.split(arg_keys[4], N_DP)).reshape((N_DP, PAGES)).astype(jnp.int32),
        "prompt_len": uneven(arg_keys[5], N_DP, N_DP * PAGES * PAGE // 2, PAGES * PAGE, 2).astype(jnp.int32),
        "tail_pool": gaussian(arg_keys[6], (CONTS, TAIL, 2, KVH, HD), 1.0, 6.0, ((0, 64), (3, 8))),
        "tail_len": jax.vmap(lambda own: uneven(own, CONT, CONT * TAIL // 2, TAIL, 2))(jax.random.split(arg_keys[7], N_DP)).reshape((N_DP, CONT)).astype(jnp.int32),
        "migration": jax.random.permutation(arg_keys[8], CONTS).astype(jnp.int32),
        "out_w": gaussian(arg_keys[9], (HQ * HD, D), (HQ * HD) ** -0.5, 0.125, ((0, 8),)),
        "mlp_gain": jnp.clip(1.0 + 0.18 * jax.random.normal(arg_keys[10], (D,), jnp.float32), 0.099609375, 1.8984375).astype(jnp.bfloat16),
        "gate_w": gaussian(arg_keys[11], (D, FF), D ** -0.5, 0.125, ((0, 8), (1, 64))),
        "up_w": gaussian(arg_keys[12], (D, FF), D ** -0.5, 0.125, ((0, 8), (1, 64))),
        "down_w": gaussian(arg_keys[13], (FF, D), FF ** -0.5, 0.078125, ((0, 64), (1, 8))),
        "final_gain": jnp.clip(1.0 + 0.18 * jax.random.normal(arg_keys[14], (D,), jnp.float32), 0.099609375, 1.8984375).astype(jnp.bfloat16),
        "score_w": gaussian(arg_keys[15], (D,), D ** -0.5, 0.125, ((0, 8),)),
    }


NEG = -1e+30
EPS = 1e-06

def attend_prompt(queries, pool, table, prompt_len, tails, tail_len, pairs):
    token_rows, heads, width = queries.shape
    groups = pairs.shape[2]
    repeat = heads // groups
    conts = tails.shape[0]
    fresh = token_rows // conts
    prefix = jnp.take(pool, table, axis=0).reshape(-1, 2, groups, width).astype(jnp.float32)
    span = prefix.shape[0]
    grouped = queries.reshape(conts, fresh, groups, repeat, width).astype(jnp.float32)
    recent = pairs.reshape(conts, fresh, 2, groups, width).astype(jnp.float32)
    tail_vals = tails.astype(jnp.float32)
    factor = 1.0 / math.sqrt(width)
    pre_scores = jnp.einsum('cngrd,pgd->gcnrp', grouped, prefix[:, 0]) * factor
    tail_scores = jnp.einsum('cngrd,ctgd->gcnrt', grouped, tail_vals[:, :, 0]) * factor
    new_scores = jnp.einsum('cngrd,cmgd->gcnrm', grouped, recent[:, :, 0]) * factor
    pre_mask = (jnp.arange(span) < prompt_len)[None, None, None, None, :]
    tail_mask = (jnp.arange(tails.shape[1])[None, :] < tail_len[:, None])[None, :, None, None, :]
    new_mask = (jnp.arange(fresh)[None, :] <= jnp.arange(fresh)[:, None])[None, None, :, None, :]
    pre_scores = jnp.where(pre_mask, pre_scores, NEG)
    tail_scores = jnp.where(tail_mask, tail_scores, NEG)
    new_scores = jnp.where(new_mask, new_scores, NEG)
    highest = jnp.maximum(jnp.maximum(lax.optimization_barrier(jnp.max(pre_scores, -1)), lax.optimization_barrier(jnp.max(tail_scores, -1))), lax.optimization_barrier(jnp.max(new_scores, -1)))[..., None]
    pre_weights = jnp.where(pre_mask, jnp.exp(pre_scores - highest), 0.0)
    tail_weights = jnp.where(tail_mask, jnp.exp(tail_scores - highest), 0.0)
    new_weights = jnp.where(new_mask, jnp.exp(new_scores - highest), 0.0)
    total = lax.optimization_barrier(jnp.sum(pre_weights, -1)) + lax.optimization_barrier(jnp.sum(tail_weights, -1)) + lax.optimization_barrier(jnp.sum(new_weights, -1))
    pre_round = lax.optimization_barrier(pre_weights.astype(jnp.bfloat16)).astype(jnp.float32)
    tail_round = lax.optimization_barrier(tail_weights.astype(jnp.bfloat16)).astype(jnp.float32)
    new_round = lax.optimization_barrier(new_weights.astype(jnp.bfloat16)).astype(jnp.float32)
    mixed = jnp.einsum('gcnrp,pgd->cngrd', pre_round, prefix[:, 1])
    mixed = mixed + jnp.einsum('gcnrt,ctgd->cngrd', tail_round, tail_vals[:, :, 1])
    mixed = mixed + jnp.einsum('gcnrm,cmgd->cngrd', new_round, recent[:, :, 1])
    mixed = mixed / jnp.transpose(total, (1, 2, 0, 3))[..., None]
    return mixed.reshape(token_rows, heads * width).astype(jnp.bfloat16)

def reference(resid, queries, new_kv, prefix_pool, page_table, prompt_len, tail_pool, tail_len, migration, out_w, mlp_gain, gate_w, up_w, down_w, final_gain, score_w):
    per_dev = CONT * NEW
    grouped = queries.reshape(N_DP, per_dev, HQ, HD)
    pools = prefix_pool.reshape(N_DP, PAGES, PAGE, 2, KVH, HD)
    tails = tail_pool.reshape(N_DP, CONT, TAIL, 2, KVH, HD)
    pairs = new_kv.reshape(N_DP, per_dev, 2, KVH, HD)

    def one_prompt(items):
        return attend_prompt(items[0], items[1], items[2], items[3], items[4], items[5], items[6])
    attn = lax.map(one_prompt, (grouped, pools, page_table, prompt_len, tails, tail_len, pairs))
    attn = attn.reshape(TOKENS, HQ * HD)
    mid = resid.astype(jnp.float32) + jnp.dot(attn, out_w, preferred_element_type=jnp.float32)
    normed = (mid * lax.rsqrt(lax.optimization_barrier(jnp.mean(mid * mid, -1, keepdims=True)) + EPS) * mlp_gain.astype(jnp.float32)).astype(jnp.bfloat16)
    gate = jnp.dot(normed, gate_w, preferred_element_type=jnp.float32)
    upper = jnp.dot(normed, up_w, preferred_element_type=jnp.float32)
    hidden = (jax.nn.silu(gate) * upper).astype(jnp.bfloat16)
    after = mid + jnp.dot(hidden, down_w, preferred_element_type=jnp.float32)
    moved = after.reshape(CONTS, NEW, D)[migration].reshape(TOKENS, D)
    weighted = final_gain.astype(jnp.float32) * score_w.astype(jnp.float32)
    score = lax.optimization_barrier(jnp.sum(moved * weighted, -1)) * lax.rsqrt(lax.optimization_barrier(jnp.mean(moved * moved, -1)) + EPS)
    return (moved.astype(jnp.bfloat16), score)
```

```python
import functools
import math

import jax
import jax.numpy as jnp
from jax import lax
from jax.experimental import pallas as pl
from jax.experimental.pallas import tpu as pltpu
from jax.sharding import PartitionSpec as P

MESH = pl.DeviceIdType.MESH
F32 = jnp.float32
BF16 = jnp.bfloat16
NEG = -1e30
EPS = 1e-06
D = 2048
NB = 8
FB = 256
HOLD = 96
CONT = 16
PAGES = 32
HD = 128


def iota(shape, dim):
    return lax.broadcasted_iota(jnp.int32, shape, dim)


def dot(a, b):
    return lax.dot_general(a, b, (((1,), (0,)), ((), ())), preferred_element_type=F32)


def dot_nt(a, b):
    return lax.dot_general(a, b, (((1,), (1,)), ((), ())), preferred_element_type=F32)


def onehot(cond):
    return jnp.where(cond, 1.0, 0.0).astype(BF16)


def kernel(
    nz,
    radix,
    *refs,
):
    sources, (out_ref, score_ref), held, refs = refs[:16], refs[16:18], refs[18:34], refs[34:]
    (kv, tail, q_ref, new_ref, tab_ref, plen_ref, tlen_ref, down_ref, ow, resid_ref, mig_ref, gate_ref, up_ref, gain_ref, fg_ref, sw_ref) = held
    (limits, sbuf, wbuf, s2, r2, xall, perm, hs, gs, r4, auxs, r5, ms, r6, fs, r7, load_sem, w_ssem, w_rsem, wc_ssem, wc_rsem, s2_ssem, s2_rsem, z_ssem, z_rsem, y_ssem, y_rsem, c_ssem, c_rsem, s4_ssem, s4_rsem, s5_ssem, s5_rsem, s6_ssem, s6_rsem, s7_ssem, s7_rsem) = refs
    dp = lax.axis_index("dp")
    b = lax.axis_index("blk")
    c = lax.rem(dp, 2)
    z = lax.rem(lax.div(dp, 2), nz)
    y = lax.div(dp, 2 * nz)
    yc = 2 * y + c
    conts = 4 * nz * CONT
    rows = 2 * nz

    def dev(y_, z_, c_, b_):
        return ((y_ * nz + z_) * 2 + c_, b_)

    def remote(src, dst, ssem, rsem, target):
        return pltpu.make_async_remote_copy(
            src_ref=src, dst_ref=dst, send_sem=ssem, recv_sem=rsem, device_id=target, device_id_type=MESH
        )

    barrier = pltpu.get_barrier_semaphore()

    def greet_plane(k, _):
        other = lax.rem(b * 4 + yc + k, 32)
        oyc, ob = lax.rem(other, 4), lax.div(other, 4)
        pl.semaphore_signal(
            barrier, inc=1, device_id=dev(lax.div(oyc, 2), z, lax.rem(oyc, 2), ob), device_id_type=MESH
        )
        return 0

    def greet_line(k, _):
        pl.semaphore_signal(barrier, inc=1, device_id=dev(y, lax.rem(z + k, nz), c, b), device_id_type=MESH)
        return 0

    loads = [pltpu.make_async_copy(sources[i], held[i], load_sem.at[i]) for i in range(16)]
    for load in loads:
        load.start()

    lax.fori_loop(1, 32, greet_plane, 0)
    lax.fori_loop(1, nz, greet_line, 0)

    for load in loads[2:8]:
        load.wait()

    wbuf[yc, b] = down_ref[...]
    me16 = y * NB + b

    def w_copy(k):
        other = lax.rem(me16 + k, 16)
        return remote(
            wbuf.at[yc, b],
            wbuf.at[yc, b],
            w_ssem.at[k],
            w_rsem.at[k],
            dev(lax.div(other, NB), z, c, lax.rem(other, NB)),
        )

    def wc_copy(i):
        return remote(
            wbuf.at[2 * i + c], wbuf.at[2 * i + c], wc_ssem.at[i], wc_rsem.at[i], dev(y, z, 1 - c, b)
        )

    r64, c64 = iota((64, 64), 0), iota((64, 64), 1)
    q_src = (r64 % 16) * 4 + ((r64 // 16) % 2) * 2 + r64 // 32
    q = dot(onehot(q_src == c64), q_ref[...]).astype(BF16)

    pl.semaphore_wait(barrier, 31 + nz - 1)
    lax.fori_loop(1, 16, lambda k, _: (w_copy(k).start(), 0)[1], 0)

    lane = iota((64, 256), 1)
    even = lane % 2 == 0
    tok = lane // 2
    page_no = iota((PAGES, PAGES), 0) == jnp.broadcast_to(tab_ref[...], (PAGES, PAGES))
    logical = jnp.sum(jnp.where(page_no, iota((PAGES, PAGES), 1), 0), -1, keepdims=True)
    limits[...] = jnp.broadcast_to(plen_ref[0] - logical * 128, (PAGES, 256))
    factor = 1.0 / math.sqrt(HD)

    def page_rows(l):
        return kv[pl.ds(pl.multiple_of(l * 256, 256), 256), :]

    loads[0].wait()

    def scores(i, best):
        for u in range(4):
            l = i * 4 + u
            s = dot_nt(q, page_rows(l))
            s = jnp.where(even & (tok < limits[pl.ds(l, 1), :]), s, NEG)
            sbuf[:, pl.ds(pl.multiple_of(l * 256, 256), 256)] = s
            best = jnp.maximum(best, s)
        return best

    best = lax.fori_loop(0, PAGES // 4, scores, jnp.full((64, 256), NEG, F32))
    loads[1].wait()
    owner = iota((64, 256), 0) % 16

    def tail_scores(i, s_tail):
        for u in range(4):
            t = i * 4 + u
            s = dot_nt(q, tail[pl.ds(pl.multiple_of(t * 256, 256), 256), :])
            s_tail = jnp.where((owner == t) & even & (tok < tlen_ref[0, t]), s, s_tail)
        return s_tail

    s_tail = lax.fori_loop(0, CONT // 4, tail_scores, jnp.full((64, 256), NEG, F32))
    new_cont, new_tok = c64 // 4, (c64 // 2) % 2
    new_ok = (c64 % 2 == 0) & (new_cont == r64 % 16) & (new_tok <= (r64 // 16) % 2)
    s_new = jnp.where(new_ok, dot_nt(q, new_ref[...]), NEG)
    top = jnp.maximum(
        jnp.max(jnp.maximum(best, s_tail), -1, keepdims=True), jnp.max(s_new, -1, keepdims=True)
    )
    w_tail = jnp.exp((s_tail - top) * factor)
    w_new = jnp.exp((s_new - top) * factor)
    v_tail = pltpu.roll(w_tail, 1, 1)
    mixed = dot(pltpu.roll(w_new, 1, 1).astype(BF16), new_ref[...])

    def values(i, state):
        total, acc = state
        for u in range(4):
            l = i * 4 + u
            w = jnp.exp((sbuf[:, pl.ds(pl.multiple_of(l * 256, 256), 256)] - top) * factor)
            total = total + w
            acc = acc + dot(pltpu.roll(w, 1, 1).astype(BF16), page_rows(l))
        return total, acc

    total, mixed = lax.fori_loop(0, PAGES // 4, values, (w_tail, mixed))

    def tail_values(i, acc):
        for u in range(4):
            t = i * 4 + u
            w = jnp.where(owner == t, v_tail, 0.0).astype(BF16)
            acc = acc + dot(w, tail[pl.ds(pl.multiple_of(t * 256, 256), 256), :])
        return acc

    mixed = lax.fori_loop(0, CONT // 4, tail_values, mixed)
    total = jnp.sum(total, -1, keepdims=True) + jnp.sum(w_new, -1, keepdims=True)
    attn = (mixed / total).astype(BF16)

    loads[8].wait()
    for i in range(NB):
        cols = slice(i * FB, (i + 1) * FB)
        s2[i] = (dot(attn[:32], ow[:HD, cols]) + dot(attn[32:], ow[HD:, cols])).astype(BF16)

    def s2_copy(k):
        other = lax.rem(b + k, NB)
        return remote(s2.at[other], r2.at[k - 1], s2_ssem.at[k], s2_rsem.at[k], dev(y, z, c, other))

    lax.fori_loop(1, NB, lambda k, _: (s2_copy(k).start(), 0)[1], 0)

    for load in loads[9:]:
        load.wait()
    mig = mig_ref[...]
    home = mig // CONT
    stored = ((home // (2 * nz) * 2 + home % 2) * nz + (home // 2) % nz) * CONT + mig % CONT
    chunk = 4 * rows
    lines = mig.shape[0]
    p_row = iota((chunk, 1), 0)
    first = ((p_row // (2 * rows)) * nz + (p_row // 2) % nz) * 32 + ((p_row // rows) % 2) * 16 + p_row % 2
    line = onehot(iota((chunk, lines), 1) == first // 128)
    spread_mig = dot(line, (stored // 32).astype(F32).astype(BF16)) * 32.0 + dot(
        line, (stored % 32).astype(F32).astype(BF16)
    )
    slot_lane = iota((chunk, 128), 1) - first % 128
    for i in range(NB):
        column = jnp.sum(jnp.where(slot_lane == 2 * i, spread_mig, 0.0), -1, keepdims=True)
        perm[i] = onehot(iota((chunk, conts), 1) == column.astype(jnp.int32))
    gains = gain_ref[...].astype(F32)
    g_row = iota((16, 128), 0)
    gain = jnp.concatenate(
        [
            jnp.sum(jnp.where(g_row == 2 * b, gains, 0.0), 0, keepdims=True),
            jnp.sum(jnp.where(g_row == 2 * b + 1, gains, 0.0), 0, keepdims=True),
        ],
        1,
    )
    gate_t = (gate_ref[...].astype(F32) * gain).astype(BF16)
    up_t = (up_ref[...].astype(F32) * gain).astype(BF16)
    none32 = jnp.zeros((32, FB), BF16)
    none96 = jnp.zeros((96, FB), BF16)
    w_first = jnp.concatenate([gate_t, none32, up_t, none32], 0)
    w_second = jnp.concatenate(
        [none96, gate_t[:32], none96, up_t[:32], gate_t[32:], up_t[32:]], 0
    )
    r32, c32 = iota((32, 32), 0), iota((32, 32), 1)
    order = onehot((r32 % 16) * 2 + r32 // 16 == c32)
    resid = dot(order, resid_ref[:, pl.ds(pl.multiple_of(b * FB, FB), FB)])

    sel_r, sel_c = iota((128, NB * rows), 0), iota((128, NB * rows), 1)
    place = sel_r % 16
    own_rows = jnp.concatenate([perm[i, pl.ds(pl.multiple_of(yc * rows, rows), rows), :] for i in range(NB)], 0)
    sel = [
        dot(
            onehot(
                (place < 4)
                & (place % 2 == n)
                & (sel_c == (sel_r // 16) * rows + z * 2 + (place // 2) % 2)
            ),
            own_rows,
        ).astype(BF16)
        for n in range(2)
    ]

    lax.fori_loop(1, NB, lambda k, _: (s2_copy(k).wait_recv(), 0)[1], 0)
    mid = resid + s2[b].astype(F32)
    for k in range(1, NB):
        mid = mid + r2[k - 1].astype(F32)
    xall[0, yc, z] = mid[:16].astype(BF16)
    xall[1, yc, z] = mid[16:].astype(BF16)

    def z_copy(source, step, slot):
        piece = xall.at[:, yc, source]
        return remote(piece, piece, z_ssem.at[slot], z_rsem.at[slot], dev(y, lax.rem(z + step + nz, nz), c, b))

    def y_copy(source, slot):
        piece = xall.at[:, yc, source]
        return remote(piece, piece, y_ssem.at[slot], y_rsem.at[slot], dev(1 - y, z, c, b))

    def c_copy(i):
        piece = xall.at[:, 2 * i + c]
        return remote(piece, piece, c_ssem.at[i], c_rsem.at[i], dev(y, z, 1 - c, b))

    far = {1: nz // 2, -1: (nz - 1) // 2}
    z_waits = []

    def z_forward(way, stage):
        source = lax.rem(z - way * stage * radix + nz, nz)
        for j in range(1, radix + 1):
            dist = stage * radix + j
            if dist <= far[way]:
                copy = z_copy(source, way * j, (way * dist) % nz)
                copy.start()
                z_waits.append(copy)

    def z_arrived(way, dist):
        slot = (way * dist) % nz
        z_copy(z, 0, slot).wait_recv()
        return lax.rem(z - way * dist + nz, nz)

    z_forward(1, 0)
    z_forward(-1, 0)
    y_waits = [y_copy(z, 0)]
    y_waits[0].start()
    for dist in range(1, nz // 2 + 1):
        for way in (1, -1):
            if dist <= far[way]:
                source = z_arrived(way, dist)
                if dist % radix == 0:
                    z_forward(way, dist // radix)
                copy = y_copy(source, (way * dist) % nz)
                copy.start()
                y_waits.append(copy)
    c_copy(y).start()
    for copy in y_waits:
        copy.wait_recv()
    c_copy(1 - y).start()

    lax.fori_loop(1, 16, lambda k, _: (w_copy(k).wait_recv(), 0)[1], 0)
    wc_copy(0).start()
    wc_copy(1).start()

    c_copy(0).wait_recv()
    c_copy(1).wait_recv()

    x0 = xall[0].reshape(conts, FB)
    x1 = xall[1].reshape(conts, FB)
    h1 = dot_nt(x1, w_second)
    hs[:, :256] = (dot_nt(x0, w_first) + h1[:, :256]).astype(BF16)
    hs[:, 256:384] = h1[:, 256:].astype(BF16)
    e_lane = iota((FB, 128), 1)
    sq0 = (x0.astype(F32) * x0.astype(F32)).astype(BF16)
    sq1 = (x1.astype(F32) * x1.astype(F32)).astype(BF16)
    squares = dot(sq0, onehot((e_lane == 0) | (e_lane == 2))) + dot(sq1, onehot((e_lane == 1) | (e_lane == 3)))
    high = squares.astype(BF16).astype(F32)
    hs[:, 384:] = jnp.where(iota((conts, 128), 1) < 2, high, squares - high).astype(BF16)

    res = dot(sel[0], x0) + dot(sel[1], x1)
    fg = fg_ref[...].astype(F32)
    sw = sw_ref[...].astype(F32)
    a_row = iota((128, FB), 0) % 16
    res = jnp.where(a_row == 4, jnp.concatenate([fg[0:1], fg[1:2]], 1), res)
    res = jnp.where(a_row == 5, jnp.concatenate([sw[0:1], sw[1:2]], 1), res).astype(BF16)
    for i in range(NB):
        auxs[i, rows : rows + 16, :] = res[i * 16 : (i + 1) * 16]

    def s4_copy(i, j):
        ob, oyc = lax.rem(b + i, NB), lax.rem(yc + j, 4)
        return remote(
            gs.at[ob, oyc],
            r4.at[yc, b],
            s4_ssem.at[i * 4 + j],
            s4_rsem.at[i * 4 + j],
            dev(lax.div(oyc, 2), z, lax.rem(oyc, 2), ob),
        )

    def s5_copy(i):
        ob = lax.rem(b + i, NB)
        return remote(auxs.at[ob], r5.at[b], s5_ssem.at[i], s5_rsem.at[i], dev(y, z, c, ob))

    def serve(i):
        ob = lax.rem(b + i, NB)
        g = dot(perm[ob], hs[...]).astype(BF16)
        gs[ob] = g[:, :384].reshape(4, rows, 384)
        return ob, g[:, 384:].reshape(4, rows, 128)

    def aux_rows(ob, squares4):
        pick = jnp.zeros((rows, 128), BF16)
        for i in range(4):
            pick = jnp.where(yc == i, squares4[i], pick)
        auxs[ob, :rows, :128] = pick
        auxs[ob, :rows, 128:] = jnp.zeros((rows, 128), BF16)

    def serve_send(i, _):
        ob, squares4 = serve(i)
        for j in range(4):
            s4_copy(i, j).start()
        aux_rows(ob, squares4)
        s5_copy(i).start()
        return 0

    lax.fori_loop(1, NB, serve_send, 0)
    ob, squares4 = serve(0)
    for j in range(1, 4):
        s4_copy(0, j).start()
    aux_rows(ob, squares4)
    r4[yc, b] = gs[b, yc]
    r5[b] = auxs[b]

    lax.fori_loop(1, NB, lambda k, _: (s5_copy(k).wait_recv(), 0)[1], 0)
    stats = r5[0, :rows, :128].astype(F32)
    for i in range(1, NB):
        stats = stats + r5[i, :rows, :128].astype(F32)
    l128 = iota((rows, 128), 1)

    def inverse_rms(n):
        picked = jnp.where(l128 % 2 == n, jnp.where(l128 < 4, stats, 0.0), 0.0)
        return lax.rsqrt(jnp.sum(picked, -1, keepdims=True) / D + EPS)

    scale0, scale1 = inverse_rms(0), inverse_rms(1)
    scale_ab = jnp.where(l128 < 96, scale0, scale1)

    lax.fori_loop(1, 32, lambda k, _: (s4_copy(lax.div(k, 4), lax.rem(k, 4)).wait_recv(), 0)[1], 0)

    def silu(v):
        return v / (1.0 + jnp.exp(-v))

    mr, mc = iota((nz * 16, 2 * rows), 0), iota((nz * 16, 2 * rows), 1)
    m_in = mr % 4
    m_src = (m_in % 2) * rows + (mr // 16) * 2 + m_in // 2
    spread = [onehot((mc == m_src) & ((mr // 4) % 4 == j)) for j in range(4)]

    def hidden(g):
        acc = r4[g, 0].astype(F32)
        for i in range(1, NB):
            acc = acc + r4[g, i].astype(F32)
        h_ab = silu(acc[:, :128] * scale_ab) * (acc[:, 128:256] * scale_ab)
        last = acc[:, 256:] * scale1
        h_c = silu(last) * pltpu.roll(last, 64, 1)
        h_one = jnp.where(l128 < 32, pltpu.roll(h_ab, 32, 1), pltpu.roll(h_c, 32, 1))
        return jnp.concatenate([h_ab, h_one], 0).astype(BF16)

    hids = [hidden(g) for g in range(4)]
    wc_copy(0).wait_recv()
    wc_copy(1).wait_recv()
    left = jnp.zeros((nz * 16, FB), F32)
    right = jnp.zeros((nz * 16, FB), F32)
    for g in range(4):
        for j in range(4):
            lhs = dot(spread[j], hids[g]).astype(BF16)[:, :HOLD]
            left = left + dot(lhs, wbuf[g, 2 * j])
            right = right + dot(lhs, wbuf[g, 2 * j + 1])
    ms[:, :, :FB] = left.astype(BF16).reshape(nz, 16, FB)
    ms[:, :, FB:] = right.astype(BF16).reshape(nz, 16, FB)

    def s6_copy(k):
        other = lax.rem(z + k, nz)
        return remote(ms.at[other], r6.at[z], s6_ssem.at[k], s6_rsem.at[k], dev(y, other, c, b))

    lax.fori_loop(1, nz, lambda k, _: (s6_copy(k).start(), 0)[1], 0)
    r6[z] = ms[z]

    def gathered(pick):
        return jnp.concatenate(
            [jnp.concatenate([pick(2 * j), pick(2 * j + 1)], 1) for j in range(4)], 0
        )

    resid4 = gathered(lambda i: r5[i, rows : rows + 16, :].astype(F32)[0:4])
    weight4 = gathered(
        lambda i: jnp.broadcast_to(
            r5[i, rows : rows + 16, :].astype(F32)[4:5] * r5[i, rows : rows + 16, :].astype(F32)[5:6], (4, FB)
        )
    )

    lax.fori_loop(1, nz, lambda k, _: (s6_copy(k).wait_recv(), 0)[1], 0)
    moved = resid4
    for k in range(nz):
        moved = moved + r6[k].astype(F32)
    ss = jnp.sum(moved * moved, -1, keepdims=True)
    st = jnp.sum(moved * weight4, -1, keepdims=True)
    ss = ss[0:4] + ss[4:8] + ss[8:12] + ss[12:16]
    st = st[0:4] + st[4:8] + st[8:12] + st[12:16]
    score = jnp.broadcast_to(st * lax.rsqrt(ss / D + EPS), (4, FB))
    for i in range(NB):
        j, half = i // 2, i % 2
        fs[i] = jnp.concatenate([moved[4 * j : 4 * j + 4, half * FB : (half + 1) * FB], score], 0)

    def s7_copy(k):
        other = lax.rem(b + k, NB)
        return remote(fs.at[other], r7.at[b], s7_ssem.at[k], s7_rsem.at[k], dev(y, z, c, other))

    lax.fori_loop(1, NB, lambda k, _: (s7_copy(k).start(), 0)[1], 0)
    r7[b] = fs[b]

    lax.fori_loop(1, 16, lambda k, _: (w_copy(k).wait_send(), 0)[1], 0)
    wc_copy(0).wait_send()
    wc_copy(1).wait_send()
    lax.fori_loop(1, NB, lambda k, _: (s2_copy(k).wait_send(), 0)[1], 0)
    for copy in z_waits + y_waits:
        copy.wait_send()
    c_copy(0).wait_send()
    c_copy(1).wait_send()
    lax.fori_loop(1, 32, lambda k, _: (s4_copy(lax.div(k, 4), lax.rem(k, 4)).wait_send(), 0)[1], 0)
    lax.fori_loop(1, NB, lambda k, _: (s5_copy(k).wait_send(), 0)[1], 0)
    lax.fori_loop(1, nz, lambda k, _: (s6_copy(k).wait_send(), 0)[1], 0)

    lax.fori_loop(1, NB, lambda k, _: (s7_copy(k).wait_recv(), 0)[1], 0)
    final = jnp.concatenate([r7[i][:4] for i in range(NB)], 0)
    out_ref[...] = final.astype(BF16)
    col = jnp.concatenate([r7[i][4:, :32] for i in range(NB)], 0)
    score_ref[...] = jnp.sum(jnp.where(r32 == c32, col, 0.0), 0, keepdims=True)
    lax.fori_loop(1, NB, lambda k, _: (s7_copy(k).wait_send(), 0)[1], 0)


def shards(
    nz,
    resid,
    queries,
    new_kv,
    prefix_pool,
    page_table,
    prompt_len,
    tail_pool,
    tail_len,
    migration,
    out_w,
    mlp_gain,
    gate_w,
    up_w,
    down_w,
    final_gain,
    score_w,
):
    conts = 4 * nz * CONT
    rows = 2 * nz
    vmem = pl.BlockSpec(memory_space=pltpu.VMEM)
    hbm = pl.BlockSpec(memory_space=pl.ANY)
    dma = pltpu.SemaphoreType.DMA
    out, score = pl.pallas_call(
        functools.partial(kernel, nz, 4),
        out_shape=(
            jax.ShapeDtypeStruct((32, FB), BF16),
            jax.ShapeDtypeStruct((1, 32), F32),
        ),
        in_specs=[hbm] * 16,
        out_specs=(vmem, vmem),
        scratch_shapes=[
            pltpu.VMEM((PAGES * 256, HD), BF16),
            pltpu.VMEM((CONT * 256, HD), BF16),
            pltpu.VMEM((64, HD), BF16),
            pltpu.VMEM((64, HD), BF16),
            pltpu.VMEM((1, PAGES), jnp.int32),
            pltpu.SMEM((1,), jnp.int32),
            pltpu.SMEM((1, CONT), jnp.int32),
            pltpu.VMEM((HOLD, FB), BF16),
            pltpu.VMEM((2 * HD, D), BF16),
            pltpu.VMEM((32, D), BF16),
            pltpu.VMEM((conts // 128, 128), jnp.int32),
            pltpu.VMEM((HOLD, FB), BF16),
            pltpu.VMEM((HOLD, FB), BF16),
            pltpu.VMEM((16, 128), BF16),
            pltpu.VMEM((2, 128), BF16),
            pltpu.VMEM((2, 128), BF16),
            pltpu.VMEM((PAGES, 256), jnp.int32),
            pltpu.VMEM((64, PAGES * 256), F32),
            pltpu.VMEM((4, NB, HOLD, FB), BF16),
            pltpu.VMEM((NB, 32, FB), BF16),
            pltpu.VMEM((NB - 1, 32, FB), BF16),
            pltpu.VMEM((2, 4, nz, CONT, FB), BF16),
            pltpu.VMEM((NB, 4 * rows, conts), BF16),
            pltpu.VMEM((conts, 512), BF16),
            pltpu.VMEM((NB, 4, rows, 384), BF16),
            pltpu.VMEM((4, NB, rows, 384), BF16),
            pltpu.VMEM((NB, rows + 16, FB), BF16),
            pltpu.VMEM((NB, rows + 16, FB), BF16),
            pltpu.VMEM((nz, 16, 512), BF16),
            pltpu.VMEM((nz, 16, 512), BF16),
            pltpu.VMEM((NB, 8, FB), F32),
            pltpu.VMEM((NB, 8, FB), F32),
            dma((16,)),
            dma((16,)),
            dma((16,)),
            dma((2,)),
            dma((2,)),
            dma((NB,)),
            dma((NB,)),
            dma((nz,)),
            dma((nz,)),
            dma((nz,)),
            dma((nz,)),
            dma((2,)),
            dma((2,)),
            dma((32,)),
            dma((32,)),
            dma((NB,)),
            dma((NB,)),
            dma((nz,)),
            dma((nz,)),
            dma((NB,)),
            dma((NB,)),
        ],
        compiler_params=pltpu.CompilerParams(
            collective_id=0, has_side_effects=True, vmem_limit_bytes=58 * 1024 * 1024
        ),
    )(
        prefix_pool.reshape(PAGES * 256, HD),
        tail_pool.reshape(CONT * 256, HD),
        queries.reshape(64, HD),
        new_kv.reshape(64, HD),
        page_table,
        prompt_len,
        tail_len,
        down_w,
        out_w,
        resid,
        migration.reshape(conts // 128, 128),
        gate_w.T,
        up_w.T,
        mlp_gain.reshape(16, 128),
        final_gain.reshape(2, 128),
        score_w.reshape(2, 128),
    )
    return out, score.reshape(32)


def solution(mesh):
    nz = mesh.shape["dp"] // 4
    return jax.shard_map(
        functools.partial(shards, nz),
        mesh=mesh,
        in_specs=(
            P("dp", None),
            P("dp", "blk", None),
            P("dp", None, "blk", None),
            P("dp", None, None, "blk", None),
            P("dp", None),
            P("dp"),
            P("dp", None, None, "blk", None),
            P("dp", None),
            P(),
            P("blk", None),
            P(),
            P("blk", "dp"),
            P("blk", "dp"),
            P("dp", "blk"),
            P("blk"),
            P("blk"),
        ),
        out_specs=(P("dp", "blk"), P("dp")),
        check_vma=False,
    )
```

```python
import functools
import math

import jax
import jax.numpy as jnp
from jax import lax
from jax.experimental import pallas as pl
from jax.experimental.pallas import tpu as pltpu
from jax.sharding import PartitionSpec as P

MESH = pl.DeviceIdType.MESH
F32 = jnp.float32
BF16 = jnp.bfloat16
NEG = -1e30
EPS = 1e-06
D = 2048
NB = 8
FB = 256
HOLD = 96
CONT = 16
PAGES = 32
HD = 128
TREE = ((0, (5, 2, 1)), (2, (4, 3)), (5, (8, 7, 6)))


def iota(shape, dim):
    return lax.broadcasted_iota(jnp.int32, shape, dim)


def dot(a, b):
    return lax.dot_general(a, b, (((1,), (0,)), ((), ())), preferred_element_type=F32)


def dot_nt(a, b):
    return lax.dot_general(a, b, (((1,), (1,)), ((), ())), preferred_element_type=F32)


def onehot(cond):
    return jnp.where(cond, 1.0, 0.0).astype(BF16)


def kernel(
    nz,
    *refs,
):
    sources, out_ref, held, refs = refs[:16], refs[16], refs[17:33], refs[33:]
    (kv, tail, q_ref, new_ref, tab_ref, plen_ref, tlen_ref, down_ref, ow, resid_ref, mig_ref, gate_ref, up_ref, gain_ref, fg_ref, sw_ref) = held
    (bias, sbuf, wbuf, s2, r2, xall, perm, sel, hs, gs, r4, auxs, r5, ms, ags, r6, fs, r7, load_sem, w_ssem, w_rsem, wc_ssem, wc_rsem, s2_ssem, s2_rsem, z_ssem, z_rsem, y_ssem, y_rsem, c_ssem, c_rsem, s4_ssem, s4_rsem, s5_ssem, s5_rsem, s6_ssem, s6_rsem, s7_ssem, s7_rsem) = refs
    dp = lax.axis_index("dp")
    b = lax.axis_index("blk")
    c = lax.rem(dp, 2)
    z = lax.rem(lax.div(dp, 2), nz)
    y = lax.div(dp, 2 * nz)
    yc = 2 * y + c
    conts = 4 * nz * CONT
    rows = 2 * nz

    def dev(y_, z_, c_, b_):
        return ((y_ * nz + z_) * 2 + c_, b_)

    def remote(src, dst, ssem, rsem, target):
        return pltpu.make_async_remote_copy(
            src_ref=src, dst_ref=dst, send_sem=ssem, recv_sem=rsem, device_id=target, device_id_type=MESH
        )

    barrier = pltpu.get_barrier_semaphore()

    def greet_plane(k, _):
        other = lax.rem(b * 4 + yc + k, 32)
        oyc, ob = lax.rem(other, 4), lax.div(other, 4)
        pl.semaphore_signal(
            barrier, inc=1, device_id=dev(lax.div(oyc, 2), z, lax.rem(oyc, 2), ob), device_id_type=MESH
        )
        return 0

    def greet_line(k, _):
        pl.semaphore_signal(barrier, inc=1, device_id=dev(y, lax.rem(z + k, nz), c, b), device_id_type=MESH)
        return 0

    loads = [pltpu.make_async_copy(sources[i], held[i], load_sem.at[i]) for i in range(16)]
    for load in loads:
        load.start()

    lax.fori_loop(1, 32, greet_plane, 0)
    lax.fori_loop(1, nz, greet_line, 0)

    for load in loads[2:8]:
        load.wait()

    wbuf[yc, b] = down_ref[...]
    me16 = y * NB + b

    def w_copy(k):
        other = lax.rem(me16 + k, 16)
        return remote(
            wbuf.at[yc, b],
            wbuf.at[yc, b],
            w_ssem.at[k],
            w_rsem.at[k],
            dev(lax.div(other, NB), z, c, lax.rem(other, NB)),
        )

    def wc_copy(i):
        return remote(
            wbuf.at[2 * i + c], wbuf.at[2 * i + c], wc_ssem.at[i], wc_rsem.at[i], dev(y, z, 1 - c, b)
        )

    r64, c64 = iota((64, 64), 0), iota((64, 64), 1)
    q_src = (r64 % 16) * 4 + ((r64 // 16) % 2) * 2 + r64 // 32
    q = dot(onehot(q_src == c64), q_ref[...]).astype(BF16)

    lane = iota((PAGES, 256), 1)
    page_no = iota((PAGES, PAGES), 0) == jnp.broadcast_to(tab_ref[...], (PAGES, PAGES))
    logical = jnp.sum(jnp.where(page_no, iota((PAGES, PAGES), 1), 0), -1, keepdims=True)
    limit = jnp.broadcast_to(plen_ref[0] - logical * 128, (PAGES, 256))
    bias[...] = jnp.where((lane % 2 == 0) & (lane // 2 < limit), 0.0, NEG)
    unit = math.log2(math.e) / math.sqrt(HD)

    def widest(best, s):
        for i in range(s.shape[1] // 128):
            best = jnp.maximum(best, s[:, i * 128 : (i + 1) * 128])
        return best

    def next_lane(w):
        return jnp.concatenate(
            [pltpu.roll(w[:, i * 128 : (i + 1) * 128], 1, 1) for i in range(w.shape[1] // 128)], 1
        ).astype(BF16)

    loads[0].wait()
    best = jnp.full((64, 128), NEG, F32)
    for i in range(PAGES // 8):
        s = dot_nt(q, kv[i * 2048 : (i + 1) * 2048, :])
        for u in range(8):
            l = i * 8 + u
            part = s[:, u * 256 : (u + 1) * 256] + bias[l : l + 1, :]
            sbuf[:, l * 256 : (l + 1) * 256] = part
            best = widest(best, part)
    loads[1].wait()
    owner = iota((64, 256), 0) % 16
    t_lane = iota((1, 256), 1)
    s_tail = jnp.full((64, 256), NEG, F32)
    for i in range(CONT // 8):
        s = dot_nt(q, tail[i * 2048 : (i + 1) * 2048, :])
        for u in range(8):
            t = i * 8 + u
            t_bias = jnp.where((t_lane % 2 == 0) & (t_lane // 2 < tlen_ref[0, t]), 0.0, NEG)
            s_tail = jnp.where(owner == t, s[:, u * 256 : (u + 1) * 256] + t_bias, s_tail)

    pl.semaphore_wait(barrier, 31 + nz - 1)
    lax.fori_loop(1, 16, lambda k, _: (w_copy(k).start(), 0)[1], 0)

    new_cont, new_tok = c64 // 4, (c64 // 2) % 2
    new_ok = (c64 % 2 == 0) & (new_cont == r64 % 16) & (new_tok <= (r64 // 16) % 2)
    s_new = jnp.where(new_ok, dot_nt(q, new_ref[...]), NEG)
    top = jnp.maximum(
        jnp.max(widest(best, s_tail), -1, keepdims=True), jnp.max(s_new, -1, keepdims=True)
    )
    w_tail = jnp.exp2((s_tail - top) * unit)
    w_new = jnp.exp2((s_new - top) * unit)
    total = w_tail[:, :128] + w_tail[:, 128:]
    mixed = dot(pltpu.roll(w_new, 1, 1).astype(BF16), new_ref[...])
    for i in range(PAGES // 8):
        w = jnp.exp2((sbuf[:, i * 2048 : (i + 1) * 2048] - top) * unit)
        for u in range(16):
            total = total + w[:, u * 128 : (u + 1) * 128]
        mixed = mixed + dot(next_lane(w), kv[i * 2048 : (i + 1) * 2048, :])
    v_tail = next_lane(w_tail)
    for i in range(CONT // 8):
        w = jnp.concatenate(
            [jnp.where(owner == i * 8 + u, v_tail, jnp.zeros_like(v_tail)) for u in range(8)], 1
        )
        mixed = mixed + dot(w, tail[i * 2048 : (i + 1) * 2048, :])
    total = jnp.sum(total, -1, keepdims=True) + jnp.sum(w_new, -1, keepdims=True)
    attn = (mixed / total).astype(BF16)

    loads[8].wait()
    for i in range(NB):
        cols = slice(i * FB, (i + 1) * FB)
        s2[i] = (dot(attn[:32], ow[:HD, cols]) + dot(attn[32:], ow[HD:, cols])).astype(BF16)

    def s2_copy(k):
        other = lax.rem(b + k, NB)
        return remote(s2.at[other], r2.at[k - 1], s2_ssem.at[k], s2_rsem.at[k], dev(y, z, c, other))

    lax.fori_loop(1, NB, lambda k, _: (s2_copy(k).start(), 0)[1], 0)

    for load in loads[9:]:
        load.wait()
    mig = mig_ref[...]
    home = mig // CONT
    stored = ((home // (2 * nz) * 2 + home % 2) * nz + (home // 2) % nz) * CONT + mig % CONT
    chunk = 4 * rows
    lines = mig.shape[0]
    p_row = iota((chunk, 1), 0)
    first = ((p_row // (2 * rows)) * nz + (p_row // 2) % nz) * 32 + ((p_row // rows) % 2) * 16 + p_row % 2
    line = onehot(iota((chunk, lines), 1) == first // 128)
    spread_mig = dot(line, (stored // 32).astype(F32).astype(BF16)) * 32.0 + dot(
        line, (stored % 32).astype(F32).astype(BF16)
    )
    slot_lane = iota((chunk, 128), 1) - first % 128
    for i in range(NB):
        column = jnp.sum(jnp.where(slot_lane == 2 * i, spread_mig, 0.0), -1, keepdims=True)
        perm[i] = onehot(iota((chunk, conts), 1) == column.astype(jnp.int32))
    gains = gain_ref[...].astype(F32)
    g_row = iota((16, 128), 0)
    gain = jnp.concatenate(
        [
            jnp.sum(jnp.where(g_row == 2 * b, gains, 0.0), 0, keepdims=True),
            jnp.sum(jnp.where(g_row == 2 * b + 1, gains, 0.0), 0, keepdims=True),
        ],
        1,
    )
    gate_t = (gate_ref[...].astype(F32) * gain).astype(BF16)
    up_t = (up_ref[...].astype(F32) * gain).astype(BF16)
    none32 = jnp.zeros((32, FB), BF16)
    none96 = jnp.zeros((96, FB), BF16)
    w_first = jnp.concatenate([gate_t, none32, up_t, none32], 0)
    w_second = jnp.concatenate(
        [none96, gate_t[:32], none96, up_t[:32], gate_t[32:], up_t[32:]], 0
    )
    r32, c32 = iota((32, 32), 0), iota((32, 32), 1)
    order = onehot((r32 % 16) * 2 + r32 // 16 == c32)
    resid = dot(order, resid_ref[:, pl.ds(pl.multiple_of(b * FB, FB), FB)])

    sel_r, sel_c = iota((128, NB * rows), 0), iota((128, NB * rows), 1)
    place = sel_r % 16
    own_rows = jnp.concatenate([perm[i, pl.ds(pl.multiple_of(yc * rows, rows), rows), :] for i in range(NB)], 0)
    for n in range(2):
        picked = dot(
            onehot(
                (place < 4)
                & (place % 2 == n)
                & (sel_c == (sel_r // 16) * rows + z * 2 + (place // 2) % 2)
            ),
            own_rows,
        ).astype(BF16)
        for i in range(4):
            sel[n, i] = picked[:, i * nz * CONT : (i + 1) * nz * CONT]

    lax.fori_loop(1, NB, lambda k, _: (s2_copy(k).wait_recv(), 0)[1], 0)
    mid = resid + s2[b].astype(F32)
    for k in range(1, NB):
        mid = mid + r2[k - 1].astype(F32)
    xall[0, yc, z] = mid[:16].astype(BF16)
    xall[1, yc, z] = mid[16:].astype(BF16)

    def z_copy(source, step, slot):
        piece = xall.at[:, yc, source]
        return remote(piece, piece, z_ssem.at[slot], z_rsem.at[slot], dev(y, lax.rem(z + step + nz, nz), c, b))

    def y_copy(source, slot):
        piece = xall.at[:, yc, source]
        return remote(piece, piece, y_ssem.at[slot], y_rsem.at[slot], dev(1 - y, z, c, b))

    def c_copy(i):
        piece = xall.at[:, 2 * i + c]
        return remote(piece, piece, c_ssem.at[i], c_rsem.at[i], dev(y, z, 1 - c, b))

    far = {1: nz // 2, -1: (nz - 1) // 2}
    z_waits, y_waits = [], []

    def z_forward(way, parent, kids):
        source = lax.rem(z - way * parent + nz, nz)
        for kid in kids:
            if kid <= far[way]:
                copy = z_copy(source, way * (kid - parent), (way * kid) % nz)
                copy.start()
                z_waits.append(copy)

    def y_forward(way, dist):
        slot = (way * dist) % nz
        copy = y_copy(lax.rem(z - way * dist + nz, nz), slot)
        copy.start()
        y_waits.append(copy)

    for way in (1, -1):
        z_forward(way, *TREE[0])
    y_forward(1, 0)
    kids_of = dict(TREE)
    for dist in (2, 5, 1, 4, 3, 6, 7, 8):
        for way in (1, -1):
            if dist <= far[way]:
                z_copy(z, 0, (way * dist) % nz).wait_recv()
                if dist in kids_of:
                    z_forward(way, dist, kids_of[dist])
                y_forward(way, dist)

    e_lane = iota((FB, 128), 1)
    e_first = onehot((e_lane == 0) | (e_lane == 2))
    e_second = onehot((e_lane == 1) | (e_lane == 3))

    def project(block, res):
        x0 = xall[0, block].reshape(nz * CONT, FB)
        x1 = xall[1, block].reshape(nz * CONT, FB)
        h1 = dot_nt(x1, w_second)
        hs[block, :, :256] = (dot_nt(x0, w_first) + h1[:, :256]).astype(BF16)
        hs[block, :, 256:384] = h1[:, 256:].astype(BF16)
        sq0 = (x0.astype(F32) * x0.astype(F32)).astype(BF16)
        sq1 = (x1.astype(F32) * x1.astype(F32)).astype(BF16)
        squares = dot(sq0, e_first) + dot(sq1, e_second)
        high = squares.astype(BF16).astype(F32)
        hs[block, :, 384:] = jnp.where(iota((nz * CONT, 128), 1) < 2, high, squares - high).astype(BF16)
        return res + dot(sel[0, block], x0) + dot(sel[1, block], x1)

    c_copy(y).start()
    res = project(yc, jnp.zeros((128, FB), F32))
    c_copy(y).wait_recv()
    res = project(2 * y + 1 - c, res)
    for copy in y_waits:
        copy.wait_recv()
    c_copy(1 - y).start()
    res = project(2 * (1 - y) + c, res)

    lax.fori_loop(1, 16, lambda k, _: (w_copy(k).wait_recv(), 0)[1], 0)
    wc_copy(0).start()
    wc_copy(1).start()

    c_copy(1 - y).wait_recv()
    res = project(2 * (1 - y) + 1 - c, res)

    fg = fg_ref[...].astype(F32)
    sw = sw_ref[...].astype(F32)
    a_row = iota((128, FB), 0) % 16
    res = jnp.where(a_row == 4, jnp.concatenate([fg[0:1], fg[1:2]], 1), res)
    res = jnp.where(a_row == 5, jnp.concatenate([sw[0:1], sw[1:2]], 1), res).astype(BF16)
    for i in range(NB):
        auxs[i, rows : rows + 16, :] = res[i * 16 : (i + 1) * 16]

    def s4_copy(i, j):
        ob, oyc = lax.rem(b + i, NB), lax.rem(yc + j, 4)
        return remote(
            gs.at[ob, oyc],
            r4.at[yc, b],
            s4_ssem.at[i * 4 + j],
            s4_rsem.at[i * 4 + j],
            dev(lax.div(oyc, 2), z, lax.rem(oyc, 2), ob),
        )

    def s5_copy(i):
        ob = lax.rem(b + i, NB)
        return remote(auxs.at[ob], r5.at[b], s5_ssem.at[i], s5_rsem.at[i], dev(y, z, c, ob))

    def serve(i):
        ob = lax.rem(b + i, NB)
        g = dot(perm[ob], hs[...].reshape(conts, 512)).astype(BF16)
        gs[ob] = g[:, :384].reshape(4, rows, 384)
        return ob, g[:, 384:].reshape(4, rows, 128)

    def aux_rows(ob, squares4):
        pick = jnp.zeros((rows, 128), BF16)
        for i in range(4):
            pick = jnp.where(yc == i, squares4[i], pick)
        auxs[ob, :rows, :128] = pick
        auxs[ob, :rows, 128:] = jnp.zeros((rows, 128), BF16)

    def serve_send(i, _):
        ob, squares4 = serve(i)
        for j in range(4):
            s4_copy(i, j).start()
        aux_rows(ob, squares4)
        s5_copy(i).start()
        return 0

    lax.fori_loop(1, NB, serve_send, 0)
    ob, squares4 = serve(0)
    for j in range(1, 4):
        s4_copy(0, j).start()
    aux_rows(ob, squares4)
    r4[yc, b] = gs[b, yc]
    r5[b] = auxs[b]

    lax.fori_loop(1, NB, lambda k, _: (s5_copy(k).wait_recv(), 0)[1], 0)
    stats = r5[0, :rows, :128].astype(F32)
    for i in range(1, NB):
        stats = stats + r5[i, :rows, :128].astype(F32)
    l128 = iota((rows, 128), 1)

    def inverse_rms(n):
        picked = jnp.where(l128 % 2 == n, jnp.where(l128 < 4, stats, 0.0), 0.0)
        return lax.rsqrt(jnp.sum(picked, -1, keepdims=True) / D + EPS)

    scale0, scale1 = inverse_rms(0), inverse_rms(1)
    scale_ab = jnp.where(l128 < 96, scale0, scale1)

    lax.fori_loop(1, 32, lambda k, _: (s4_copy(lax.div(k, 4), lax.rem(k, 4)).wait_recv(), 0)[1], 0)

    def silu(v):
        return v / (1.0 + jnp.exp(-v))

    mr, mc = iota((nz * 16, 2 * rows), 0), iota((nz * 16, 2 * rows), 1)
    m_in = mr % 4
    m_src = (m_in % 2) * rows + (mr // 16) * 2 + m_in // 2
    spread = [onehot((mc == m_src) & ((mr // 4) % 4 == j)) for j in range(4)]

    def hidden(g):
        acc = r4[g, 0].astype(F32)
        for i in range(1, NB):
            acc = acc + r4[g, i].astype(F32)
        h_ab = silu(acc[:, :128] * scale_ab) * (acc[:, 128:256] * scale_ab)
        last = acc[:, 256:] * scale1
        h_c = silu(last) * pltpu.roll(last, 64, 1)
        h_one = jnp.where(l128 < 32, pltpu.roll(h_ab, 32, 1), pltpu.roll(h_c, 32, 1))
        return jnp.concatenate([h_ab, h_one], 0).astype(BF16)

    hids = [hidden(g) for g in range(4)]
    wc_copy(0).wait_recv()
    wc_copy(1).wait_recv()
    left = jnp.zeros((nz * 16, FB), F32)
    right = jnp.zeros((nz * 16, FB), F32)
    for g in range(4):
        for j in range(4):
            lhs = dot(spread[j], hids[g]).astype(BF16)[:, :HOLD]
            left = left + dot(lhs, wbuf[g, 2 * j])
            right = right + dot(lhs, wbuf[g, 2 * j + 1])
    ms[:, :, :FB] = left.astype(BF16).reshape(nz, 16, FB)
    ms[:, :, FB:] = right.astype(BF16).reshape(nz, 16, FB)

    def s6_copy(src, step, slot):
        return remote(src, r6.at[slot], s6_ssem.at[slot], s6_rsem.at[slot], dev(y, lax.rem(z + step + nz, nz), c, b))

    s6_waits = []

    def s6_send(way, dist, step, src):
        copy = s6_copy(src, way * step, (way * dist) % nz)
        copy.start()
        s6_waits.append(copy)

    for parent, kids in reversed(TREE):
        for kid in kids:
            for way in (1, -1):
                if kid <= far[way] and kid not in kids_of:
                    s6_send(way, kid, kid - parent, ms.at[lax.rem(z + way * kid + nz, nz)])

    def gathered(pick):
        return jnp.concatenate(
            [jnp.concatenate([pick(2 * j), pick(2 * j + 1)], 1) for j in range(4)], 0
        )

    resid4 = gathered(lambda i: r5[i, rows : rows + 16, :].astype(F32)[0:4])
    weight4 = gathered(
        lambda i: jnp.broadcast_to(
            r5[i, rows : rows + 16, :].astype(F32)[4:5] * r5[i, rows : rows + 16, :].astype(F32)[5:6], (4, FB)
        )
    )

    def s6_sum(way, kids, acc):
        for kid in kids:
            if kid <= far[way]:
                slot = (way * kid) % nz
                s6_copy(ms.at[z], 0, slot).wait_recv()
                acc = acc + r6[slot].astype(F32)
        return acc

    for at, (parent, kids) in reversed(list(enumerate(TREE[1:]))):
        for way in (1, -1):
            if parent <= far[way]:
                share = ms[lax.rem(z + way * parent + nz, nz)].astype(F32)
                ags[(1 - way) // 2, at] = s6_sum(way, kids, share).astype(BF16)
                s6_send(way, parent, parent, ags.at[(1 - way) // 2, at])
    moved = resid4 + ms[z].astype(F32)
    moved = s6_sum(-1, TREE[0][1][::-1], s6_sum(1, TREE[0][1][::-1], moved))
    ss = jnp.sum(moved * moved, -1, keepdims=True)
    st = jnp.sum(moved * weight4, -1, keepdims=True)
    ss = ss[0:4] + ss[4:8] + ss[8:12] + ss[12:16]
    st = st[0:4] + st[4:8] + st[8:12] + st[12:16]
    score = jnp.broadcast_to(st * lax.rsqrt(ss / D + EPS), (4, FB))
    for i in range(NB):
        j, half = i // 2, i % 2
        fs[i] = jnp.concatenate([moved[4 * j : 4 * j + 4, half * FB : (half + 1) * FB], score], 0)

    def s7_copy(k):
        other = lax.rem(b + k, NB)
        return remote(fs.at[other], r7.at[b], s7_ssem.at[k], s7_rsem.at[k], dev(y, z, c, other))

    lax.fori_loop(1, NB, lambda k, _: (s7_copy(k).start(), 0)[1], 0)
    r7[b] = fs[b]

    lax.fori_loop(1, 16, lambda k, _: (w_copy(k).wait_send(), 0)[1], 0)
    wc_copy(0).wait_send()
    wc_copy(1).wait_send()
    lax.fori_loop(1, NB, lambda k, _: (s2_copy(k).wait_send(), 0)[1], 0)
    for copy in z_waits + y_waits:
        copy.wait_send()
    c_copy(0).wait_send()
    c_copy(1).wait_send()
    lax.fori_loop(1, 32, lambda k, _: (s4_copy(lax.div(k, 4), lax.rem(k, 4)).wait_send(), 0)[1], 0)
    lax.fori_loop(1, NB, lambda k, _: (s5_copy(k).wait_send(), 0)[1], 0)
    for copy in s6_waits:
        copy.wait_send()

    lax.fori_loop(1, NB, lambda k, _: (s7_copy(k).wait_recv(), 0)[1], 0)
    out_ref[...] = r7[...]
    lax.fori_loop(1, NB, lambda k, _: (s7_copy(k).wait_send(), 0)[1], 0)


def finish(parts_ref, out_ref, score_ref):
    out_ref[...] = jnp.concatenate([parts_ref[i, :4, :] for i in range(NB)], 0).astype(BF16)
    col = jnp.concatenate([parts_ref[i, 4:, :32] for i in range(NB)], 0)
    score_ref[...] = jnp.sum(jnp.where(iota((32, 32), 0) == iota((32, 32), 1), col, 0.0), 0, keepdims=True)


def shards(
    nz,
    resid,
    queries,
    new_kv,
    prefix_pool,
    page_table,
    prompt_len,
    tail_pool,
    tail_len,
    migration,
    out_w,
    mlp_gain,
    gate_w,
    up_w,
    down_w,
    final_gain,
    score_w,
):
    conts = 4 * nz * CONT
    rows = 2 * nz
    vmem = pl.BlockSpec(memory_space=pltpu.VMEM)
    hbm = pl.BlockSpec(memory_space=pl.ANY)
    dma = pltpu.SemaphoreType.DMA
    parts = pl.pallas_call(
        functools.partial(kernel, nz),
        out_shape=jax.ShapeDtypeStruct((NB, 8, FB), F32),
        in_specs=[hbm] * 16,
        out_specs=vmem,
        scratch_shapes=[
            pltpu.VMEM((PAGES * 256, HD), BF16),
            pltpu.VMEM((CONT * 256, HD), BF16),
            pltpu.VMEM((64, HD), BF16),
            pltpu.VMEM((64, HD), BF16),
            pltpu.VMEM((1, PAGES), jnp.int32),
            pltpu.SMEM((1,), jnp.int32),
            pltpu.SMEM((1, CONT), jnp.int32),
            pltpu.VMEM((HOLD, FB), BF16),
            pltpu.VMEM((2 * HD, D), BF16),
            pltpu.VMEM((32, D), BF16),
            pltpu.VMEM((conts // 128, 128), jnp.int32),
            pltpu.VMEM((HOLD, FB), BF16),
            pltpu.VMEM((HOLD, FB), BF16),
            pltpu.VMEM((16, 128), BF16),
            pltpu.VMEM((2, 128), BF16),
            pltpu.VMEM((2, 128), BF16),
            pltpu.VMEM((PAGES, 256), F32),
            pltpu.VMEM((64, PAGES * 256), F32),
            pltpu.VMEM((4, NB, HOLD, FB), BF16),
            pltpu.VMEM((NB, 32, FB), BF16),
            pltpu.VMEM((NB - 1, 32, FB), BF16),
            pltpu.VMEM((2, 4, nz, CONT, FB), BF16),
            pltpu.VMEM((NB, 4 * rows, conts), BF16),
            pltpu.VMEM((2, 4, 128, nz * CONT), BF16),
            pltpu.VMEM((4, nz * CONT, 512), BF16),
            pltpu.VMEM((NB, 4, rows, 384), BF16),
            pltpu.VMEM((4, NB, rows, 384), BF16),
            pltpu.VMEM((NB, rows + 16, FB), BF16),
            pltpu.VMEM((NB, rows + 16, FB), BF16),
            pltpu.VMEM((nz, 16, 512), BF16),
            pltpu.VMEM((2, len(TREE) - 1, 16, 512), BF16),
            pltpu.VMEM((nz, 16, 512), BF16),
            pltpu.VMEM((NB, 8, FB), F32),
            pltpu.VMEM((NB, 8, FB), F32),
            dma((16,)),
            dma((16,)),
            dma((16,)),
            dma((2,)),
            dma((2,)),
            dma((NB,)),
            dma((NB,)),
            dma((nz,)),
            dma((nz,)),
            dma((nz,)),
            dma((nz,)),
            dma((2,)),
            dma((2,)),
            dma((32,)),
            dma((32,)),
            dma((NB,)),
            dma((NB,)),
            dma((nz,)),
            dma((nz,)),
            dma((NB,)),
            dma((NB,)),
        ],
        compiler_params=pltpu.CompilerParams(
            collective_id=0, has_side_effects=True, vmem_limit_bytes=58 * 1024 * 1024
        ),
    )(
        prefix_pool.reshape(PAGES * 256, HD),
        tail_pool.reshape(CONT * 256, HD),
        queries.reshape(64, HD),
        new_kv.reshape(64, HD),
        page_table,
        prompt_len,
        tail_len,
        down_w,
        out_w,
        resid,
        migration.reshape(conts // 128, 128),
        gate_w.T,
        up_w.T,
        mlp_gain.reshape(16, 128),
        final_gain.reshape(2, 128),
        score_w.reshape(2, 128),
    )
    out, score = pl.pallas_call(
        finish,
        out_shape=(
            jax.ShapeDtypeStruct((32, FB), BF16),
            jax.ShapeDtypeStruct((1, 32), F32),
        ),
        in_specs=[vmem],
        out_specs=(vmem, vmem),
    )(parts)
    return out, score.reshape(32)


def solution(mesh):
    nz = mesh.shape["dp"] // 4
    return jax.shard_map(
        functools.partial(shards, nz),
        mesh=mesh,
        in_specs=(
            P("dp", None),
            P("dp", "blk", None),
            P("dp", None, "blk", None),
            P("dp", None, None, "blk", None),
            P("dp", None),
            P("dp"),
            P("dp", None, None, "blk", None),
            P("dp", None),
            P(),
            P("blk", None),
            P(),
            P("blk", "dp"),
            P("blk", "dp"),
            P("dp", "blk"),
            P("blk"),
            P("blk"),
        ),
        out_specs=(P("dp", "blk"), P("dp")),
        check_vma=False,
    )
```

```python
import functools
import math

import jax
import jax.numpy as jnp
from jax import lax
from jax.experimental import pallas as pl
from jax.experimental.pallas import tpu as pltpu
from jax.sharding import PartitionSpec as P

MESH = pl.DeviceIdType.MESH
F32 = jnp.float32
BF16 = jnp.bfloat16
NEG = -1e30
EPS = 1e-06
D = 2048
NB = 8
FB = 256
HOLD = 96
CONT = 16
PAGES = 32
HD = 128
TREE = ((0, (5, 2, 1)), (2, (4, 3)), (5, (8, 7, 6)))


def iota(shape, dim):
    return lax.broadcasted_iota(jnp.int32, shape, dim)


def dot(a, b):
    return lax.dot_general(a, b, (((1,), (0,)), ((), ())), preferred_element_type=F32)


def dot_nt(a, b):
    return lax.dot_general(a, b, (((1,), (1,)), ((), ())), preferred_element_type=F32)


def onehot(cond):
    return jnp.where(cond, 1.0, 0.0).astype(BF16)


def kernel(
    nz,
    *refs,
):
    sources, out_ref, held, refs = refs[:16], refs[16], refs[17:33], refs[33:]
    (kv, tail, q_ref, new_ref, tab_ref, plen_ref, tlen_ref, down_ref, ow, resid_ref, mig_ref, gate_ref, up_ref, gain_ref, fg_ref, sw_ref) = held
    (bias, sbuf, wbuf, s2, r2, xall, perm, sel, hs, gs, r4, auxs, r5, ms, ags, r6, fs, r7, load_sem, w_ssem, w_rsem, s2_ssem, s2_rsem, z_ssem, z_rsem, y_ssem, y_rsem, c_ssem, c_rsem, s4_ssem, s4_rsem, s5_ssem, s5_rsem, s6_ssem, s6_rsem, s7_ssem, s7_rsem) = refs
    dp = lax.axis_index("dp")
    b = lax.axis_index("blk")
    c = lax.rem(dp, 2)
    z = lax.rem(lax.div(dp, 2), nz)
    y = lax.div(dp, 2 * nz)
    yc = 2 * y + c
    x, yh = lax.rem(b, 4), lax.div(b, 4)
    conts = 4 * nz * CONT
    rows = 2 * nz

    def dev(y_, z_, c_, b_):
        return ((y_ * nz + z_) * 2 + c_, b_)

    def remote(src, dst, ssem, rsem, target):
        return pltpu.make_async_remote_copy(
            src_ref=src, dst_ref=dst, send_sem=ssem, recv_sem=rsem, device_id=target, device_id_type=MESH
        )

    barrier = pltpu.get_barrier_semaphore()

    def greet_plane(k, _):
        other = lax.rem(b * 4 + yc + k, 32)
        oyc, ob = lax.rem(other, 4), lax.div(other, 4)
        pl.semaphore_signal(
            barrier, inc=1, device_id=dev(lax.div(oyc, 2), z, lax.rem(oyc, 2), ob), device_id_type=MESH
        )
        return 0

    def greet_line(k, _):
        pl.semaphore_signal(barrier, inc=1, device_id=dev(y, lax.rem(z + k, nz), c, b), device_id_type=MESH)
        return 0

    loads = [pltpu.make_async_copy(sources[i], held[i], load_sem.at[i]) for i in range(16)]
    for load in loads:
        load.start()

    lax.fori_loop(1, 32, greet_plane, 0)
    lax.fori_loop(1, nz, greet_line, 0)

    for load in loads[2:8]:
        load.wait()

    wbuf[y, c, yh, x] = down_ref[...]
    row4 = y * 2 + yh

    def wy_copy(k):
        other = lax.rem(row4 + k, 4)
        piece = wbuf.at[y, c, yh, x]
        return remote(piece, piece, w_ssem.at[k], w_rsem.at[k], dev(lax.div(other, 2), z, c, lax.rem(other, 2) * 4 + x))

    def wx_copy(k):
        piece = wbuf.at[:, c, :, x]
        return remote(piece, piece, w_ssem.at[3 + k], w_rsem.at[3 + k], dev(y, z, c, yh * 4 + lax.rem(x + k, 4)))

    def wc_copy():
        piece = wbuf.at[:, c]
        return remote(piece, piece, w_ssem.at[7], w_rsem.at[7], dev(y, z, 1 - c, b))

    r64, c64 = iota((64, 64), 0), iota((64, 64), 1)
    q_src = (r64 % 16) * 4 + ((r64 // 16) % 2) * 2 + r64 // 32
    q = dot(onehot(q_src == c64), q_ref[...]).astype(BF16)

    lane = iota((PAGES, 256), 1)
    page_no = iota((PAGES, PAGES), 0) == jnp.broadcast_to(tab_ref[...], (PAGES, PAGES))
    logical = jnp.sum(jnp.where(page_no, iota((PAGES, PAGES), 1), 0), -1, keepdims=True)
    limit = jnp.broadcast_to(plen_ref[0, 0] - logical * 128, (PAGES, 256))
    bias[...] = jnp.where((lane % 2 == 0) & (lane // 2 < limit), 0.0, NEG)
    unit = math.log2(math.e) / math.sqrt(HD)

    def widest(best, s):
        for i in range(s.shape[1] // 128):
            best = jnp.maximum(best, s[:, i * 128 : (i + 1) * 128])
        return best

    def next_lane(w):
        return jnp.concatenate(
            [pltpu.roll(w[:, i * 128 : (i + 1) * 128], 1, 1) for i in range(w.shape[1] // 128)], 1
        ).astype(BF16)

    loads[0].wait()
    best = jnp.full((64, 128), NEG, F32)
    for i in range(PAGES // 8):
        s = dot_nt(q, kv[i * 2048 : (i + 1) * 2048, :])
        for u in range(8):
            l = i * 8 + u
            part = s[:, u * 256 : (u + 1) * 256] + bias[l : l + 1, :]
            sbuf[:, l * 256 : (l + 1) * 256] = part
            best = widest(best, part)
    loads[1].wait()
    owner = iota((64, 256), 0) % 16
    t_lane = iota((1, 256), 1)
    s_tail = jnp.full((64, 256), NEG, F32)
    for i in range(CONT // 8):
        s = dot_nt(q, tail[i * 2048 : (i + 1) * 2048, :])
        for u in range(8):
            t = i * 8 + u
            t_bias = jnp.where((t_lane % 2 == 0) & (t_lane // 2 < tlen_ref[0, t]), 0.0, NEG)
            s_tail = jnp.where(owner == t, s[:, u * 256 : (u + 1) * 256] + t_bias, s_tail)

    new_cont, new_tok = c64 // 4, (c64 // 2) % 2
    new_ok = (c64 % 2 == 0) & (new_cont == r64 % 16) & (new_tok <= (r64 // 16) % 2)
    s_new = jnp.where(new_ok, dot_nt(q, new_ref[...]), NEG)
    top = jnp.maximum(
        jnp.max(widest(best, s_tail), -1, keepdims=True), jnp.max(s_new, -1, keepdims=True)
    )
    w_tail = jnp.exp2((s_tail - top) * unit)
    w_new = jnp.exp2((s_new - top) * unit)
    total = w_tail[:, :128] + w_tail[:, 128:]
    mixed = dot(pltpu.roll(w_new, 1, 1).astype(BF16), new_ref[...])
    for i in range(PAGES // 8):
        w = jnp.exp2((sbuf[:, i * 2048 : (i + 1) * 2048] - top) * unit)
        for u in range(16):
            total = total + w[:, u * 128 : (u + 1) * 128]
        mixed = mixed + dot(next_lane(w), kv[i * 2048 : (i + 1) * 2048, :])
    v_tail = next_lane(w_tail)
    for i in range(CONT // 8):
        w = jnp.concatenate(
            [jnp.where(owner == i * 8 + u, v_tail, jnp.zeros_like(v_tail)) for u in range(8)], 1
        )
        mixed = mixed + dot(w, tail[i * 2048 : (i + 1) * 2048, :])
    total = jnp.sum(total, -1, keepdims=True) + jnp.sum(w_new, -1, keepdims=True)
    attn = (mixed / total).astype(BF16)

    pl.semaphore_wait(barrier, 31 + nz - 1)

    loads[8].wait()
    for i in range(NB):
        cols = slice(i * FB, (i + 1) * FB)
        s2[i] = (dot(attn[:32], ow[:HD, cols]) + dot(attn[32:], ow[HD:, cols])).astype(BF16)

    def s2_copy(k):
        other = lax.rem(b + k, NB)
        return remote(s2.at[other], r2.at[k - 1], s2_ssem.at[k], s2_rsem.at[k], dev(y, z, c, other))

    lax.fori_loop(1, NB, lambda k, _: (s2_copy(k).start(), 0)[1], 0)
    lax.fori_loop(1, 4, lambda k, _: (wy_copy(k).start(), 0)[1], 0)

    for load in loads[9:]:
        load.wait()
    mig = mig_ref[...]
    home = mig // CONT
    stored = ((home // (2 * nz) * 2 + home % 2) * nz + (home // 2) % nz) * CONT + mig % CONT
    chunk = 4 * rows
    lines = mig.shape[0]
    p_row = iota((chunk, 1), 0)
    first = ((p_row // (2 * rows)) * nz + (p_row // 2) % nz) * 32 + ((p_row // rows) % 2) * 16 + p_row % 2
    line = onehot(iota((chunk, lines), 1) == first // 128)
    spread_mig = dot(line, (stored // 32).astype(F32).astype(BF16)) * 32.0 + dot(
        line, (stored % 32).astype(F32).astype(BF16)
    )
    slot_lane = iota((chunk, 128), 1) - first % 128
    for i in range(NB):
        column = jnp.sum(jnp.where(slot_lane == 2 * i, spread_mig, 0.0), -1, keepdims=True)
        perm[i] = onehot(iota((chunk, conts), 1) == column.astype(jnp.int32))
    gains = gain_ref[...].astype(F32)
    g_row = iota((16, 128), 0)
    gain = jnp.concatenate(
        [
            jnp.sum(jnp.where(g_row == 2 * b, gains, 0.0), 0, keepdims=True),
            jnp.sum(jnp.where(g_row == 2 * b + 1, gains, 0.0), 0, keepdims=True),
        ],
        1,
    )
    gate_t = (gate_ref[...].astype(F32) * gain).astype(BF16)
    up_t = (up_ref[...].astype(F32) * gain).astype(BF16)
    none32 = jnp.zeros((32, FB), BF16)
    none96 = jnp.zeros((96, FB), BF16)
    w_first = jnp.concatenate([gate_t, none32, up_t, none32], 0)
    w_second = jnp.concatenate(
        [none96, gate_t[:32], none96, up_t[:32], gate_t[32:], up_t[32:]], 0
    )
    r32, c32 = iota((32, 32), 0), iota((32, 32), 1)
    order = onehot((r32 % 16) * 2 + r32 // 16 == c32)
    resid = dot(order, resid_ref[:, pl.ds(pl.multiple_of(b * FB, FB), FB)])

    sel_r, sel_c = iota((128, NB * rows), 0), iota((128, NB * rows), 1)
    place = sel_r % 16
    own_rows = jnp.concatenate([perm[i, pl.ds(pl.multiple_of(yc * rows, rows), rows), :] for i in range(NB)], 0)
    for n in range(2):
        picked = dot(
            onehot(
                (place < 4)
                & (place % 2 == n)
                & (sel_c == (sel_r // 16) * rows + z * 2 + (place // 2) % 2)
            ),
            own_rows,
        ).astype(BF16)
        for i in range(4):
            sel[n, i] = picked[:, i * nz * CONT : (i + 1) * nz * CONT]

    lax.fori_loop(1, NB, lambda k, _: (s2_copy(k).wait_recv(), 0)[1], 0)
    mid = resid + s2[b].astype(F32)
    for k in range(1, NB):
        mid = mid + r2[k - 1].astype(F32)
    xall[0, yc, z] = mid[:16].astype(BF16)
    xall[1, yc, z] = mid[16:].astype(BF16)

    def z_copy(source, step, slot):
        piece = xall.at[:, yc, source]
        return remote(piece, piece, z_ssem.at[slot], z_rsem.at[slot], dev(y, lax.rem(z + step + nz, nz), c, b))

    def y_copy(source, slot):
        piece = xall.at[:, yc, source]
        return remote(piece, piece, y_ssem.at[slot], y_rsem.at[slot], dev(1 - y, z, c, b))

    def c_copy(i):
        piece = xall.at[:, 2 * i + c]
        return remote(piece, piece, c_ssem.at[i], c_rsem.at[i], dev(y, z, 1 - c, b))

    far = {1: nz // 2, -1: (nz - 1) // 2}
    z_waits, y_waits = [], []

    def z_forward(way, parent, kids):
        source = lax.rem(z - way * parent + nz, nz)
        for kid in kids:
            if kid <= far[way]:
                copy = z_copy(source, way * (kid - parent), (way * kid) % nz)
                copy.start()
                z_waits.append(copy)

    def y_forward(way, dist):
        slot = (way * dist) % nz
        copy = y_copy(lax.rem(z - way * dist + nz, nz), slot)
        copy.start()
        y_waits.append(copy)

    for way in (1, -1):
        z_forward(way, *TREE[0])
    y_forward(1, 0)
    lax.fori_loop(1, 4, lambda k, _: (wy_copy(k).wait_recv(), 0)[1], 0)
    lax.fori_loop(1, 4, lambda k, _: (wx_copy(k).start(), 0)[1], 0)
    kids_of = dict(TREE)
    for dist in (2, 5, 1, 4, 3, 6, 7, 8):
        for way in (1, -1):
            if dist <= far[way]:
                z_copy(z, 0, (way * dist) % nz).wait_recv()
                if dist in kids_of:
                    z_forward(way, dist, kids_of[dist])
                y_forward(way, dist)

    e_lane = iota((FB, 128), 1)
    e_first = onehot((e_lane == 0) | (e_lane == 2))
    e_second = onehot((e_lane == 1) | (e_lane == 3))

    def project(block, res):
        x0 = xall[0, block].reshape(nz * CONT, FB)
        x1 = xall[1, block].reshape(nz * CONT, FB)
        h1 = dot_nt(x1, w_second)
        hs[block, :, :256] = (dot_nt(x0, w_first) + h1[:, :256]).astype(BF16)
        hs[block, :, 256:384] = h1[:, 256:].astype(BF16)
        sq0 = (x0.astype(F32) * x0.astype(F32)).astype(BF16)
        sq1 = (x1.astype(F32) * x1.astype(F32)).astype(BF16)
        squares = dot(sq0, e_first) + dot(sq1, e_second)
        high = squares.astype(BF16).astype(F32)
        hs[block, :, 384:] = jnp.where(iota((nz * CONT, 128), 1) < 2, high, squares - high).astype(BF16)
        return res + dot(sel[0, block], x0) + dot(sel[1, block], x1)

    c_copy(y).start()
    res = project(yc, jnp.zeros((128, FB), F32))
    c_copy(y).wait_recv()
    res = project(2 * y + 1 - c, res)
    for copy in y_waits:
        copy.wait_recv()
    c_copy(1 - y).start()
    res = project(2 * (1 - y) + c, res)

    lax.fori_loop(1, 4, lambda k, _: (wx_copy(k).wait_recv(), 0)[1], 0)
    wc_copy().start()

    c_copy(1 - y).wait_recv()
    res = project(2 * (1 - y) + 1 - c, res)

    fg = fg_ref[...].astype(F32)
    sw = sw_ref[...].astype(F32)
    a_row = iota((128, FB), 0) % 16
    res = jnp.where(a_row == 4, jnp.concatenate([fg[0:1], fg[1:2]], 1), res)
    res = jnp.where(a_row == 5, jnp.concatenate([sw[0:1], sw[1:2]], 1), res).astype(BF16)
    for i in range(NB):
        auxs[i, rows : rows + 16, :] = res[i * 16 : (i + 1) * 16]

    def s4_copy(i, j):
        ob, oyc = lax.rem(b + i, NB), lax.rem(yc + j, 4)
        return remote(
            gs.at[ob, oyc],
            r4.at[yc, b],
            s4_ssem.at[i * 4 + j],
            s4_rsem.at[i * 4 + j],
            dev(lax.div(oyc, 2), z, lax.rem(oyc, 2), ob),
        )

    def s5_copy(i):
        ob = lax.rem(b + i, NB)
        return remote(auxs.at[ob], r5.at[b], s5_ssem.at[i], s5_rsem.at[i], dev(y, z, c, ob))

    def serve(pair):
        lhs = jnp.concatenate([perm[2 * pair], perm[2 * pair + 1]], 0)
        g = dot(lhs, hs[...].reshape(conts, 512)).astype(BF16)
        for u in range(2):
            half = g[u * 4 * rows : (u + 1) * 4 * rows]
            ob = 2 * pair + u
            gs[ob] = half[:, :384].reshape(4, rows, 384)
            squares4 = half[:, 384:].reshape(4, rows, 128)
            pick = jnp.zeros((rows, 128), BF16)
            for i in range(4):
                pick = jnp.where(yc == i, squares4[i], pick)
            auxs[ob, :rows, :128] = pick
            auxs[ob, :rows, 128:] = jnp.zeros((rows, 128), BF16)

    def serve_send(step, _):
        pair = lax.rem(lax.div(b, 2) + step, NB // 2)
        serve(pair)
        for u in range(2):
            away = lax.rem(2 * pair + u - b + NB, NB)
            for j in range(4):
                s4_copy(away, j).start()
            s5_copy(away).start()
        return 0

    lax.fori_loop(1, NB // 2, serve_send, 0)
    serve(lax.div(b, 2))
    away = lax.rem(1 - 2 * lax.rem(b, 2) + NB, NB)
    for j in range(4):
        s4_copy(away, j).start()
    s5_copy(away).start()
    for j in range(1, 4):
        s4_copy(0, j).start()
    r4[yc, b] = gs[b, yc]
    r5[b] = auxs[b]

    lax.fori_loop(1, NB, lambda k, _: (s5_copy(k).wait_recv(), 0)[1], 0)
    stats = r5[0, :rows, :128].astype(F32)
    for i in range(1, NB):
        stats = stats + r5[i, :rows, :128].astype(F32)
    l128 = iota((rows, 128), 1)

    def inverse_rms(n):
        picked = jnp.where(l128 % 2 == n, jnp.where(l128 < 4, stats, 0.0), 0.0)
        return lax.rsqrt(jnp.sum(picked, -1, keepdims=True) / D + EPS)

    scale0, scale1 = inverse_rms(0), inverse_rms(1)
    scale_ab = jnp.where(l128 < 96, scale0, scale1)

    lax.fori_loop(1, 32, lambda k, _: (s4_copy(lax.div(k, 4), lax.rem(k, 4)).wait_recv(), 0)[1], 0)

    def silu(v):
        return v / (1.0 + jnp.exp(-v))

    mr, mc = iota((nz * 16, 2 * rows), 0), iota((nz * 16, 2 * rows), 1)
    m_in = mr % 4
    m_src = (m_in % 2) * rows + (mr // 16) * 2 + m_in // 2
    spread = [onehot((mc == m_src) & ((mr // 4) % 4 == j)) for j in range(4)]

    def hidden(g):
        acc = r4[g, 0].astype(F32)
        for i in range(1, NB):
            acc = acc + r4[g, i].astype(F32)
        h_ab = silu(acc[:, :128] * scale_ab) * (acc[:, 128:256] * scale_ab)
        last = acc[:, 256:] * scale1
        h_c = silu(last) * pltpu.roll(last, 64, 1)
        h_one = jnp.where(l128 < 32, pltpu.roll(h_ab, 32, 1), pltpu.roll(h_c, 32, 1))
        return jnp.concatenate([h_ab, h_one], 0).astype(BF16)

    hids = [hidden(g) for g in range(4)]
    wc_copy().wait_recv()
    left = jnp.zeros((nz * 16, FB), F32)
    right = jnp.zeros((nz * 16, FB), F32)
    for g in range(4):
        for j in range(4):
            lhs = dot(spread[j], hids[g]).astype(BF16)[:, :HOLD]
            left = left + dot(lhs, wbuf[g // 2, g % 2, j // 2, 2 * (j % 2)])
            right = right + dot(lhs, wbuf[g // 2, g % 2, j // 2, 2 * (j % 2) + 1])
    ms[:, :, :FB] = left.astype(BF16).reshape(nz, 16, FB)
    ms[:, :, FB:] = right.astype(BF16).reshape(nz, 16, FB)

    def s6_copy(src, step, slot):
        return remote(src, r6.at[slot], s6_ssem.at[slot], s6_rsem.at[slot], dev(y, lax.rem(z + step + nz, nz), c, b))

    s6_waits = []

    def s6_send(way, dist, step, src):
        copy = s6_copy(src, way * step, (way * dist) % nz)
        copy.start()
        s6_waits.append(copy)

    for parent, kids in reversed(TREE):
        for kid in kids:
            for way in (1, -1):
                if kid <= far[way] and kid not in kids_of:
                    s6_send(way, kid, kid - parent, ms.at[lax.rem(z + way * kid + nz, nz)])

    def gathered(pick):
        return jnp.concatenate(
            [jnp.concatenate([pick(2 * j), pick(2 * j + 1)], 1) for j in range(4)], 0
        )

    resid4 = gathered(lambda i: r5[i, rows : rows + 16, :].astype(F32)[0:4])
    weight4 = gathered(
        lambda i: jnp.broadcast_to(
            r5[i, rows : rows + 16, :].astype(F32)[4:5] * r5[i, rows : rows + 16, :].astype(F32)[5:6], (4, FB)
        )
    )

    def s6_sum(way, kids, acc):
        for kid in kids:
            if kid <= far[way]:
                slot = (way * kid) % nz
                s6_copy(ms.at[z], 0, slot).wait_recv()
                acc = acc + r6[slot].astype(F32)
        return acc

    for at, (parent, kids) in reversed(list(enumerate(TREE[1:]))):
        for way in (1, -1):
            if parent <= far[way]:
                share = ms[lax.rem(z + way * parent + nz, nz)].astype(F32)
                ags[(1 - way) // 2, at] = s6_sum(way, kids, share).astype(BF16)
                s6_send(way, parent, parent, ags.at[(1 - way) // 2, at])
    moved = resid4 + ms[z].astype(F32)
    moved = s6_sum(-1, TREE[0][1][::-1], s6_sum(1, TREE[0][1][::-1], moved))
    ss = jnp.sum(moved * moved, -1, keepdims=True)
    st = jnp.sum(moved * weight4, -1, keepdims=True)
    ss = ss[0:4] + ss[4:8] + ss[8:12] + ss[12:16]
    st = st[0:4] + st[4:8] + st[8:12] + st[12:16]
    score = jnp.broadcast_to(st * lax.rsqrt(ss / D + EPS), (4, FB))
    for i in range(NB):
        j, half = i // 2, i % 2
        fs[i] = jnp.concatenate([moved[4 * j : 4 * j + 4, half * FB : (half + 1) * FB], score], 0)

    def s7_copy(k):
        other = lax.rem(b + k, NB)
        return remote(fs.at[other], r7.at[b], s7_ssem.at[k], s7_rsem.at[k], dev(y, z, c, other))

    lax.fori_loop(1, NB, lambda k, _: (s7_copy(k).start(), 0)[1], 0)
    r7[b] = fs[b]

    lax.fori_loop(1, 4, lambda k, _: (wy_copy(k).wait_send(), 0)[1], 0)
    lax.fori_loop(1, 4, lambda k, _: (wx_copy(k).wait_send(), 0)[1], 0)
    wc_copy().wait_send()
    lax.fori_loop(1, NB, lambda k, _: (s2_copy(k).wait_send(), 0)[1], 0)
    for copy in z_waits + y_waits:
        copy.wait_send()
    c_copy(0).wait_send()
    c_copy(1).wait_send()
    lax.fori_loop(1, 32, lambda k, _: (s4_copy(lax.div(k, 4), lax.rem(k, 4)).wait_send(), 0)[1], 0)
    lax.fori_loop(1, NB, lambda k, _: (s5_copy(k).wait_send(), 0)[1], 0)
    for copy in s6_waits:
        copy.wait_send()

    lax.fori_loop(1, NB, lambda k, _: (s7_copy(k).wait_recv(), 0)[1], 0)
    out_ref[...] = r7[...]
    lax.fori_loop(1, NB, lambda k, _: (s7_copy(k).wait_send(), 0)[1], 0)


def finish(parts_ref, out_ref, score_ref):
    out_ref[...] = jnp.concatenate([parts_ref[i, :4, :] for i in range(NB)], 0).astype(BF16)
    col = jnp.concatenate([parts_ref[i, 4:, :32] for i in range(NB)], 0)
    score_ref[...] = jnp.sum(jnp.where(iota((32, 32), 0) == iota((32, 32), 1), col, 0.0), 0, keepdims=True)


def shards(
    nz,
    resid,
    queries,
    new_kv,
    prefix_pool,
    page_table,
    prompt_len,
    tail_pool,
    tail_len,
    migration,
    out_w,
    mlp_gain,
    gate_w,
    up_w,
    down_w,
    final_gain,
    score_w,
):
    conts = 4 * nz * CONT
    rows = 2 * nz
    vmem = pl.BlockSpec(memory_space=pltpu.VMEM)
    hbm = pl.BlockSpec(memory_space=pl.ANY)
    dma = pltpu.SemaphoreType.DMA
    parts = pl.pallas_call(
        functools.partial(kernel, nz),
        out_shape=jax.ShapeDtypeStruct((NB, 8, FB), F32),
        in_specs=[hbm] * 16,
        out_specs=vmem,
        scratch_shapes=[
            pltpu.VMEM((PAGES * 256, HD), BF16),
            pltpu.VMEM((CONT * 256, HD), BF16),
            pltpu.VMEM((64, HD), BF16),
            pltpu.VMEM((64, HD), BF16),
            pltpu.VMEM((1, PAGES), jnp.int32),
            pltpu.SMEM((1, 1), jnp.int32),
            pltpu.SMEM((1, CONT), jnp.int32),
            pltpu.VMEM((HOLD, FB), BF16),
            pltpu.VMEM((2 * HD, D), BF16),
            pltpu.VMEM((32, D), BF16),
            pltpu.VMEM((conts // 128, 128), jnp.int32),
            pltpu.VMEM((HOLD, FB), BF16),
            pltpu.VMEM((HOLD, FB), BF16),
            pltpu.VMEM((16, 128), BF16),
            pltpu.VMEM((2, 128), BF16),
            pltpu.VMEM((2, 128), BF16),
            pltpu.VMEM((PAGES, 256), F32),
            pltpu.VMEM((64, PAGES * 256), F32),
            pltpu.VMEM((2, 2, 2, 4, HOLD, FB), BF16),
            pltpu.VMEM((NB, 32, FB), BF16),
            pltpu.VMEM((NB - 1, 32, FB), BF16),
            pltpu.VMEM((2, 4, nz, CONT, FB), BF16),
            pltpu.VMEM((NB, 4 * rows, conts), BF16),
            pltpu.VMEM((2, 4, 128, nz * CONT), BF16),
            pltpu.VMEM((4, nz * CONT, 512), BF16),
            pltpu.VMEM((NB, 4, rows, 384), BF16),
            pltpu.VMEM((4, NB, rows, 384), BF16),
            pltpu.VMEM((NB, rows + 16, FB), BF16),
            pltpu.VMEM((NB, rows + 16, FB), BF16),
            pltpu.VMEM((nz, 16, 512), BF16),
            pltpu.VMEM((2, len(TREE) - 1, 16, 512), BF16),
            pltpu.VMEM((nz, 16, 512), BF16),
            pltpu.VMEM((NB, 8, FB), F32),
            pltpu.VMEM((NB, 8, FB), F32),
            dma((16,)),
            dma((8,)),
            dma((8,)),
            dma((NB,)),
            dma((NB,)),
            dma((nz,)),
            dma((nz,)),
            dma((nz,)),
            dma((nz,)),
            dma((2,)),
            dma((2,)),
            dma((32,)),
            dma((32,)),
            dma((NB,)),
            dma((NB,)),
            dma((nz,)),
            dma((nz,)),
            dma((NB,)),
            dma((NB,)),
        ],
        compiler_params=pltpu.CompilerParams(
            collective_id=0, has_side_effects=True, vmem_limit_bytes=58 * 1024 * 1024
        ),
    )(
        prefix_pool.reshape(PAGES * 256, HD),
        tail_pool.reshape(CONT * 256, HD),
        queries.reshape(64, HD),
        new_kv.reshape(64, HD),
        page_table,
        prompt_len.reshape(1, 1),
        tail_len,
        down_w,
        out_w,
        resid,
        migration.reshape(conts // 128, 128),
        gate_w.T,
        up_w.T,
        mlp_gain.reshape(16, 128),
        final_gain.reshape(2, 128),
        score_w.reshape(2, 128),
    )
    out, score = pl.pallas_call(
        finish,
        out_shape=(
            jax.ShapeDtypeStruct((32, FB), BF16),
            jax.ShapeDtypeStruct((1, 32), F32),
        ),
        in_specs=[vmem],
        out_specs=(vmem, vmem),
    )(parts)
    return out, score.reshape(32)


def solution(mesh):
    nz = mesh.shape["dp"] // 4
    return jax.shard_map(
        functools.partial(shards, nz),
        mesh=mesh,
        in_specs=(
            P("dp", None),
            P("dp", "blk", None),
            P("dp", None, "blk", None),
            P("dp", None, None, "blk", None),
            P("dp", None),
            P("dp"),
            P("dp", None, None, "blk", None),
            P("dp", None),
            P(),
            P("blk", None),
            P(),
            P("blk", "dp"),
            P("blk", "dp"),
            P("dp", "blk"),
            P("blk"),
            P("blk"),
        ),
        out_specs=(P("dp", "blk"), P("dp")),
        check_vma=False,
    )
```

```python
import functools
import math

import jax
import jax.numpy as jnp
from jax import lax
from jax.experimental import pallas as pl
from jax.experimental.pallas import tpu as pltpu
from jax.sharding import PartitionSpec as P

MESH = pl.DeviceIdType.MESH
F32 = jnp.float32
BF16 = jnp.bfloat16
NEG = -1e30
EPS = 1e-06
D = 2048
NB = 8
FB = 256
HOLD = 96
CONT = 16
PAGES = 32
HD = 128
TREE = ((0, (5, 2, 1)), (2, (4, 3)), (5, (8, 7, 6)))


def iota(shape, dim):
    return lax.broadcasted_iota(jnp.int32, shape, dim)


def dot(a, b):
    return lax.dot_general(a, b, (((1,), (0,)), ((), ())), preferred_element_type=F32)


def dot_nt(a, b):
    return lax.dot_general(a, b, (((1,), (1,)), ((), ())), preferred_element_type=F32)


def onehot(cond):
    return jnp.where(cond, 1.0, 0.0).astype(BF16)


def kernel(
    nz,
    *refs,
):
    sources, out_ref, held, refs = refs[:16], refs[16], refs[17:33], refs[33:]
    (kv, tail, q_ref, new_ref, tab_ref, plen_ref, tlen_ref, down_ref, ow, resid_ref, mig_ref, gate_ref, up_ref, gain_ref, fg_ref, sw_ref) = held
    (bias, sbuf, wbuf, s2, r2, xall, perm, sel, hs, gs, r4, auxs, r5, ms, ags, r6, fs, r7, load_sem, w_ssem, w_rsem, s2_ssem, s2_rsem, z_ssem, z_rsem, y_ssem, y_rsem, c_ssem, c_rsem, s4_ssem, s4_rsem, s5_ssem, s5_rsem, s6_ssem, s6_rsem, s7_ssem, s7_rsem) = refs
    dp = lax.axis_index("dp")
    b = lax.axis_index("blk")
    c = lax.rem(dp, 2)
    z = lax.rem(lax.div(dp, 2), nz)
    y = lax.div(dp, 2 * nz)
    yc = 2 * y + c
    x, yh = lax.rem(b, 4), lax.div(b, 4)
    conts = 4 * nz * CONT
    rows = 2 * nz

    def dev(y_, z_, c_, b_):
        return ((y_ * nz + z_) * 2 + c_, b_)

    def remote(src, dst, ssem, rsem, target):
        return pltpu.make_async_remote_copy(
            src_ref=src, dst_ref=dst, send_sem=ssem, recv_sem=rsem, device_id=target, device_id_type=MESH
        )

    barrier = pltpu.get_barrier_semaphore()

    def greet_plane(k, _):
        other = lax.rem(b * 4 + yc + k, 32)
        oyc, ob = lax.rem(other, 4), lax.div(other, 4)
        pl.semaphore_signal(
            barrier, inc=1, device_id=dev(lax.div(oyc, 2), z, lax.rem(oyc, 2), ob), device_id_type=MESH
        )
        return 0

    def greet_line(k, _):
        pl.semaphore_signal(barrier, inc=1, device_id=dev(y, lax.rem(z + k, nz), c, b), device_id_type=MESH)
        return 0

    loads = [pltpu.make_async_copy(sources[i], held[i], load_sem.at[i]) for i in range(16)]
    for load in loads:
        load.start()

    lax.fori_loop(1, 32, greet_plane, 0)
    lax.fori_loop(1, nz, greet_line, 0)

    for load in loads[2:8]:
        load.wait()

    wbuf[y, c, yh, x] = down_ref[...]
    row4 = y * 2 + yh

    def wy_copy(k):
        other = lax.rem(row4 + k, 4)
        piece = wbuf.at[y, c, yh, x]
        return remote(piece, piece, w_ssem.at[k], w_rsem.at[k], dev(lax.div(other, 2), z, c, lax.rem(other, 2) * 4 + x))

    def wx_copy(k):
        piece = wbuf.at[:, c, :, x]
        return remote(piece, piece, w_ssem.at[3 + k], w_rsem.at[3 + k], dev(y, z, c, yh * 4 + lax.rem(x + k, 4)))

    def wc_copy():
        piece = wbuf.at[:, c]
        return remote(piece, piece, w_ssem.at[7], w_rsem.at[7], dev(y, z, 1 - c, b))

    r64, c64 = iota((64, 64), 0), iota((64, 64), 1)
    q_src = (r64 % 16) * 4 + ((r64 // 16) % 2) * 2 + r64 // 32
    q = dot(onehot(q_src == c64), q_ref[...]).astype(BF16)

    lane = iota((PAGES, 256), 1)
    page_no = iota((PAGES, PAGES), 0) == jnp.broadcast_to(tab_ref[...], (PAGES, PAGES))
    logical = jnp.sum(jnp.where(page_no, iota((PAGES, PAGES), 1), 0), -1, keepdims=True)
    limit = jnp.broadcast_to(plen_ref[0, 0] - logical * 128, (PAGES, 256))
    bias[...] = jnp.where((lane % 2 == 0) & (lane // 2 < limit), 0.0, NEG)
    unit = math.log2(math.e) / math.sqrt(HD)

    def widest(best, s):
        for i in range(s.shape[1] // 128):
            best = jnp.maximum(best, s[:, i * 128 : (i + 1) * 128])
        return best

    def next_lane(w):
        return jnp.concatenate(
            [pltpu.roll(w[:, i * 128 : (i + 1) * 128], 1, 1) for i in range(w.shape[1] // 128)], 1
        ).astype(BF16)

    loads[0].wait()
    best = jnp.full((64, 128), NEG, F32)
    for i in range(PAGES // 8):
        s = dot_nt(q, kv[i * 2048 : (i + 1) * 2048, :])
        for u in range(8):
            l = i * 8 + u
            part = s[:, u * 256 : (u + 1) * 256] + bias[l : l + 1, :]
            sbuf[:, l * 256 : (l + 1) * 256] = part
            best = widest(best, part)
    loads[1].wait()
    owner = iota((64, 256), 0) % 16
    t_lane = iota((1, 256), 1)
    s_tail = jnp.full((64, 256), NEG, F32)
    for i in range(CONT // 8):
        s = dot_nt(q, tail[i * 2048 : (i + 1) * 2048, :])
        for u in range(8):
            t = i * 8 + u
            t_bias = jnp.where((t_lane % 2 == 0) & (t_lane // 2 < tlen_ref[0, t]), 0.0, NEG)
            s_tail = jnp.where(owner == t, s[:, u * 256 : (u + 1) * 256] + t_bias, s_tail)

    new_cont, new_tok = c64 // 4, (c64 // 2) % 2
    new_ok = (c64 % 2 == 0) & (new_cont == r64 % 16) & (new_tok <= (r64 // 16) % 2)
    s_new = jnp.where(new_ok, dot_nt(q, new_ref[...]), NEG)
    top = jnp.maximum(
        jnp.max(widest(best, s_tail), -1, keepdims=True), jnp.max(s_new, -1, keepdims=True)
    )
    w_tail = jnp.exp2((s_tail - top) * unit)
    w_new = jnp.exp2((s_new - top) * unit)
    total = w_tail[:, :128] + w_tail[:, 128:]
    mixed = dot(pltpu.roll(w_new, 1, 1).astype(BF16), new_ref[...])
    for i in range(PAGES // 8):
        w = jnp.exp2((sbuf[:, i * 2048 : (i + 1) * 2048] - top) * unit)
        for u in range(16):
            total = total + w[:, u * 128 : (u + 1) * 128]
        mixed = mixed + dot(next_lane(w), kv[i * 2048 : (i + 1) * 2048, :])
    v_tail = next_lane(w_tail)
    for i in range(CONT // 8):
        w = jnp.concatenate(
            [jnp.where(owner == i * 8 + u, v_tail, jnp.zeros_like(v_tail)) for u in range(8)], 1
        )
        mixed = mixed + dot(w, tail[i * 2048 : (i + 1) * 2048, :])
    total = jnp.sum(total, -1, keepdims=True) + jnp.sum(w_new, -1, keepdims=True)
    attn = (mixed / total).astype(BF16)

    pl.semaphore_wait(barrier, 31 + nz - 1)

    loads[8].wait()
    for i in range(NB):
        cols = slice(i * FB, (i + 1) * FB)
        s2[i] = (dot(attn[:32], ow[:HD, cols]) + dot(attn[32:], ow[HD:, cols])).astype(BF16)

    def s2_copy(k):
        other = lax.rem(b + k, NB)
        return remote(s2.at[other], r2.at[k - 1], s2_ssem.at[k], s2_rsem.at[k], dev(y, z, c, other))

    lax.fori_loop(1, NB, lambda k, _: (s2_copy(k).start(), 0)[1], 0)
    lax.fori_loop(1, 4, lambda k, _: (wy_copy(k).start(), 0)[1], 0)

    for load in loads[9:]:
        load.wait()
    mig = mig_ref[...]
    home = mig // CONT
    stored = ((home // (2 * nz) * 2 + home % 2) * nz + (home // 2) % nz) * CONT + mig % CONT
    chunk = 4 * rows
    lines = mig.shape[0]
    p_row = iota((chunk, 1), 0)
    first = ((p_row // (2 * rows)) * nz + (p_row // 2) % nz) * 32 + ((p_row // rows) % 2) * 16 + p_row % 2
    line = onehot(iota((chunk, lines), 1) == first // 128)
    spread_mig = dot(line, (stored // 32).astype(F32).astype(BF16)) * 32.0 + dot(
        line, (stored % 32).astype(F32).astype(BF16)
    )
    slot_lane = iota((chunk, 128), 1) - first % 128
    for i in range(NB):
        column = jnp.sum(jnp.where(slot_lane == 2 * i, spread_mig, 0.0), -1, keepdims=True)
        perm[i] = onehot(iota((chunk, conts), 1) == column.astype(jnp.int32))
    gains = gain_ref[...].astype(F32)
    g_row = iota((16, 128), 0)
    gain = jnp.concatenate(
        [
            jnp.sum(jnp.where(g_row == 2 * b, gains, 0.0), 0, keepdims=True),
            jnp.sum(jnp.where(g_row == 2 * b + 1, gains, 0.0), 0, keepdims=True),
        ],
        1,
    )
    gate_t = (gate_ref[...].astype(F32) * gain).astype(BF16)
    up_t = (up_ref[...].astype(F32) * gain).astype(BF16)
    none32 = jnp.zeros((32, FB), BF16)
    none96 = jnp.zeros((96, FB), BF16)
    w_first = jnp.concatenate([gate_t, none32, up_t, none32], 0)
    w_second = jnp.concatenate(
        [none96, gate_t[:32], none96, up_t[:32], gate_t[32:], up_t[32:]], 0
    )
    r32, c32 = iota((32, 32), 0), iota((32, 32), 1)
    order = onehot((r32 % 16) * 2 + r32 // 16 == c32)
    resid = dot(order, resid_ref[:, pl.ds(pl.multiple_of(b * FB, FB), FB)])

    sel_r, sel_c = iota((128, NB * rows), 0), iota((128, NB * rows), 1)
    place = sel_r % 16
    own_rows = jnp.concatenate([perm[i, pl.ds(pl.multiple_of(yc * rows, rows), rows), :] for i in range(NB)], 0)
    for n in range(2):
        picked = dot(
            onehot(
                (place < 4)
                & (place % 2 == n)
                & (sel_c == (sel_r // 16) * rows + z * 2 + (place // 2) % 2)
            ),
            own_rows,
        ).astype(BF16)
        for i in range(4):
            sel[n, i] = picked[:, i * nz * CONT : (i + 1) * nz * CONT]

    lax.fori_loop(1, NB, lambda k, _: (s2_copy(k).wait_recv(), 0)[1], 0)
    mid = resid + s2[b].astype(F32)
    for k in range(1, NB):
        mid = mid + r2[k - 1].astype(F32)
    xall[0, yc, z] = mid[:16].astype(BF16)
    xall[1, yc, z] = mid[16:].astype(BF16)

    def z_copy(source, step, slot):
        piece = xall.at[:, yc, source]
        return remote(piece, piece, z_ssem.at[slot], z_rsem.at[slot], dev(y, lax.rem(z + step + nz, nz), c, b))

    def y_copy(source, slot):
        piece = xall.at[:, yc, source]
        return remote(piece, piece, y_ssem.at[slot], y_rsem.at[slot], dev(1 - y, z, c, b))

    def c_copy(i):
        piece = xall.at[:, 2 * i + c]
        return remote(piece, piece, c_ssem.at[i], c_rsem.at[i], dev(y, z, 1 - c, b))

    far = {1: nz // 2, -1: (nz - 1) // 2}
    z_waits, y_waits = [], []

    def z_forward(way, parent, kids):
        source = lax.rem(z - way * parent + nz, nz)
        for kid in kids:
            if kid <= far[way]:
                copy = z_copy(source, way * (kid - parent), (way * kid) % nz)
                copy.start()
                z_waits.append(copy)

    def y_forward(way, dist):
        slot = (way * dist) % nz
        copy = y_copy(lax.rem(z - way * dist + nz, nz), slot)
        copy.start()
        y_waits.append(copy)

    for way in (1, -1):
        z_forward(way, *TREE[0])
    y_forward(1, 0)
    lax.fori_loop(1, 4, lambda k, _: (wy_copy(k).wait_recv(), 0)[1], 0)
    lax.fori_loop(1, 4, lambda k, _: (wx_copy(k).start(), 0)[1], 0)
    kids_of = dict(TREE)
    for dist in (2, 5, 1, 4, 3, 6, 7, 8):
        for way in (1, -1):
            if dist <= far[way]:
                z_copy(z, 0, (way * dist) % nz).wait_recv()
                if dist in kids_of:
                    z_forward(way, dist, kids_of[dist])
                y_forward(way, dist)

    e_lane = iota((FB, 128), 1)
    e_first = onehot((e_lane == 0) | (e_lane == 2))
    e_second = onehot((e_lane == 1) | (e_lane == 3))

    def project(block, res):
        x0 = xall[0, block].reshape(nz * CONT, FB)
        x1 = xall[1, block].reshape(nz * CONT, FB)
        h1 = dot_nt(x1, w_second)
        hs[block, :, :256] = (dot_nt(x0, w_first) + h1[:, :256]).astype(BF16)
        hs[block, :, 256:384] = h1[:, 256:].astype(BF16)
        sq0 = (x0.astype(F32) * x0.astype(F32)).astype(BF16)
        sq1 = (x1.astype(F32) * x1.astype(F32)).astype(BF16)
        squares = dot(sq0, e_first) + dot(sq1, e_second)
        high = squares.astype(BF16).astype(F32)
        hs[block, :, 384:] = jnp.where(iota((nz * CONT, 128), 1) < 2, high, squares - high).astype(BF16)
        return res + dot(sel[0, block], x0) + dot(sel[1, block], x1)

    c_copy(y).start()
    res = project(yc, jnp.zeros((128, FB), F32))
    c_copy(y).wait_recv()
    res = project(2 * y + 1 - c, res)
    for copy in y_waits:
        copy.wait_recv()
    c_copy(1 - y).start()
    res = project(2 * (1 - y) + c, res)

    lax.fori_loop(1, 4, lambda k, _: (wx_copy(k).wait_recv(), 0)[1], 0)
    wc_copy().start()

    c_copy(1 - y).wait_recv()
    res = project(2 * (1 - y) + 1 - c, res)

    fg = fg_ref[...].astype(F32)
    sw = sw_ref[...].astype(F32)
    a_row = iota((128, FB), 0) % 16
    res = jnp.where(a_row == 4, jnp.concatenate([fg[0:1], fg[1:2]], 1), res)
    res = jnp.where(a_row == 5, jnp.concatenate([sw[0:1], sw[1:2]], 1), res).astype(BF16)
    for i in range(NB):
        auxs[i, rows : rows + 16, :] = res[i * 16 : (i + 1) * 16]

    def s4_copy(i, j):
        ob, oyc = lax.rem(b + i, NB), lax.rem(yc + j, 4)
        return remote(
            gs.at[ob, oyc],
            r4.at[yc, b],
            s4_ssem.at[i * 4 + j],
            s4_rsem.at[i * 4 + j],
            dev(lax.div(oyc, 2), z, lax.rem(oyc, 2), ob),
        )

    def s5_copy(i):
        ob = lax.rem(b + i, NB)
        return remote(auxs.at[ob], r5.at[b], s5_ssem.at[i], s5_rsem.at[i], dev(y, z, c, ob))

    def serve(pair):
        lhs = jnp.concatenate([perm[2 * pair], perm[2 * pair + 1]], 0)
        g = dot(lhs, hs[...].reshape(conts, 512)).astype(BF16)
        for u in range(2):
            half = g[u * 4 * rows : (u + 1) * 4 * rows]
            ob = 2 * pair + u
            gs[ob] = half[:, :384].reshape(4, rows, 384)
            squares4 = half[:, 384:].reshape(4, rows, 128)
            pick = jnp.zeros((rows, 128), BF16)
            for i in range(4):
                pick = jnp.where(yc == i, squares4[i], pick)
            auxs[ob, :rows, :128] = pick
            auxs[ob, :rows, 128:] = jnp.zeros((rows, 128), BF16)

    def serve_send(step, _):
        pair = lax.rem(lax.div(b, 2) + step, NB // 2)
        serve(pair)
        for u in range(2):
            away = lax.rem(2 * pair + u - b + NB, NB)
            s5_copy(away).start()
            s4_copy(away, 1).start()
            s4_copy(away, 2).start()
        return 0

    lax.fori_loop(1, NB // 2, serve_send, 0)
    serve(lax.div(b, 2))
    sibling = lax.rem(1 - 2 * lax.rem(b, 2) + NB, NB)
    s5_copy(sibling).start()
    for j in (1, 2):
        s4_copy(sibling, j).start()
        s4_copy(0, j).start()
    for j in (3, 0):
        lax.fori_loop(0, NB - 1, lambda k, _: (s4_copy(lax.rem(k + 3, NB - 1) + 1, j).start(), 0)[1], 0)
        if j:
            s4_copy(0, j).start()
    r4[yc, b] = gs[b, yc]
    r5[b] = auxs[b]

    lax.fori_loop(1, NB, lambda k, _: (s5_copy(k).wait_recv(), 0)[1], 0)
    stats = r5[0, :rows, :128].astype(F32)
    for i in range(1, NB):
        stats = stats + r5[i, :rows, :128].astype(F32)
    l128 = iota((rows, 128), 1)

    def inverse_rms(n):
        picked = jnp.where(l128 % 2 == n, jnp.where(l128 < 4, stats, 0.0), 0.0)
        return lax.rsqrt(jnp.sum(picked, -1, keepdims=True) / D + EPS)

    scale0, scale1 = inverse_rms(0), inverse_rms(1)
    scale_ab = jnp.where(l128 < 96, scale0, scale1)


    def silu(v):
        return v / (1.0 + jnp.exp(-v))

    mr, mc = iota((nz * 16, 2 * rows), 0), iota((nz * 16, 2 * rows), 1)
    m_in = mr % 4
    m_src = (m_in % 2) * rows + (mr // 16) * 2 + m_in // 2
    spread = [onehot((mc == m_src) & ((mr // 4) % 4 == j)) for j in range(4)]

    def hidden(g):
        acc = r4[g, 0].astype(F32)
        for i in range(1, NB):
            acc = acc + r4[g, i].astype(F32)
        h_ab = silu(acc[:, :128] * scale_ab) * (acc[:, 128:256] * scale_ab)
        last = acc[:, 256:] * scale1
        h_c = silu(last) * pltpu.roll(last, 64, 1)
        h_one = jnp.where(l128 < 32, pltpu.roll(h_ab, 32, 1), pltpu.roll(h_c, 32, 1))
        return jnp.concatenate([h_ab, h_one], 0).astype(BF16)

    wc_copy().wait_recv()
    left = jnp.zeros((nz * 16, FB), F32)
    right = jnp.zeros((nz * 16, FB), F32)
    for j in (1, 2, 3, 0):
        lax.fori_loop(0 if j else 1, NB, lambda k, _: (s4_copy(k, j).wait_recv(), 0)[1], 0)
        g = lax.rem(yc - j + 4, 4)
        hid = hidden(g)
        for i in range(4):
            lhs = dot(spread[i], hid).astype(BF16)[:, :HOLD]
            left = left + dot(lhs, wbuf[lax.div(g, 2), lax.rem(g, 2), i // 2, 2 * (i % 2)])
            right = right + dot(lhs, wbuf[lax.div(g, 2), lax.rem(g, 2), i // 2, 2 * (i % 2) + 1])
    ms[:, :, :FB] = left.astype(BF16).reshape(nz, 16, FB)
    ms[:, :, FB:] = right.astype(BF16).reshape(nz, 16, FB)

    def s6_copy(src, step, slot):
        return remote(src, r6.at[slot], s6_ssem.at[slot], s6_rsem.at[slot], dev(y, lax.rem(z + step + nz, nz), c, b))

    s6_waits = []

    def s6_send(way, dist, step, src):
        copy = s6_copy(src, way * step, (way * dist) % nz)
        copy.start()
        s6_waits.append(copy)

    for parent, kids in reversed(TREE):
        for kid in kids:
            for way in (1, -1):
                if kid <= far[way] and kid not in kids_of:
                    s6_send(way, kid, kid - parent, ms.at[lax.rem(z + way * kid + nz, nz)])

    def gathered(pick):
        return jnp.concatenate(
            [jnp.concatenate([pick(2 * j), pick(2 * j + 1)], 1) for j in range(4)], 0
        )

    resid4 = gathered(lambda i: r5[i, rows : rows + 16, :].astype(F32)[0:4])
    weight4 = gathered(
        lambda i: jnp.broadcast_to(
            r5[i, rows : rows + 16, :].astype(F32)[4:5] * r5[i, rows : rows + 16, :].astype(F32)[5:6], (4, FB)
        )
    )

    def s6_sum(way, kids, acc):
        for kid in kids:
            if kid <= far[way]:
                slot = (way * kid) % nz
                s6_copy(ms.at[z], 0, slot).wait_recv()
                acc = acc + r6[slot].astype(F32)
        return acc

    for at, (parent, kids) in reversed(list(enumerate(TREE[1:]))):
        for way in (1, -1):
            if parent <= far[way]:
                share = ms[lax.rem(z + way * parent + nz, nz)].astype(F32)
                ags[(1 - way) // 2, at] = s6_sum(way, kids, share).astype(BF16)
                s6_send(way, parent, parent, ags.at[(1 - way) // 2, at])
    moved = resid4 + ms[z].astype(F32)
    moved = s6_sum(-1, TREE[0][1][::-1], s6_sum(1, TREE[0][1][::-1], moved))
    ss = jnp.sum(moved * moved, -1, keepdims=True)
    st = jnp.sum(moved * weight4, -1, keepdims=True)
    ss = ss[0:4] + ss[4:8] + ss[8:12] + ss[12:16]
    st = st[0:4] + st[4:8] + st[8:12] + st[12:16]
    score = jnp.broadcast_to(st * lax.rsqrt(ss / D + EPS), (4, FB))
    for i in range(NB):
        j, half = i // 2, i % 2
        fs[i] = jnp.concatenate([moved[4 * j : 4 * j + 4, half * FB : (half + 1) * FB], score], 0)

    def s7_copy(k):
        other = lax.rem(b + k, NB)
        return remote(fs.at[other], r7.at[b], s7_ssem.at[k], s7_rsem.at[k], dev(y, z, c, other))

    lax.fori_loop(1, NB, lambda k, _: (s7_copy(k).start(), 0)[1], 0)
    r7[b] = fs[b]

    lax.fori_loop(1, 4, lambda k, _: (wy_copy(k).wait_send(), 0)[1], 0)
    lax.fori_loop(1, 4, lambda k, _: (wx_copy(k).wait_send(), 0)[1], 0)
    wc_copy().wait_send()
    lax.fori_loop(1, NB, lambda k, _: (s2_copy(k).wait_send(), 0)[1], 0)
    for copy in z_waits + y_waits:
        copy.wait_send()
    c_copy(0).wait_send()
    c_copy(1).wait_send()
    lax.fori_loop(1, 32, lambda k, _: (s4_copy(lax.div(k, 4), lax.rem(k, 4)).wait_send(), 0)[1], 0)
    lax.fori_loop(1, NB, lambda k, _: (s5_copy(k).wait_send(), 0)[1], 0)
    for copy in s6_waits:
        copy.wait_send()

    lax.fori_loop(1, NB, lambda k, _: (s7_copy(k).wait_recv(), 0)[1], 0)
    out_ref[...] = r7[...]
    lax.fori_loop(1, NB, lambda k, _: (s7_copy(k).wait_send(), 0)[1], 0)


def finish(parts_ref, out_ref, score_ref):
    out_ref[...] = jnp.concatenate([parts_ref[i, :4, :] for i in range(NB)], 0).astype(BF16)
    col = jnp.concatenate([parts_ref[i, 4:, :32] for i in range(NB)], 0)
    score_ref[...] = jnp.sum(jnp.where(iota((32, 32), 0) == iota((32, 32), 1), col, 0.0), 0, keepdims=True)


def shards(
    nz,
    resid,
    queries,
    new_kv,
    prefix_pool,
    page_table,
    prompt_len,
    tail_pool,
    tail_len,
    migration,
    out_w,
    mlp_gain,
    gate_w,
    up_w,
    down_w,
    final_gain,
    score_w,
):
    conts = 4 * nz * CONT
    rows = 2 * nz
    vmem = pl.BlockSpec(memory_space=pltpu.VMEM)
    hbm = pl.BlockSpec(memory_space=pl.ANY)
    dma = pltpu.SemaphoreType.DMA
    parts = pl.pallas_call(
        functools.partial(kernel, nz),
        out_shape=jax.ShapeDtypeStruct((NB, 8, FB), F32),
        in_specs=[hbm] * 16,
        out_specs=vmem,
        scratch_shapes=[
            pltpu.VMEM((PAGES * 256, HD), BF16),
            pltpu.VMEM((CONT * 256, HD), BF16),
            pltpu.VMEM((64, HD), BF16),
            pltpu.VMEM((64, HD), BF16),
            pltpu.VMEM((1, PAGES), jnp.int32),
            pltpu.SMEM((1, 1), jnp.int32),
            pltpu.SMEM((1, CONT), jnp.int32),
            pltpu.VMEM((HOLD, FB), BF16),
            pltpu.VMEM((2 * HD, D), BF16),
            pltpu.VMEM((32, D), BF16),
            pltpu.VMEM((conts // 128, 128), jnp.int32),
            pltpu.VMEM((HOLD, FB), BF16),
            pltpu.VMEM((HOLD, FB), BF16),
            pltpu.VMEM((16, 128), BF16),
            pltpu.VMEM((2, 128), BF16),
            pltpu.VMEM((2, 128), BF16),
            pltpu.VMEM((PAGES, 256), F32),
            pltpu.VMEM((64, PAGES * 256), F32),
            pltpu.VMEM((2, 2, 2, 4, HOLD, FB), BF16),
            pltpu.VMEM((NB, 32, FB), BF16),
            pltpu.VMEM((NB - 1, 32, FB), BF16),
            pltpu.VMEM((2, 4, nz, CONT, FB), BF16),
            pltpu.VMEM((NB, 4 * rows, conts), BF16),
            pltpu.VMEM((2, 4, 128, nz * CONT), BF16),
            pltpu.VMEM((4, nz * CONT, 512), BF16),
            pltpu.VMEM((NB, 4, rows, 384), BF16),
            pltpu.VMEM((4, NB, rows, 384), BF16),
            pltpu.VMEM((NB, rows + 16, FB), BF16),
            pltpu.VMEM((NB, rows + 16, FB), BF16),
            pltpu.VMEM((nz, 16, 512), BF16),
            pltpu.VMEM((2, len(TREE) - 1, 16, 512), BF16),
            pltpu.VMEM((nz, 16, 512), BF16),
            pltpu.VMEM((NB, 8, FB), F32),
            pltpu.VMEM((NB, 8, FB), F32),
            dma((16,)),
            dma((8,)),
            dma((8,)),
            dma((NB,)),
            dma((NB,)),
            dma((nz,)),
            dma((nz,)),
            dma((nz,)),
            dma((nz,)),
            dma((2,)),
            dma((2,)),
            dma((32,)),
            dma((32,)),
            dma((NB,)),
            dma((NB,)),
            dma((nz,)),
            dma((nz,)),
            dma((NB,)),
            dma((NB,)),
        ],
        compiler_params=pltpu.CompilerParams(
            collective_id=0, has_side_effects=True, vmem_limit_bytes=58 * 1024 * 1024
        ),
    )(
        prefix_pool.reshape(PAGES * 256, HD),
        tail_pool.reshape(CONT * 256, HD),
        queries.reshape(64, HD),
        new_kv.reshape(64, HD),
        page_table,
        prompt_len.reshape(1, 1),
        tail_len,
        down_w,
        out_w,
        resid,
        migration.reshape(conts // 128, 128),
        gate_w.T,
        up_w.T,
        mlp_gain.reshape(16, 128),
        final_gain.reshape(2, 128),
        score_w.reshape(2, 128),
    )
    out, score = pl.pallas_call(
        finish,
        out_shape=(
            jax.ShapeDtypeStruct((32, FB), BF16),
            jax.ShapeDtypeStruct((1, 32), F32),
        ),
        in_specs=[vmem],
        out_specs=(vmem, vmem),
    )(parts)
    return out, score.reshape(32)


def solution(mesh):
    nz = mesh.shape["dp"] // 4
    return jax.shard_map(
        functools.partial(shards, nz),
        mesh=mesh,
        in_specs=(
            P("dp", None),
            P("dp", "blk", None),
            P("dp", None, "blk", None),
            P("dp", None, None, "blk", None),
            P("dp", None),
            P("dp"),
            P("dp", None, None, "blk", None),
            P("dp", None),
            P(),
            P("blk", None),
            P(),
            P("blk", "dp"),
            P("blk", "dp"),
            P("dp", "blk"),
            P("blk"),
            P("blk"),
        ),
        out_specs=(P("dp", "blk"), P("dp")),
        check_vma=False,
    )
```

```python
import functools
import math

import jax
import jax.numpy as jnp
from jax import lax
from jax.experimental import pallas as pl
from jax.experimental.pallas import tpu as pltpu
from jax.sharding import PartitionSpec as P

MESH = pl.DeviceIdType.MESH
F32 = jnp.float32
BF16 = jnp.bfloat16
NEG = -1e30
EPS = 1e-06
D = 2048
NB = 8
FB = 256
HOLD = 96
CONT = 16
PAGES = 32
HD = 128
TREE = ((0, (5, 2, 1)), (2, (4, 3)), (5, (8, 7, 6)))


def iota(shape, dim):
    return lax.broadcasted_iota(jnp.int32, shape, dim)


def dot(a, b):
    return lax.dot_general(a, b, (((1,), (0,)), ((), ())), preferred_element_type=F32)


def dot_nt(a, b):
    return lax.dot_general(a, b, (((1,), (1,)), ((), ())), preferred_element_type=F32)


def onehot(cond):
    return jnp.where(cond, 1.0, 0.0).astype(BF16)


def kernel(
    nz,
    *refs,
):
    sources, out_ref, held, refs = refs[:16], refs[16], refs[17:33], refs[33:]
    (kv, tail, q_ref, new_ref, tab_ref, plen_ref, tlen_ref, down_ref, ow, resid_ref, mig_ref, gate_ref, up_ref, gain_ref, fg_ref, sw_ref) = held
    (bias, sbuf, wbuf, s2, r2, xall, perm, sel, hs, served, gs, r4, auxs, r5, ms, ags, r6, fs, r7, load_sem, w_ssem, w_rsem, s2_ssem, s2_rsem, z_ssem, z_rsem, y_ssem, y_rsem, c_ssem, c_rsem, s4_ssem, s4_rsem, s5_ssem, s5_rsem, s6_ssem, s6_rsem, s7_ssem, s7_rsem) = refs
    dp = lax.axis_index("dp")
    b = lax.axis_index("blk")
    c = lax.rem(dp, 2)
    z = lax.rem(lax.div(dp, 2), nz)
    y = lax.div(dp, 2 * nz)
    yc = 2 * y + c
    x, yh = lax.rem(b, 4), lax.div(b, 4)
    conts = 4 * nz * CONT
    rows = 2 * nz

    def dev(y_, z_, c_, b_):
        return ((y_ * nz + z_) * 2 + c_, b_)

    def remote(src, dst, ssem, rsem, target):
        return pltpu.make_async_remote_copy(
            src_ref=src, dst_ref=dst, send_sem=ssem, recv_sem=rsem, device_id=target, device_id_type=MESH
        )

    barrier = pltpu.get_barrier_semaphore()

    def greet_plane(k, _):
        other = lax.rem(b * 4 + yc + k, 32)
        oyc, ob = lax.rem(other, 4), lax.div(other, 4)
        pl.semaphore_signal(
            barrier, inc=1, device_id=dev(lax.div(oyc, 2), z, lax.rem(oyc, 2), ob), device_id_type=MESH
        )
        return 0

    def greet_line(k, _):
        pl.semaphore_signal(barrier, inc=1, device_id=dev(y, lax.rem(z + k, nz), c, b), device_id_type=MESH)
        return 0

    loads = [pltpu.make_async_copy(sources[i], held[i], load_sem.at[i]) for i in range(16)]
    for load in loads:
        load.start()

    lax.fori_loop(1, 32, greet_plane, 0)
    lax.fori_loop(1, nz, greet_line, 0)

    for load in loads[2:8]:
        load.wait()

    wbuf[y, c, yh, x] = down_ref[...]
    row4 = y * 2 + yh

    def wy_copy(k):
        other = lax.rem(row4 + k, 4)
        piece = wbuf.at[y, c, yh, x]
        return remote(piece, piece, w_ssem.at[k], w_rsem.at[k], dev(lax.div(other, 2), z, c, lax.rem(other, 2) * 4 + x))

    def wx_copy(k):
        piece = wbuf.at[:, c, :, x]
        return remote(piece, piece, w_ssem.at[3 + k], w_rsem.at[3 + k], dev(y, z, c, yh * 4 + lax.rem(x + k, 4)))

    def wc_copy():
        piece = wbuf.at[:, c]
        return remote(piece, piece, w_ssem.at[7], w_rsem.at[7], dev(y, z, 1 - c, b))

    r64, c64 = iota((64, 64), 0), iota((64, 64), 1)
    q_src = (r64 % 16) * 4 + ((r64 // 16) % 2) * 2 + r64 // 32
    q = dot(onehot(q_src == c64), q_ref[...]).astype(BF16)

    lane = iota((PAGES, 256), 1)
    page_no = iota((PAGES, PAGES), 0) == jnp.broadcast_to(tab_ref[...], (PAGES, PAGES))
    logical = jnp.sum(jnp.where(page_no, iota((PAGES, PAGES), 1), 0), -1, keepdims=True)
    limit = jnp.broadcast_to(plen_ref[0, 0] - logical * 128, (PAGES, 256))
    bias[...] = jnp.where((lane % 2 == 0) & (lane // 2 < limit), 0.0, NEG)
    unit = math.log2(math.e) / math.sqrt(HD)

    def widest(best, s):
        for i in range(s.shape[1] // 128):
            best = jnp.maximum(best, s[:, i * 128 : (i + 1) * 128])
        return best

    def next_lane(w):
        return jnp.concatenate(
            [pltpu.roll(w[:, i * 128 : (i + 1) * 128], 1, 1) for i in range(w.shape[1] // 128)], 1
        ).astype(BF16)

    loads[0].wait()
    best = jnp.full((64, 128), NEG, F32)
    for i in range(PAGES // 8):
        s = dot_nt(q, kv[i * 2048 : (i + 1) * 2048, :])
        for u in range(8):
            l = i * 8 + u
            part = s[:, u * 256 : (u + 1) * 256] + bias[l : l + 1, :]
            sbuf[:, l * 256 : (l + 1) * 256] = part
            best = widest(best, part)
    loads[1].wait()
    owner = iota((64, 256), 0) % 16
    t_lane = iota((1, 256), 1)
    s_tail = jnp.full((64, 256), NEG, F32)
    for i in range(CONT // 8):
        s = dot_nt(q, tail[i * 2048 : (i + 1) * 2048, :])
        for u in range(8):
            t = i * 8 + u
            t_bias = jnp.where((t_lane % 2 == 0) & (t_lane // 2 < tlen_ref[0, t]), 0.0, NEG)
            s_tail = jnp.where(owner == t, s[:, u * 256 : (u + 1) * 256] + t_bias, s_tail)

    new_cont, new_tok = c64 // 4, (c64 // 2) % 2
    new_ok = (c64 % 2 == 0) & (new_cont == r64 % 16) & (new_tok <= (r64 // 16) % 2)
    s_new = jnp.where(new_ok, dot_nt(q, new_ref[...]), NEG)
    top = jnp.maximum(
        jnp.max(widest(best, s_tail), -1, keepdims=True), jnp.max(s_new, -1, keepdims=True)
    )
    w_tail = jnp.exp2((s_tail - top) * unit)
    w_new = jnp.exp2((s_new - top) * unit)
    total = w_tail[:, :128] + w_tail[:, 128:]
    mixed = dot(pltpu.roll(w_new, 1, 1).astype(BF16), new_ref[...])
    for i in range(PAGES // 8):
        w = jnp.exp2((sbuf[:, i * 2048 : (i + 1) * 2048] - top) * unit)
        for u in range(16):
            total = total + w[:, u * 128 : (u + 1) * 128]
        mixed = mixed + dot(next_lane(w), kv[i * 2048 : (i + 1) * 2048, :])
    v_tail = next_lane(w_tail)
    for i in range(CONT // 8):
        w = jnp.concatenate(
            [jnp.where(owner == i * 8 + u, v_tail, jnp.zeros_like(v_tail)) for u in range(8)], 1
        )
        mixed = mixed + dot(w, tail[i * 2048 : (i + 1) * 2048, :])
    total = jnp.sum(total, -1, keepdims=True) + jnp.sum(w_new, -1, keepdims=True)
    attn = (mixed / total).astype(BF16)

    pl.semaphore_wait(barrier, 31 + nz - 1)

    loads[8].wait()
    for i in range(NB):
        cols = slice(i * FB, (i + 1) * FB)
        s2[i] = (dot(attn[:32], ow[:HD, cols]) + dot(attn[32:], ow[HD:, cols])).astype(BF16)

    def s2_copy(k):
        other = lax.rem(b + k, NB)
        return remote(s2.at[other], r2.at[k - 1], s2_ssem.at[k], s2_rsem.at[k], dev(y, z, c, other))

    lax.fori_loop(1, NB, lambda k, _: (s2_copy(k).start(), 0)[1], 0)
    lax.fori_loop(1, 4, lambda k, _: (wy_copy(k).start(), 0)[1], 0)

    for load in loads[9:]:
        load.wait()
    mig = mig_ref[...]
    home = mig // CONT
    stored = ((home // (2 * nz) * 2 + home % 2) * nz + (home // 2) % nz) * CONT + mig % CONT
    chunk = 4 * rows
    lines = mig.shape[0]
    p_row = iota((chunk, 1), 0)
    first = ((p_row // (2 * rows)) * nz + (p_row // 2) % nz) * 32 + ((p_row // rows) % 2) * 16 + p_row % 2
    line = onehot(iota((chunk, lines), 1) == first // 128)
    spread_mig = dot(line, (stored // 32).astype(F32).astype(BF16)) * 32.0 + dot(
        line, (stored % 32).astype(F32).astype(BF16)
    )
    slot_lane = iota((chunk, 128), 1) - first % 128
    for i in range(NB):
        column = jnp.sum(jnp.where(slot_lane == 2 * i, spread_mig, 0.0), -1, keepdims=True)
        perm[i] = onehot(iota((chunk, conts), 1) == column.astype(jnp.int32))
    gains = gain_ref[...].astype(F32)
    g_row = iota((16, 128), 0)
    gain = jnp.concatenate(
        [
            jnp.sum(jnp.where(g_row == 2 * b, gains, 0.0), 0, keepdims=True),
            jnp.sum(jnp.where(g_row == 2 * b + 1, gains, 0.0), 0, keepdims=True),
        ],
        1,
    )
    gate_t = (gate_ref[...].astype(F32) * gain).astype(BF16)
    up_t = (up_ref[...].astype(F32) * gain).astype(BF16)
    none32 = jnp.zeros((32, FB), BF16)
    none96 = jnp.zeros((96, FB), BF16)
    w_first = jnp.concatenate([gate_t, none32, up_t, none32], 0)
    w_second = jnp.concatenate(
        [none96, gate_t[:32], none96, up_t[:32], gate_t[32:], up_t[32:]], 0
    )
    r32, c32 = iota((32, 32), 0), iota((32, 32), 1)
    order = onehot((r32 % 16) * 2 + r32 // 16 == c32)
    resid = dot(order, resid_ref[:, pl.ds(pl.multiple_of(b * FB, FB), FB)])

    sel_r, sel_c = iota((128, NB * rows), 0), iota((128, NB * rows), 1)
    place = sel_r % 16
    own_rows = jnp.concatenate([perm[i, pl.ds(pl.multiple_of(yc * rows, rows), rows), :] for i in range(NB)], 0)
    for n in range(2):
        picked = dot(
            onehot(
                (place < 4)
                & (place % 2 == n)
                & (sel_c == (sel_r // 16) * rows + z * 2 + (place // 2) % 2)
            ),
            own_rows,
        ).astype(BF16)
        for i in range(4):
            sel[n, i] = picked[:, i * nz * CONT : (i + 1) * nz * CONT]

    lax.fori_loop(1, NB, lambda k, _: (s2_copy(k).wait_recv(), 0)[1], 0)
    mid = resid + s2[b].astype(F32)
    for k in range(1, NB):
        mid = mid + r2[k - 1].astype(F32)
    xall[0, yc, z] = mid[:16].astype(BF16)
    xall[1, yc, z] = mid[16:].astype(BF16)

    def z_copy(source, step, slot):
        piece = xall.at[:, yc, source]
        return remote(piece, piece, z_ssem.at[slot], z_rsem.at[slot], dev(y, lax.rem(z + step + nz, nz), c, b))

    def y_copy(source, slot):
        piece = xall.at[:, yc, source]
        return remote(piece, piece, y_ssem.at[slot], y_rsem.at[slot], dev(1 - y, z, c, b))

    def c_copy(i):
        piece = xall.at[:, 2 * i + c]
        return remote(piece, piece, c_ssem.at[i], c_rsem.at[i], dev(y, z, 1 - c, b))

    far = {1: nz // 2, -1: (nz - 1) // 2}
    z_waits, y_waits = [], []

    def z_forward(way, parent, kids):
        source = lax.rem(z - way * parent + nz, nz)
        for kid in kids:
            if kid <= far[way]:
                copy = z_copy(source, way * (kid - parent), (way * kid) % nz)
                copy.start()
                z_waits.append(copy)

    def y_forward(way, dist):
        slot = (way * dist) % nz
        copy = y_copy(lax.rem(z - way * dist + nz, nz), slot)
        copy.start()
        y_waits.append(copy)

    for way in (1, -1):
        z_forward(way, *TREE[0])
    y_forward(1, 0)
    kids_of = dict(TREE)
    for dist in (2, 5, 1, 4, 3, 6, 7, 8):
        for way in (1, -1):
            if dist <= far[way]:
                z_copy(z, 0, (way * dist) % nz).wait_recv()
                if dist in kids_of:
                    z_forward(way, dist, kids_of[dist])
                y_forward(way, dist)
        if dist == 1:
            lax.fori_loop(1, 4, lambda k, _: (wy_copy(k).wait_recv(), 0)[1], 0)
            lax.fori_loop(1, 4, lambda k, _: (wx_copy(k).start(), 0)[1], 0)

    e_lane = iota((FB, 128), 1)
    e_first = onehot((e_lane == 0) | (e_lane == 2))
    e_second = onehot((e_lane == 1) | (e_lane == 3))

    def project(block, res):
        x0 = xall[0, block].reshape(nz * CONT, FB)
        x1 = xall[1, block].reshape(nz * CONT, FB)
        h1 = dot_nt(x1, w_second)
        hs[block, :, :256] = (dot_nt(x0, w_first) + h1[:, :256]).astype(BF16)
        hs[block, :, 256:384] = h1[:, 256:].astype(BF16)
        sq0 = (x0.astype(F32) * x0.astype(F32)).astype(BF16)
        sq1 = (x1.astype(F32) * x1.astype(F32)).astype(BF16)
        squares = dot(sq0, e_first) + dot(sq1, e_second)
        high = squares.astype(BF16).astype(F32)
        hs[block, :, 384:] = jnp.where(iota((nz * CONT, 128), 1) < 2, high, squares - high).astype(BF16)
        return res + dot(sel[0, block], x0) + dot(sel[1, block], x1)

    c_copy(y).start()
    res = project(yc, jnp.zeros((128, FB), F32))
    c_copy(y).wait_recv()
    res = project(2 * y + 1 - c, res)

    half = 2 * nz * CONT

    def share(pair, side):
        cols = pl.ds(pl.multiple_of(side * half, half), half)
        lhs = jnp.concatenate([perm[2 * pair, :, cols], perm[2 * pair + 1, :, cols]], 0)
        return dot(lhs, hs[pl.ds(2 * side, 2)].reshape(half, 512))

    def first_share(pair, _):
        served[pair] = share(pair, y)
        return 0

    lax.fori_loop(0, NB // 2, first_share, 0)
    for copy in y_waits:
        copy.wait_recv()
    c_copy(1 - y).start()
    res = project(2 * (1 - y) + c, res)

    c_copy(1 - y).wait_recv()
    res = project(2 * (1 - y) + 1 - c, res)

    fg = fg_ref[...].astype(F32)
    sw = sw_ref[...].astype(F32)
    a_row = iota((128, FB), 0) % 16
    res = jnp.where(a_row == 4, jnp.concatenate([fg[0:1], fg[1:2]], 1), res)
    res = jnp.where(a_row == 5, jnp.concatenate([sw[0:1], sw[1:2]], 1), res).astype(BF16)
    for i in range(NB):
        auxs[i, rows : rows + 16, :] = res[i * 16 : (i + 1) * 16]

    def s4_copy(i, j):
        ob, oyc = lax.rem(b + i, NB), lax.rem(yc + j, 4)
        return remote(
            gs.at[ob, oyc],
            r4.at[yc, b],
            s4_ssem.at[i * 4 + j],
            s4_rsem.at[i * 4 + j],
            dev(lax.div(oyc, 2), z, lax.rem(oyc, 2), ob),
        )

    def s5_copy(i):
        ob = lax.rem(b + i, NB)
        return remote(auxs.at[ob], r5.at[b], s5_ssem.at[i], s5_rsem.at[i], dev(y, z, c, ob))

    def serve(pair):
        g = (served[pair] + share(pair, 1 - y)).astype(BF16)
        for u in range(2):
            quads = g[u * 4 * rows : (u + 1) * 4 * rows]
            ob = 2 * pair + u
            gs[ob] = quads[:, :384].reshape(4, rows, 384)
            squares4 = quads[:, 384:].reshape(4, rows, 128)
            pick = jnp.zeros((rows, 128), BF16)
            for i in range(4):
                pick = jnp.where(yc == i, squares4[i], pick)
            auxs[ob, :rows, :128] = pick
            auxs[ob, :rows, 128:] = jnp.zeros((rows, 128), BF16)

    def serve_send(step, _):
        pair = lax.rem(lax.div(b, 2) + step, NB // 2)
        serve(pair)
        for u in range(2):
            away = lax.rem(2 * pair + u - b + NB, NB)
            s5_copy(away).start()
            s4_copy(away, 1).start()
            s4_copy(away, 2).start()
        return 0

    lax.fori_loop(1, NB // 2, serve_send, 0)
    serve(lax.div(b, 2))
    sibling = lax.rem(1 - 2 * lax.rem(b, 2) + NB, NB)
    s5_copy(sibling).start()
    for j in (1, 2):
        s4_copy(sibling, j).start()
        s4_copy(0, j).start()
    lax.fori_loop(1, 4, lambda k, _: (wx_copy(k).wait_recv(), 0)[1], 0)
    wc_copy().start()
    for j in (3, 0):
        lax.fori_loop(0, NB - 1, lambda k, _: (s4_copy(lax.rem(k + 3, NB - 1) + 1, j).start(), 0)[1], 0)
        if j:
            s4_copy(0, j).start()
    r4[yc, b] = gs[b, yc]
    r5[b] = auxs[b]

    lax.fori_loop(1, NB, lambda k, _: (s5_copy(k).wait_recv(), 0)[1], 0)
    stats = r5[0, :rows, :128].astype(F32)
    for i in range(1, NB):
        stats = stats + r5[i, :rows, :128].astype(F32)
    l128 = iota((rows, 128), 1)

    def inverse_rms(n):
        picked = jnp.where(l128 % 2 == n, jnp.where(l128 < 4, stats, 0.0), 0.0)
        return lax.rsqrt(jnp.sum(picked, -1, keepdims=True) / D + EPS)

    scale0, scale1 = inverse_rms(0), inverse_rms(1)
    scale_ab = jnp.where(l128 < 96, scale0, scale1)


    def silu(v):
        return v / (1.0 + jnp.exp(-v))

    mr, mc = iota((nz * 16, 2 * rows), 0), iota((nz * 16, 2 * rows), 1)
    m_in = mr % 4
    m_src = (m_in % 2) * rows + (mr // 16) * 2 + m_in // 2
    spread = [onehot((mc == m_src) & ((mr // 4) % 4 == j)) for j in range(4)]

    def hidden(g):
        acc = r4[g, 0].astype(F32)
        for i in range(1, NB):
            acc = acc + r4[g, i].astype(F32)
        h_ab = silu(acc[:, :128] * scale_ab) * (acc[:, 128:256] * scale_ab)
        last = acc[:, 256:] * scale1
        h_c = silu(last) * pltpu.roll(last, 64, 1)
        h_one = jnp.where(l128 < 32, pltpu.roll(h_ab, 32, 1), pltpu.roll(h_c, 32, 1))
        return jnp.concatenate([h_ab, h_one], 0).astype(BF16)

    wc_copy().wait_recv()
    left = jnp.zeros((nz * 16, FB), F32)
    right = jnp.zeros((nz * 16, FB), F32)
    for j in (1, 2, 3, 0):
        lax.fori_loop(0 if j else 1, NB, lambda k, _: (s4_copy(k, j).wait_recv(), 0)[1], 0)
        g = lax.rem(yc - j + 4, 4)
        hid = hidden(g)
        for i in range(4):
            lhs = dot(spread[i], hid).astype(BF16)[:, :HOLD]
            left = left + dot(lhs, wbuf[lax.div(g, 2), lax.rem(g, 2), i // 2, 2 * (i % 2)])
            right = right + dot(lhs, wbuf[lax.div(g, 2), lax.rem(g, 2), i // 2, 2 * (i % 2) + 1])
    ms[:, :, :FB] = left.astype(BF16).reshape(nz, 16, FB)
    ms[:, :, FB:] = right.astype(BF16).reshape(nz, 16, FB)

    def s6_copy(src, step, slot):
        return remote(src, r6.at[slot], s6_ssem.at[slot], s6_rsem.at[slot], dev(y, lax.rem(z + step + nz, nz), c, b))

    s6_waits = []

    def s6_send(way, dist, step, src):
        copy = s6_copy(src, way * step, (way * dist) % nz)
        copy.start()
        s6_waits.append(copy)

    for parent, kids in reversed(TREE):
        for kid in kids:
            for way in (1, -1):
                if kid <= far[way] and kid not in kids_of:
                    s6_send(way, kid, kid - parent, ms.at[lax.rem(z + way * kid + nz, nz)])

    def gathered(pick):
        return jnp.concatenate(
            [jnp.concatenate([pick(2 * j), pick(2 * j + 1)], 1) for j in range(4)], 0
        )

    resid4 = gathered(lambda i: r5[i, rows : rows + 16, :].astype(F32)[0:4])
    weight4 = gathered(
        lambda i: jnp.broadcast_to(
            r5[i, rows : rows + 16, :].astype(F32)[4:5] * r5[i, rows : rows + 16, :].astype(F32)[5:6], (4, FB)
        )
    )

    def s6_sum(way, kids, acc):
        for kid in kids:
            if kid <= far[way]:
                slot = (way * kid) % nz
                s6_copy(ms.at[z], 0, slot).wait_recv()
                acc = acc + r6[slot].astype(F32)
        return acc

    for at, (parent, kids) in reversed(list(enumerate(TREE[1:]))):
        for way in (1, -1):
            if parent <= far[way]:
                share = ms[lax.rem(z + way * parent + nz, nz)].astype(F32)
                ags[(1 - way) // 2, at] = s6_sum(way, kids, share).astype(BF16)
                s6_send(way, parent, parent, ags.at[(1 - way) // 2, at])
    moved = resid4 + ms[z].astype(F32)
    moved = s6_sum(-1, TREE[0][1][::-1], s6_sum(1, TREE[0][1][::-1], moved))
    ss = jnp.sum(moved * moved, -1, keepdims=True)
    st = jnp.sum(moved * weight4, -1, keepdims=True)
    ss = ss[0:4] + ss[4:8] + ss[8:12] + ss[12:16]
    st = st[0:4] + st[4:8] + st[8:12] + st[12:16]
    score = jnp.broadcast_to(st * lax.rsqrt(ss / D + EPS), (4, FB))
    for i in range(NB):
        j, half = i // 2, i % 2
        fs[i] = jnp.concatenate([moved[4 * j : 4 * j + 4, half * FB : (half + 1) * FB], score], 0)

    def s7_copy(k):
        other = lax.rem(b + k, NB)
        return remote(fs.at[other], r7.at[b], s7_ssem.at[k], s7_rsem.at[k], dev(y, z, c, other))

    lax.fori_loop(1, NB, lambda k, _: (s7_copy(k).start(), 0)[1], 0)
    r7[b] = fs[b]

    lax.fori_loop(1, 4, lambda k, _: (wy_copy(k).wait_send(), 0)[1], 0)
    lax.fori_loop(1, 4, lambda k, _: (wx_copy(k).wait_send(), 0)[1], 0)
    wc_copy().wait_send()
    lax.fori_loop(1, NB, lambda k, _: (s2_copy(k).wait_send(), 0)[1], 0)
    for copy in z_waits + y_waits:
        copy.wait_send()
    c_copy(0).wait_send()
    c_copy(1).wait_send()
    lax.fori_loop(1, 32, lambda k, _: (s4_copy(lax.div(k, 4), lax.rem(k, 4)).wait_send(), 0)[1], 0)
    lax.fori_loop(1, NB, lambda k, _: (s5_copy(k).wait_send(), 0)[1], 0)
    for copy in s6_waits:
        copy.wait_send()

    lax.fori_loop(1, NB, lambda k, _: (s7_copy(k).wait_recv(), 0)[1], 0)
    out_ref[...] = r7[...]
    lax.fori_loop(1, NB, lambda k, _: (s7_copy(k).wait_send(), 0)[1], 0)


def finish(parts_ref, out_ref, score_ref):
    out_ref[...] = jnp.concatenate([parts_ref[i, :4, :] for i in range(NB)], 0).astype(BF16)
    col = jnp.concatenate([parts_ref[i, 4:, :32] for i in range(NB)], 0)
    score_ref[...] = jnp.sum(jnp.where(iota((32, 32), 0) == iota((32, 32), 1), col, 0.0), 0, keepdims=True)


def shards(
    nz,
    resid,
    queries,
    new_kv,
    prefix_pool,
    page_table,
    prompt_len,
    tail_pool,
    tail_len,
    migration,
    out_w,
    mlp_gain,
    gate_w,
    up_w,
    down_w,
    final_gain,
    score_w,
):
    conts = 4 * nz * CONT
    rows = 2 * nz
    vmem = pl.BlockSpec(memory_space=pltpu.VMEM)
    hbm = pl.BlockSpec(memory_space=pl.ANY)
    dma = pltpu.SemaphoreType.DMA
    parts = pl.pallas_call(
        functools.partial(kernel, nz),
        out_shape=jax.ShapeDtypeStruct((NB, 8, FB), F32),
        in_specs=[hbm] * 16,
        out_specs=vmem,
        scratch_shapes=[
            pltpu.VMEM((PAGES * 256, HD), BF16),
            pltpu.VMEM((CONT * 256, HD), BF16),
            pltpu.VMEM((64, HD), BF16),
            pltpu.VMEM((64, HD), BF16),
            pltpu.VMEM((1, PAGES), jnp.int32),
            pltpu.SMEM((1, 1), jnp.int32),
            pltpu.SMEM((1, CONT), jnp.int32),
            pltpu.VMEM((HOLD, FB), BF16),
            pltpu.VMEM((2 * HD, D), BF16),
            pltpu.VMEM((32, D), BF16),
            pltpu.VMEM((conts // 128, 128), jnp.int32),
            pltpu.VMEM((HOLD, FB), BF16),
            pltpu.VMEM((HOLD, FB), BF16),
            pltpu.VMEM((16, 128), BF16),
            pltpu.VMEM((2, 128), BF16),
            pltpu.VMEM((2, 128), BF16),
            pltpu.VMEM((PAGES, 256), F32),
            pltpu.VMEM((64, PAGES * 256), F32),
            pltpu.VMEM((2, 2, 2, 4, HOLD, FB), BF16),
            pltpu.VMEM((NB, 32, FB), BF16),
            pltpu.VMEM((NB - 1, 32, FB), BF16),
            pltpu.VMEM((2, 4, nz, CONT, FB), BF16),
            pltpu.VMEM((NB, 4 * rows, conts), BF16),
            pltpu.VMEM((2, 4, 128, nz * CONT), BF16),
            pltpu.VMEM((4, nz * CONT, 512), BF16),
            pltpu.VMEM((NB // 2, 8 * rows, 512), F32),
            pltpu.VMEM((NB, 4, rows, 384), BF16),
            pltpu.VMEM((4, NB, rows, 384), BF16),
            pltpu.VMEM((NB, rows + 16, FB), BF16),
            pltpu.VMEM((NB, rows + 16, FB), BF16),
            pltpu.VMEM((nz, 16, 512), BF16),
            pltpu.VMEM((2, len(TREE) - 1, 16, 512), BF16),
            pltpu.VMEM((nz, 16, 512), BF16),
            pltpu.VMEM((NB, 8, FB), F32),
            pltpu.VMEM((NB, 8, FB), F32),
            dma((16,)),
            dma((8,)),
            dma((8,)),
            dma((NB,)),
            dma((NB,)),
            dma((nz,)),
            dma((nz,)),
            dma((nz,)),
            dma((nz,)),
            dma((2,)),
            dma((2,)),
            dma((32,)),
            dma((32,)),
            dma((NB,)),
            dma((NB,)),
            dma((nz,)),
            dma((nz,)),
            dma((NB,)),
            dma((NB,)),
        ],
        compiler_params=pltpu.CompilerParams(
            collective_id=0, has_side_effects=True, vmem_limit_bytes=58 * 1024 * 1024
        ),
    )(
        prefix_pool.reshape(PAGES * 256, HD),
        tail_pool.reshape(CONT * 256, HD),
        queries.reshape(64, HD),
        new_kv.reshape(64, HD),
        page_table,
        prompt_len.reshape(1, 1),
        tail_len,
        down_w,
        out_w,
        resid,
        migration.reshape(conts // 128, 128),
        gate_w.T,
        up_w.T,
        mlp_gain.reshape(16, 128),
        final_gain.reshape(2, 128),
        score_w.reshape(2, 128),
    )
    out, score = pl.pallas_call(
        finish,
        out_shape=(
            jax.ShapeDtypeStruct((32, FB), BF16),
            jax.ShapeDtypeStruct((1, 32), F32),
        ),
        in_specs=[vmem],
        out_specs=(vmem, vmem),
    )(parts)
    return out, score.reshape(32)


def solution(mesh):
    nz = mesh.shape["dp"] // 4
    return jax.shard_map(
        functools.partial(shards, nz),
        mesh=mesh,
        in_specs=(
            P("dp", None),
            P("dp", "blk", None),
            P("dp", None, "blk", None),
            P("dp", None, None, "blk", None),
            P("dp", None),
            P("dp"),
            P("dp", None, None, "blk", None),
            P("dp", None),
            P(),
            P("blk", None),
            P(),
            P("blk", "dp"),
            P("blk", "dp"),
            P("dp", "blk"),
            P("blk"),
            P("blk"),
        ),
        out_specs=(P("dp", "blk"), P("dp")),
        check_vma=False,
    )
```

```python
import functools
import math

import jax
import jax.numpy as jnp
from jax import lax
from jax.experimental import pallas as pl
from jax.experimental.pallas import tpu as pltpu
from jax.sharding import PartitionSpec as P

MESH = pl.DeviceIdType.MESH
F32 = jnp.float32
BF16 = jnp.bfloat16
NEG = -1e30
EPS = 1e-06
D = 2048
NB = 8
FB = 256
HOLD = 96
CONT = 16
PAGES = 32
HD = 128
TREE = ((0, (5, 2, 1)), (2, (4, 3)), (5, (8, 7, 6)))


def iota(shape, dim):
    return lax.broadcasted_iota(jnp.int32, shape, dim)


def dot(a, b):
    return lax.dot_general(a, b, (((1,), (0,)), ((), ())), preferred_element_type=F32)


def dot_nt(a, b):
    return lax.dot_general(a, b, (((1,), (1,)), ((), ())), preferred_element_type=F32)


def onehot(cond):
    return jnp.where(cond, 1.0, 0.0).astype(BF16)


def kernel(
    nz,
    *refs,
):
    sources, out_ref, held, refs = refs[:16], refs[16], refs[17:33], refs[33:]
    (kv, tail, q_ref, new_ref, tab_ref, plen_ref, tlen_ref, down_ref, ow, resid_ref, mig_ref, gate_ref, up_ref, gain_ref, fg_ref, sw_ref) = held
    (bias, sbuf, wbuf, s2, r2, xall, perm, sel, hs, served, gs, r4, auxb, auxs, r5, ms, ags, r6, fs, r7, load_sem, w_ssem, w_rsem, s2_ssem, s2_rsem, z_ssem, z_rsem, y_ssem, y_rsem, c_ssem, c_rsem, s4_ssem, s4_rsem, s5_ssem, s5_rsem, s6_ssem, s6_rsem, s7_ssem, s7_rsem) = refs
    dp = lax.axis_index("dp")
    b = lax.axis_index("blk")
    c = lax.rem(dp, 2)
    z = lax.rem(lax.div(dp, 2), nz)
    y = lax.div(dp, 2 * nz)
    yc = 2 * y + c
    x, yh = lax.rem(b, 4), lax.div(b, 4)
    conts = 4 * nz * CONT
    rows = 2 * nz

    def dev(y_, z_, c_, b_):
        return ((y_ * nz + z_) * 2 + c_, b_)

    def remote(src, dst, ssem, rsem, target):
        return pltpu.make_async_remote_copy(
            src_ref=src, dst_ref=dst, send_sem=ssem, recv_sem=rsem, device_id=target, device_id_type=MESH
        )

    barrier = pltpu.get_barrier_semaphore()

    def greet_plane(k, _):
        other = lax.rem(b * 4 + yc + k, 32)
        oyc, ob = lax.rem(other, 4), lax.div(other, 4)
        pl.semaphore_signal(
            barrier, inc=1, device_id=dev(lax.div(oyc, 2), z, lax.rem(oyc, 2), ob), device_id_type=MESH
        )
        return 0

    def greet_line(k, _):
        pl.semaphore_signal(barrier, inc=1, device_id=dev(y, lax.rem(z + k, nz), c, b), device_id_type=MESH)
        return 0

    loads = [pltpu.make_async_copy(sources[i], held[i], load_sem.at[i]) for i in range(16)]
    for load in loads:
        load.start()

    lax.fori_loop(1, 32, greet_plane, 0)
    lax.fori_loop(1, nz, greet_line, 0)

    for load in loads[2:8]:
        load.wait()

    wbuf[y, c, yh, x] = down_ref[...]
    row4 = y * 2 + yh

    def wy_copy(k):
        other = lax.rem(row4 + k, 4)
        piece = wbuf.at[y, c, yh, x]
        return remote(piece, piece, w_ssem.at[k], w_rsem.at[k], dev(lax.div(other, 2), z, c, lax.rem(other, 2) * 4 + x))

    def wx_copy(k):
        piece = wbuf.at[:, c, :, x]
        return remote(piece, piece, w_ssem.at[3 + k], w_rsem.at[3 + k], dev(y, z, c, yh * 4 + lax.rem(x + k, 4)))

    def wc_copy():
        piece = wbuf.at[:, c]
        return remote(piece, piece, w_ssem.at[7], w_rsem.at[7], dev(y, z, 1 - c, b))

    r64, c64 = iota((64, 64), 0), iota((64, 64), 1)
    q_src = (r64 % 16) * 4 + ((r64 // 16) % 2) * 2 + r64 // 32
    q = dot(onehot(q_src == c64), q_ref[...]).astype(BF16)

    lane = iota((PAGES, 256), 1)
    page_no = iota((PAGES, PAGES), 0) == jnp.broadcast_to(tab_ref[...], (PAGES, PAGES))
    logical = jnp.sum(jnp.where(page_no, iota((PAGES, PAGES), 1), 0), -1, keepdims=True)
    limit = jnp.broadcast_to(plen_ref[0, 0] - logical * 128, (PAGES, 256))
    bias[...] = jnp.where((lane % 2 == 0) & (lane // 2 < limit), 0.0, NEG)
    unit = math.log2(math.e) / math.sqrt(HD)

    def widest(best, s):
        for i in range(s.shape[1] // 128):
            best = jnp.maximum(best, s[:, i * 128 : (i + 1) * 128])
        return best

    def next_lane(w):
        return jnp.concatenate(
            [pltpu.roll(w[:, i * 128 : (i + 1) * 128], 1, 1) for i in range(w.shape[1] // 128)], 1
        ).astype(BF16)

    loads[0].wait()
    best = jnp.full((64, 128), NEG, F32)
    for i in range(PAGES // 8):
        s = dot_nt(q, kv[i * 2048 : (i + 1) * 2048, :])
        for u in range(8):
            l = i * 8 + u
            part = s[:, u * 256 : (u + 1) * 256] + bias[l : l + 1, :]
            sbuf[:, l * 256 : (l + 1) * 256] = part
            best = widest(best, part)
    loads[1].wait()
    owner = iota((64, 256), 0) % 16
    t_lane = iota((1, 256), 1)
    s_tail = jnp.full((64, 256), NEG, F32)
    for i in range(CONT // 8):
        s = dot_nt(q, tail[i * 2048 : (i + 1) * 2048, :])
        for u in range(8):
            t = i * 8 + u
            t_bias = jnp.where((t_lane % 2 == 0) & (t_lane // 2 < tlen_ref[0, t]), 0.0, NEG)
            s_tail = jnp.where(owner == t, s[:, u * 256 : (u + 1) * 256] + t_bias, s_tail)

    new_cont, new_tok = c64 // 4, (c64 // 2) % 2
    new_ok = (c64 % 2 == 0) & (new_cont == r64 % 16) & (new_tok <= (r64 // 16) % 2)
    s_new = jnp.where(new_ok, dot_nt(q, new_ref[...]), NEG)
    top = jnp.maximum(
        jnp.max(widest(best, s_tail), -1, keepdims=True), jnp.max(s_new, -1, keepdims=True)
    )
    w_tail = jnp.exp2((s_tail - top) * unit)
    w_new = jnp.exp2((s_new - top) * unit)
    total = w_tail[:, :128] + w_tail[:, 128:]
    mixed = dot(pltpu.roll(w_new, 1, 1).astype(BF16), new_ref[...])
    for i in range(PAGES // 8):
        w = jnp.exp2((sbuf[:, i * 2048 : (i + 1) * 2048] - top) * unit)
        for u in range(16):
            total = total + w[:, u * 128 : (u + 1) * 128]
        mixed = mixed + dot(next_lane(w), kv[i * 2048 : (i + 1) * 2048, :])
    v_tail = next_lane(w_tail)
    for i in range(CONT // 8):
        w = jnp.concatenate(
            [jnp.where(owner == i * 8 + u, v_tail, jnp.zeros_like(v_tail)) for u in range(8)], 1
        )
        mixed = mixed + dot(w, tail[i * 2048 : (i + 1) * 2048, :])
    total = jnp.sum(total, -1, keepdims=True) + jnp.sum(w_new, -1, keepdims=True)
    attn = (mixed / total).astype(BF16)

    pl.semaphore_wait(barrier, 31 + nz - 1)

    loads[8].wait()
    for i in range(NB):
        cols = slice(i * FB, (i + 1) * FB)
        s2[i] = (dot(attn[:32], ow[:HD, cols]) + dot(attn[32:], ow[HD:, cols])).astype(BF16)

    def s2_copy(k):
        other = lax.rem(b + k, NB)
        return remote(s2.at[other], r2.at[k - 1], s2_ssem.at[k], s2_rsem.at[k], dev(y, z, c, other))

    lax.fori_loop(1, NB, lambda k, _: (s2_copy(k).start(), 0)[1], 0)
    lax.fori_loop(1, 4, lambda k, _: (wy_copy(k).start(), 0)[1], 0)

    for load in loads[9:]:
        load.wait()
    mig = mig_ref[...]
    home = mig // CONT
    stored = ((home // (2 * nz) * 2 + home % 2) * nz + (home // 2) % nz) * CONT + mig % CONT
    chunk = 4 * rows
    lines = mig.shape[0]
    p_row = iota((chunk, 1), 0)
    first = ((p_row // (2 * rows)) * nz + (p_row // 2) % nz) * 32 + ((p_row // rows) % 2) * 16 + p_row % 2
    line = onehot(iota((chunk, lines), 1) == first // 128)
    spread_mig = dot(line, (stored // 32).astype(F32).astype(BF16)) * 32.0 + dot(
        line, (stored % 32).astype(F32).astype(BF16)
    )
    slot_lane = iota((chunk, 128), 1) - first % 128
    for i in range(NB):
        column = jnp.sum(jnp.where(slot_lane == 2 * i, spread_mig, 0.0), -1, keepdims=True)
        perm[i] = onehot(iota((chunk, conts), 1) == column.astype(jnp.int32))
    gains = gain_ref[...].astype(F32)
    g_row = iota((16, 128), 0)
    gain = jnp.concatenate(
        [
            jnp.sum(jnp.where(g_row == 2 * b, gains, 0.0), 0, keepdims=True),
            jnp.sum(jnp.where(g_row == 2 * b + 1, gains, 0.0), 0, keepdims=True),
        ],
        1,
    )
    gate_t = (gate_ref[...].astype(F32) * gain).astype(BF16)
    up_t = (up_ref[...].astype(F32) * gain).astype(BF16)
    none32 = jnp.zeros((32, FB), BF16)
    none96 = jnp.zeros((96, FB), BF16)
    w_first = jnp.concatenate([gate_t, none32, up_t, none32], 0)
    w_second = jnp.concatenate(
        [none96, gate_t[:32], none96, up_t[:32], gate_t[32:], up_t[32:]], 0
    )
    r32, c32 = iota((32, 32), 0), iota((32, 32), 1)
    order = onehot((r32 % 16) * 2 + r32 // 16 == c32)
    resid = dot(order, resid_ref[:, pl.ds(pl.multiple_of(b * FB, FB), FB)])

    sel_r, sel_c = iota((128, NB * rows), 0), iota((128, NB * rows), 1)
    place = sel_r % 16
    own_rows = jnp.concatenate([perm[i, pl.ds(pl.multiple_of(yc * rows, rows), rows), :] for i in range(NB)], 0)
    for n in range(2):
        picked = dot(
            onehot(
                (place >= 4)
                & (place < 12)
                & (place % 2 == n)
                & (sel_c == (sel_r // 16) * rows + z * 2 + (place // 2) % 2)
            ),
            own_rows,
        ).astype(BF16)
        for i in range(4):
            sel[n, i] = picked[:, i * nz * CONT : (i + 1) * nz * CONT]

    lax.fori_loop(1, NB, lambda k, _: (s2_copy(k).wait_recv(), 0)[1], 0)
    mid = resid + s2[b].astype(F32)
    for k in range(1, NB):
        mid = mid + r2[k - 1].astype(F32)
    xall[0, yc, z] = mid[:16].astype(BF16)
    xall[1, yc, z] = mid[16:].astype(BF16)

    def z_copy(source, step, slot):
        piece = xall.at[:, yc, source]
        return remote(piece, piece, z_ssem.at[slot], z_rsem.at[slot], dev(y, lax.rem(z + step + nz, nz), c, b))

    def y_copy(source, slot):
        piece = xall.at[:, yc, source]
        return remote(piece, piece, y_ssem.at[slot], y_rsem.at[slot], dev(1 - y, z, c, b))

    def c_copy(i):
        piece = xall.at[:, 2 * i + c]
        return remote(piece, piece, c_ssem.at[i], c_rsem.at[i], dev(y, z, 1 - c, b))

    far = {1: nz // 2, -1: (nz - 1) // 2}
    z_waits, y_waits = [], []

    def z_forward(way, parent, kids):
        source = lax.rem(z - way * parent + nz, nz)
        for kid in kids:
            if kid <= far[way]:
                copy = z_copy(source, way * (kid - parent), (way * kid) % nz)
                copy.start()
                z_waits.append(copy)

    def y_forward(way, dist):
        slot = (way * dist) % nz
        copy = y_copy(lax.rem(z - way * dist + nz, nz), slot)
        copy.start()
        y_waits.append(copy)

    for way in (1, -1):
        z_forward(way, *TREE[0])
    y_forward(1, 0)
    kids_of = dict(TREE)
    for dist in (2, 5, 1, 4, 3, 6, 7, 8):
        for way in (1, -1):
            if dist <= far[way]:
                z_copy(z, 0, (way * dist) % nz).wait_recv()
                if dist in kids_of:
                    z_forward(way, dist, kids_of[dist])
                y_forward(way, dist)
        if dist == 1:
            lax.fori_loop(1, 4, lambda k, _: (wy_copy(k).wait_recv(), 0)[1], 0)
            lax.fori_loop(1, 4, lambda k, _: (wx_copy(k).start(), 0)[1], 0)

    e_lane = iota((FB, 128), 1)
    e_first = onehot((e_lane == 0) | (e_lane == 2))
    e_second = onehot((e_lane == 1) | (e_lane == 3))

    def project(block, res):
        x0 = xall[0, block].reshape(nz * CONT, FB)
        x1 = xall[1, block].reshape(nz * CONT, FB)
        h1 = dot_nt(x1, w_second)
        hs[block, :, :256] = (dot_nt(x0, w_first) + h1[:, :256]).astype(BF16)
        hs[block, :, 256:384] = h1[:, 256:].astype(BF16)
        sq0 = (x0.astype(F32) * x0.astype(F32)).astype(BF16)
        sq1 = (x1.astype(F32) * x1.astype(F32)).astype(BF16)
        squares = dot(sq0, e_first) + dot(sq1, e_second)
        high = squares.astype(BF16).astype(F32)
        hs[block, :, 384:] = jnp.where(iota((nz * CONT, 128), 1) < 2, high, squares - high).astype(BF16)
        return res + dot(sel[0, block], x0) + dot(sel[1, block], x1)

    c_copy(y).start()
    res = project(yc, jnp.zeros((128, FB), F32))
    c_copy(y).wait_recv()
    res = project(2 * y + 1 - c, res)

    half = 2 * nz * CONT

    def share(pair, side):
        cols = pl.ds(pl.multiple_of(side * half, half), half)
        lhs = jnp.concatenate([perm[2 * pair, :, cols], perm[2 * pair + 1, :, cols]], 0)
        return dot(lhs, hs[pl.ds(2 * side, 2)].reshape(half, 512))

    def first_share(pair, _):
        served[pair] = share(pair, y)
        return 0

    lax.fori_loop(0, NB // 2, first_share, 0)
    for copy in y_waits:
        copy.wait_recv()
    c_copy(1 - y).start()
    res = project(2 * (1 - y) + c, res)

    c_copy(1 - y).wait_recv()
    res = project(2 * (1 - y) + 1 - c, res)

    fg = fg_ref[...].astype(F32)
    sw = sw_ref[...].astype(F32)
    a_row = iota((128, 128), 0) % 16
    aux = jnp.where(a_row < 8, res[:, :128], res[:, 128:])
    for i, line in enumerate((fg[0:1], fg[1:2], sw[0:1], sw[1:2])):
        aux = jnp.where(a_row == 12 + i, line, aux)
    for i in range(NB):
        auxb[i] = aux[i * 16 : (i + 1) * 16]
    four = onehot((iota((16, 128), 0) == iota((16, 128), 1)) & (iota((16, 128), 0) < 4))

    def s4_copy(i, j):
        ob, oyc = lax.rem(b + i, NB), lax.rem(yc + j, 4)
        return remote(
            gs.at[ob, oyc],
            r4.at[yc, b],
            s4_ssem.at[i * 4 + j],
            s4_rsem.at[i * 4 + j],
            dev(lax.div(oyc, 2), z, lax.rem(oyc, 2), ob),
        )

    def s5_copy(i):
        ob = lax.rem(b + i, NB)
        return remote(auxs.at[ob], r5.at[b], s5_ssem.at[i], s5_rsem.at[i], dev(y, z, c, ob))

    def serve(pair):
        g = (served[pair] + share(pair, 1 - y)).astype(BF16)
        for u in range(2):
            quads = g[u * 4 * rows : (u + 1) * 4 * rows]
            ob = 2 * pair + u
            gs[ob] = quads[:, :384].reshape(4, rows, 384)
            squares4 = quads[:, 384:]
            if 4 * rows < 128:
                squares4 = jnp.concatenate([squares4, jnp.zeros((128 - 4 * rows, 128), BF16)], 0)
            auxs[ob] = (auxb[ob] + dot_nt(four, squares4)).astype(BF16)

    def serve_send(step, _):
        pair = lax.rem(lax.div(b, 2) + step, NB // 2)
        serve(pair)
        for u in range(2):
            away = lax.rem(2 * pair + u - b + NB, NB)
            s5_copy(away).start()
            s4_copy(away, 1).start()
            s4_copy(away, 2).start()
        return 0

    lax.fori_loop(1, NB // 2, serve_send, 0)
    serve(lax.div(b, 2))
    sibling = lax.rem(1 - 2 * lax.rem(b, 2) + NB, NB)
    s5_copy(sibling).start()
    for j in (1, 2):
        s4_copy(sibling, j).start()
        s4_copy(0, j).start()
    lax.fori_loop(1, 4, lambda k, _: (wx_copy(k).wait_recv(), 0)[1], 0)
    wc_copy().start()
    for j in (3, 0):
        lax.fori_loop(0, NB - 1, lambda k, _: (s4_copy(lax.rem(k + 3, NB - 1) + 1, j).start(), 0)[1], 0)
        if j:
            s4_copy(0, j).start()
    r4[yc, b] = gs[b, yc]
    r5[b] = auxs[b]

    lax.fori_loop(1, NB, lambda k, _: (s5_copy(k).wait_recv(), 0)[1], 0)
    stats = r5[0].astype(F32)
    for i in range(1, NB):
        stats = stats + r5[i].astype(F32)
    l128 = iota((rows, 128), 1)
    mine = l128 == yc * rows + iota((rows, 128), 0)

    def inverse_rms(n):
        line = stats[n : n + 1] + stats[n + 2 : n + 3]
        column = jnp.sum(jnp.where(mine, jnp.broadcast_to(line, (rows, 128)), 0.0), -1, keepdims=True)
        return lax.rsqrt(column / D + EPS)

    scale0, scale1 = inverse_rms(0), inverse_rms(1)
    scale_ab = jnp.where(l128 < 96, scale0, scale1)


    def silu(v):
        return v / (1.0 + jnp.exp(-v))

    mr, mc = iota((nz * 16, 2 * rows), 0), iota((nz * 16, 2 * rows), 1)
    m_in = mr % 4
    m_src = (m_in % 2) * rows + (mr // 16) * 2 + m_in // 2
    spread = [onehot((mc == m_src) & ((mr // 4) % 4 == j)) for j in range(4)]

    def hidden(g):
        acc = r4[g, 0].astype(F32)
        for i in range(1, NB):
            acc = acc + r4[g, i].astype(F32)
        h_ab = silu(acc[:, :128] * scale_ab) * (acc[:, 128:256] * scale_ab)
        last = acc[:, 256:] * scale1
        h_c = silu(last) * pltpu.roll(last, 64, 1)
        h_one = jnp.where(l128 < 32, pltpu.roll(h_ab, 32, 1), pltpu.roll(h_c, 32, 1))
        return jnp.concatenate([h_ab, h_one], 0).astype(BF16)

    wc_copy().wait_recv()
    left = jnp.zeros((nz * 16, FB), F32)
    right = jnp.zeros((nz * 16, FB), F32)
    for j in (1, 2, 3, 0):
        lax.fori_loop(0 if j else 1, NB, lambda k, _: (s4_copy(k, j).wait_recv(), 0)[1], 0)
        g = lax.rem(yc - j + 4, 4)
        hid = hidden(g)
        for i in range(4):
            lhs = dot(spread[i], hid).astype(BF16)[:, :HOLD]
            left = left + dot(lhs, wbuf[lax.div(g, 2), lax.rem(g, 2), i // 2, 2 * (i % 2)])
            right = right + dot(lhs, wbuf[lax.div(g, 2), lax.rem(g, 2), i // 2, 2 * (i % 2) + 1])
    ms[:, :, :FB] = left.astype(BF16).reshape(nz, 16, FB)
    ms[:, :, FB:] = right.astype(BF16).reshape(nz, 16, FB)

    def s6_copy(src, step, slot):
        return remote(src, r6.at[slot], s6_ssem.at[slot], s6_rsem.at[slot], dev(y, lax.rem(z + step + nz, nz), c, b))

    s6_waits = []

    def s6_send(way, dist, step, src):
        copy = s6_copy(src, way * step, (way * dist) % nz)
        copy.start()
        s6_waits.append(copy)

    for parent, kids in reversed(TREE):
        for kid in kids:
            for way in (1, -1):
                if kid <= far[way] and kid not in kids_of:
                    s6_send(way, kid, kid - parent, ms.at[lax.rem(z + way * kid + nz, nz)])

    def gathered(pick):
        return jnp.concatenate(
            [jnp.concatenate([pick(2 * j), pick(2 * j + 1)], 1) for j in range(4)], 0
        )

    got = [r5[i].astype(F32) for i in range(NB)]
    resid4 = gathered(lambda i: jnp.concatenate([got[i][4:8], got[i][8:12]], 1))
    weight4 = gathered(
        lambda i: jnp.broadcast_to(
            jnp.concatenate([got[i][12:13] * got[i][14:15], got[i][13:14] * got[i][15:16]], 1), (4, FB)
        )
    )

    def s6_sum(way, kids, acc):
        for kid in kids:
            if kid <= far[way]:
                slot = (way * kid) % nz
                s6_copy(ms.at[z], 0, slot).wait_recv()
                acc = acc + r6[slot].astype(F32)
        return acc

    for at, (parent, kids) in reversed(list(enumerate(TREE[1:]))):
        for way in (1, -1):
            if parent <= far[way]:
                share = ms[lax.rem(z + way * parent + nz, nz)].astype(F32)
                ags[(1 - way) // 2, at] = s6_sum(way, kids, share).astype(BF16)
                s6_send(way, parent, parent, ags.at[(1 - way) // 2, at])
    moved = resid4 + ms[z].astype(F32)
    moved = s6_sum(-1, TREE[0][1][::-1], s6_sum(1, TREE[0][1][::-1], moved))
    ss = jnp.sum(moved * moved, -1, keepdims=True)
    st = jnp.sum(moved * weight4, -1, keepdims=True)
    ss = ss[0:4] + ss[4:8] + ss[8:12] + ss[12:16]
    st = st[0:4] + st[4:8] + st[8:12] + st[12:16]
    score = jnp.broadcast_to(st * lax.rsqrt(ss / D + EPS), (4, FB))
    for i in range(NB):
        j, half = i // 2, i % 2
        fs[i] = jnp.concatenate([moved[4 * j : 4 * j + 4, half * FB : (half + 1) * FB], score], 0)

    def s7_copy(k):
        other = lax.rem(b + k, NB)
        return remote(fs.at[other], r7.at[b], s7_ssem.at[k], s7_rsem.at[k], dev(y, z, c, other))

    lax.fori_loop(1, NB, lambda k, _: (s7_copy(k).start(), 0)[1], 0)
    r7[b] = fs[b]

    lax.fori_loop(1, 4, lambda k, _: (wy_copy(k).wait_send(), 0)[1], 0)
    lax.fori_loop(1, 4, lambda k, _: (wx_copy(k).wait_send(), 0)[1], 0)
    wc_copy().wait_send()
    lax.fori_loop(1, NB, lambda k, _: (s2_copy(k).wait_send(), 0)[1], 0)
    for copy in z_waits + y_waits:
        copy.wait_send()
    c_copy(0).wait_send()
    c_copy(1).wait_send()
    lax.fori_loop(1, 32, lambda k, _: (s4_copy(lax.div(k, 4), lax.rem(k, 4)).wait_send(), 0)[1], 0)
    lax.fori_loop(1, NB, lambda k, _: (s5_copy(k).wait_send(), 0)[1], 0)
    for copy in s6_waits:
        copy.wait_send()

    lax.fori_loop(1, NB, lambda k, _: (s7_copy(k).wait_recv(), 0)[1], 0)
    out_ref[...] = r7[...]
    lax.fori_loop(1, NB, lambda k, _: (s7_copy(k).wait_send(), 0)[1], 0)


def finish(parts_ref, out_ref, score_ref):
    out_ref[...] = jnp.concatenate([parts_ref[i, :4, :] for i in range(NB)], 0).astype(BF16)
    col = jnp.concatenate([parts_ref[i, 4:, :32] for i in range(NB)], 0)
    score_ref[...] = jnp.sum(jnp.where(iota((32, 32), 0) == iota((32, 32), 1), col, 0.0), 0, keepdims=True)


def shards(
    nz,
    resid,
    queries,
    new_kv,
    prefix_pool,
    page_table,
    prompt_len,
    tail_pool,
    tail_len,
    migration,
    out_w,
    mlp_gain,
    gate_w,
    up_w,
    down_w,
    final_gain,
    score_w,
):
    conts = 4 * nz * CONT
    rows = 2 * nz
    vmem = pl.BlockSpec(memory_space=pltpu.VMEM)
    hbm = pl.BlockSpec(memory_space=pl.ANY)
    dma = pltpu.SemaphoreType.DMA
    parts = pl.pallas_call(
        functools.partial(kernel, nz),
        out_shape=jax.ShapeDtypeStruct((NB, 8, FB), F32),
        in_specs=[hbm] * 16,
        out_specs=vmem,
        scratch_shapes=[
            pltpu.VMEM((PAGES * 256, HD), BF16),
            pltpu.VMEM((CONT * 256, HD), BF16),
            pltpu.VMEM((64, HD), BF16),
            pltpu.VMEM((64, HD), BF16),
            pltpu.VMEM((1, PAGES), jnp.int32),
            pltpu.SMEM((1, 1), jnp.int32),
            pltpu.SMEM((1, CONT), jnp.int32),
            pltpu.VMEM((HOLD, FB), BF16),
            pltpu.VMEM((2 * HD, D), BF16),
            pltpu.VMEM((32, D), BF16),
            pltpu.VMEM((conts // 128, 128), jnp.int32),
            pltpu.VMEM((HOLD, FB), BF16),
            pltpu.VMEM((HOLD, FB), BF16),
            pltpu.VMEM((16, 128), BF16),
            pltpu.VMEM((2, 128), BF16),
            pltpu.VMEM((2, 128), BF16),
            pltpu.VMEM((PAGES, 256), F32),
            pltpu.VMEM((64, PAGES * 256), F32),
            pltpu.VMEM((2, 2, 2, 4, HOLD, FB), BF16),
            pltpu.VMEM((NB, 32, FB), BF16),
            pltpu.VMEM((NB - 1, 32, FB), BF16),
            pltpu.VMEM((2, 4, nz, CONT, FB), BF16),
            pltpu.VMEM((NB, 4 * rows, conts), BF16),
            pltpu.VMEM((2, 4, 128, nz * CONT), BF16),
            pltpu.VMEM((4, nz * CONT, 512), BF16),
            pltpu.VMEM((NB // 2, 8 * rows, 512), F32),
            pltpu.VMEM((NB, 4, rows, 384), BF16),
            pltpu.VMEM((4, NB, rows, 384), BF16),
            pltpu.VMEM((NB, 16, 128), F32),
            pltpu.VMEM((NB, 16, 128), BF16),
            pltpu.VMEM((NB, 16, 128), BF16),
            pltpu.VMEM((nz, 16, 512), BF16),
            pltpu.VMEM((2, len(TREE) - 1, 16, 512), BF16),
            pltpu.VMEM((nz, 16, 512), BF16),
            pltpu.VMEM((NB, 8, FB), F32),
            pltpu.VMEM((NB, 8, FB), F32),
            dma((16,)),
            dma((8,)),
            dma((8,)),
            dma((NB,)),
            dma((NB,)),
            dma((nz,)),
            dma((nz,)),
            dma((nz,)),
            dma((nz,)),
            dma((2,)),
            dma((2,)),
            dma((32,)),
            dma((32,)),
            dma((NB,)),
            dma((NB,)),
            dma((nz,)),
            dma((nz,)),
            dma((NB,)),
            dma((NB,)),
        ],
        compiler_params=pltpu.CompilerParams(
            collective_id=0, has_side_effects=True, vmem_limit_bytes=58 * 1024 * 1024
        ),
    )(
        prefix_pool.reshape(PAGES * 256, HD),
        tail_pool.reshape(CONT * 256, HD),
        queries.reshape(64, HD),
        new_kv.reshape(64, HD),
        page_table,
        prompt_len.reshape(1, 1),
        tail_len,
        down_w,
        out_w,
        resid,
        migration.reshape(conts // 128, 128),
        gate_w.T,
        up_w.T,
        mlp_gain.reshape(16, 128),
        final_gain.reshape(2, 128),
        score_w.reshape(2, 128),
    )
    out, score = pl.pallas_call(
        finish,
        out_shape=(
            jax.ShapeDtypeStruct((32, FB), BF16),
            jax.ShapeDtypeStruct((1, 32), F32),
        ),
        in_specs=[vmem],
        out_specs=(vmem, vmem),
    )(parts)
    return out, score.reshape(32)


def solution(mesh):
    nz = mesh.shape["dp"] // 4
    return jax.shard_map(
        functools.partial(shards, nz),
        mesh=mesh,
        in_specs=(
            P("dp", None),
            P("dp", "blk", None),
            P("dp", None, "blk", None),
            P("dp", None, None, "blk", None),
            P("dp", None),
            P("dp"),
            P("dp", None, None, "blk", None),
            P("dp", None),
            P(),
            P("blk", None),
            P(),
            P("blk", "dp"),
            P("blk", "dp"),
            P("dp", "blk"),
            P("blk"),
            P("blk"),
        ),
        out_specs=(P("dp", "blk"), P("dp")),
        check_vma=False,
    )
```

```python
import functools
import math

import jax
import jax.numpy as jnp
from jax import lax
from jax.experimental import pallas as pl
from jax.experimental.pallas import tpu as pltpu
from jax.sharding import PartitionSpec as P

MESH = pl.DeviceIdType.MESH
F32 = jnp.float32
BF16 = jnp.bfloat16
NEG = -1e30
EPS = 1e-06
D = 2048
NB = 8
FB = 256
HOLD = 96
CONT = 16
PAGES = 32
HD = 128
TREE = ((0, (5, 2, 1)), (2, (4, 3)), (5, (8, 7, 6)))


def iota(shape, dim):
    return lax.broadcasted_iota(jnp.int32, shape, dim)


def dot(a, b):
    return lax.dot_general(a, b, (((1,), (0,)), ((), ())), preferred_element_type=F32)


def dot_nt(a, b):
    return lax.dot_general(a, b, (((1,), (1,)), ((), ())), preferred_element_type=F32)


def onehot(cond):
    return jnp.where(cond, 1.0, 0.0).astype(BF16)


def kernel(
    nz,
    *refs,
):
    sources, out_ref, held, refs = refs[:16], refs[16], refs[17:33], refs[33:]
    (kv, tail, q_ref, new_ref, tab_ref, plen_ref, tlen_ref, down_ref, ow, resid_ref, mig_ref, gate_ref, up_ref, gain_ref, fg_ref, sw_ref) = held
    (bias, sbuf, wbuf, s2, r2, xall, perm, sel, hs, served, gs, r4, auxb, auxs, r5, ms, ags, r6, fs, r7, load_sem, w_ssem, w_rsem, s2_ssem, s2_rsem, z_ssem, z_rsem, y_ssem, y_rsem, c_ssem, c_rsem, s4_ssem, s4_rsem, s5_ssem, s5_rsem, s6_ssem, s6_rsem, s7_ssem, s7_rsem) = refs
    dp = lax.axis_index("dp")
    b = lax.axis_index("blk")
    c = lax.rem(dp, 2)
    z = lax.rem(lax.div(dp, 2), nz)
    y = lax.div(dp, 2 * nz)
    yc = 2 * y + c
    x, yh = lax.rem(b, 4), lax.div(b, 4)
    conts = 4 * nz * CONT
    rows = 2 * nz

    def dev(y_, z_, c_, b_):
        return ((y_ * nz + z_) * 2 + c_, b_)

    def remote(src, dst, ssem, rsem, target):
        return pltpu.make_async_remote_copy(
            src_ref=src, dst_ref=dst, send_sem=ssem, recv_sem=rsem, device_id=target, device_id_type=MESH
        )

    barrier = pltpu.get_barrier_semaphore()

    def greet_plane(k, _):
        other = lax.rem(b * 4 + yc + k, 32)
        oyc, ob = lax.rem(other, 4), lax.div(other, 4)
        pl.semaphore_signal(
            barrier, inc=1, device_id=dev(lax.div(oyc, 2), z, lax.rem(oyc, 2), ob), device_id_type=MESH
        )
        return 0

    def greet_line(k, _):
        pl.semaphore_signal(barrier, inc=1, device_id=dev(y, lax.rem(z + k, nz), c, b), device_id_type=MESH)
        return 0

    loads = [pltpu.make_async_copy(sources[i], held[i], load_sem.at[i]) for i in range(16)]
    piece = PAGES * 64
    kv_loads = [
        pltpu.make_async_copy(
            sources[0].at[pl.ds(i * piece, piece)], held[0].at[pl.ds(i * piece, piece)], load_sem.at[16 + i]
        )
        for i in range(4)
    ]
    for load in loads[2:8] + kv_loads + loads[1:2] + loads[8:]:
        load.start()

    lax.fori_loop(1, 32, greet_plane, 0)
    lax.fori_loop(1, nz, greet_line, 0)

    for load in loads[2:8]:
        load.wait()

    wbuf[y, c, yh, x] = down_ref[...]
    row4 = y * 2 + yh

    def wy_copy(k):
        other = lax.rem(row4 + k, 4)
        piece = wbuf.at[y, c, yh, x]
        return remote(piece, piece, w_ssem.at[k], w_rsem.at[k], dev(lax.div(other, 2), z, c, lax.rem(other, 2) * 4 + x))

    def wx_copy(k):
        piece = wbuf.at[:, c, :, x]
        return remote(piece, piece, w_ssem.at[3 + k], w_rsem.at[3 + k], dev(y, z, c, yh * 4 + lax.rem(x + k, 4)))

    def wc_copy():
        piece = wbuf.at[:, c]
        return remote(piece, piece, w_ssem.at[7], w_rsem.at[7], dev(y, z, 1 - c, b))

    r64, c64 = iota((64, 64), 0), iota((64, 64), 1)
    q_src = (r64 % 16) * 4 + ((r64 // 16) % 2) * 2 + r64 // 32
    q = dot(onehot(q_src == c64), q_ref[...]).astype(BF16)

    lane = iota((PAGES, 256), 1)
    page_no = iota((PAGES, PAGES), 0) == jnp.broadcast_to(tab_ref[...], (PAGES, PAGES))
    logical = jnp.sum(jnp.where(page_no, iota((PAGES, PAGES), 1), 0), -1, keepdims=True)
    limit = jnp.broadcast_to(plen_ref[0, 0] - logical * 128, (PAGES, 256))
    bias[...] = jnp.where((lane % 2 == 0) & (lane // 2 < limit), 0.0, NEG)
    unit = math.log2(math.e) / math.sqrt(HD)

    def widest(best, s):
        for i in range(s.shape[1] // 128):
            best = jnp.maximum(best, s[:, i * 128 : (i + 1) * 128])
        return best

    def next_lane(w):
        return jnp.concatenate(
            [pltpu.roll(w[:, i * 128 : (i + 1) * 128], 1, 1) for i in range(w.shape[1] // 128)], 1
        ).astype(BF16)

    best = jnp.full((64, 128), NEG, F32)
    for i in range(PAGES // 8):
        kv_loads[i].wait()
        s = dot_nt(q, kv[i * 2048 : (i + 1) * 2048, :])
        for u in range(8):
            l = i * 8 + u
            part = s[:, u * 256 : (u + 1) * 256] + bias[l : l + 1, :]
            sbuf[:, l * 256 : (l + 1) * 256] = part
            best = widest(best, part)
    loads[1].wait()
    owner = iota((64, 256), 0) % 16
    t_lane = iota((1, 256), 1)
    s_tail = jnp.full((64, 256), NEG, F32)
    for i in range(CONT // 8):
        s = dot_nt(q, tail[i * 2048 : (i + 1) * 2048, :])
        for u in range(8):
            t = i * 8 + u
            t_bias = jnp.where((t_lane % 2 == 0) & (t_lane // 2 < tlen_ref[0, t]), 0.0, NEG)
            s_tail = jnp.where(owner == t, s[:, u * 256 : (u + 1) * 256] + t_bias, s_tail)

    new_cont, new_tok = c64 // 4, (c64 // 2) % 2
    new_ok = (c64 % 2 == 0) & (new_cont == r64 % 16) & (new_tok <= (r64 // 16) % 2)
    s_new = jnp.where(new_ok, dot_nt(q, new_ref[...]), NEG)
    top = jnp.maximum(
        jnp.max(widest(best, s_tail), -1, keepdims=True), jnp.max(s_new, -1, keepdims=True)
    )
    w_tail = jnp.exp2((s_tail - top) * unit)
    w_new = jnp.exp2((s_new - top) * unit)
    total = w_tail[:, :128] + w_tail[:, 128:]
    mixed = dot(pltpu.roll(w_new, 1, 1).astype(BF16), new_ref[...])
    for i in range(PAGES // 8):
        w = jnp.exp2((sbuf[:, i * 2048 : (i + 1) * 2048] - top) * unit)
        for u in range(16):
            total = total + w[:, u * 128 : (u + 1) * 128]
        mixed = mixed + dot(next_lane(w), kv[i * 2048 : (i + 1) * 2048, :])
    v_tail = next_lane(w_tail)
    for i in range(CONT // 8):
        w = jnp.concatenate(
            [jnp.where(owner == i * 8 + u, v_tail, jnp.zeros_like(v_tail)) for u in range(8)], 1
        )
        mixed = mixed + dot(w, tail[i * 2048 : (i + 1) * 2048, :])
    total = jnp.sum(total, -1, keepdims=True) + jnp.sum(w_new, -1, keepdims=True)
    attn = (mixed / total).astype(BF16)

    pl.semaphore_wait(barrier, 31 + nz - 1)

    loads[8].wait()
    for i in range(NB):
        cols = slice(i * FB, (i + 1) * FB)
        s2[i] = (dot(attn[:32], ow[:HD, cols]) + dot(attn[32:], ow[HD:, cols])).astype(BF16)

    def s2_copy(k):
        other = lax.rem(b + k, NB)
        return remote(s2.at[other], r2.at[k - 1], s2_ssem.at[k], s2_rsem.at[k], dev(y, z, c, other))

    lax.fori_loop(1, NB, lambda k, _: (s2_copy(k).start(), 0)[1], 0)
    lax.fori_loop(1, 4, lambda k, _: (wy_copy(k).start(), 0)[1], 0)

    for load in loads[9:]:
        load.wait()
    mig = mig_ref[...]
    home = mig // CONT
    stored = ((home // (2 * nz) * 2 + home % 2) * nz + (home // 2) % nz) * CONT + mig % CONT
    chunk = 4 * rows
    lines = mig.shape[0]
    p_row = iota((chunk, 1), 0)
    first = ((p_row // (2 * rows)) * nz + (p_row // 2) % nz) * 32 + ((p_row // rows) % 2) * 16 + p_row % 2
    line = onehot(iota((chunk, lines), 1) == first // 128)
    spread_mig = dot(line, (stored // 32).astype(F32).astype(BF16)) * 32.0 + dot(
        line, (stored % 32).astype(F32).astype(BF16)
    )
    slot_lane = iota((chunk, 128), 1) - first % 128
    for i in range(NB):
        column = jnp.sum(jnp.where(slot_lane == 2 * i, spread_mig, 0.0), -1, keepdims=True)
        perm[i] = onehot(iota((chunk, conts), 1) == column.astype(jnp.int32))
    gains = gain_ref[...].astype(F32)
    g_row = iota((16, 128), 0)
    gain = jnp.concatenate(
        [
            jnp.sum(jnp.where(g_row == 2 * b, gains, 0.0), 0, keepdims=True),
            jnp.sum(jnp.where(g_row == 2 * b + 1, gains, 0.0), 0, keepdims=True),
        ],
        1,
    )
    gate_t = (gate_ref[...].astype(F32) * gain).astype(BF16)
    up_t = (up_ref[...].astype(F32) * gain).astype(BF16)
    none32 = jnp.zeros((32, FB), BF16)
    none96 = jnp.zeros((96, FB), BF16)
    w_first = jnp.concatenate([gate_t, none32, up_t, none32], 0)
    w_second = jnp.concatenate(
        [none96, gate_t[:32], none96, up_t[:32], gate_t[32:], up_t[32:]], 0
    )
    r32, c32 = iota((32, 32), 0), iota((32, 32), 1)
    order = onehot((r32 % 16) * 2 + r32 // 16 == c32)
    resid = dot(order, resid_ref[:, pl.ds(pl.multiple_of(b * FB, FB), FB)])

    sel_r, sel_c = iota((128, NB * rows), 0), iota((128, NB * rows), 1)
    place = sel_r % 16
    own_rows = jnp.concatenate([perm[i, pl.ds(pl.multiple_of(yc * rows, rows), rows), :] for i in range(NB)], 0)
    for n in range(2):
        picked = dot(
            onehot(
                (place >= 4)
                & (place < 12)
                & (place % 2 == n)
                & (sel_c == (sel_r // 16) * rows + z * 2 + (place // 2) % 2)
            ),
            own_rows,
        ).astype(BF16)
        for i in range(4):
            sel[n, i] = picked[:, i * nz * CONT : (i + 1) * nz * CONT]

    lax.fori_loop(1, NB, lambda k, _: (s2_copy(k).wait_recv(), 0)[1], 0)
    mid = resid + s2[b].astype(F32)
    for k in range(1, NB):
        mid = mid + r2[k - 1].astype(F32)
    xall[0, yc, z] = mid[:16].astype(BF16)
    xall[1, yc, z] = mid[16:].astype(BF16)

    def z_copy(source, step, slot):
        piece = xall.at[:, yc, source]
        return remote(piece, piece, z_ssem.at[slot], z_rsem.at[slot], dev(y, lax.rem(z + step + nz, nz), c, b))

    def y_copy(source, slot):
        piece = xall.at[:, yc, source]
        return remote(piece, piece, y_ssem.at[slot], y_rsem.at[slot], dev(1 - y, z, c, b))

    def c_copy(i):
        piece = xall.at[:, 2 * i + c]
        return remote(piece, piece, c_ssem.at[i], c_rsem.at[i], dev(y, z, 1 - c, b))

    far = {1: nz // 2, -1: (nz - 1) // 2}
    z_waits, y_waits = [], []

    def z_forward(way, parent, kids):
        source = lax.rem(z - way * parent + nz, nz)
        for kid in kids:
            if kid <= far[way]:
                copy = z_copy(source, way * (kid - parent), (way * kid) % nz)
                copy.start()
                z_waits.append(copy)

    def y_forward(way, dist):
        slot = (way * dist) % nz
        copy = y_copy(lax.rem(z - way * dist + nz, nz), slot)
        copy.start()
        y_waits.append(copy)

    for way in (1, -1):
        z_forward(way, *TREE[0])
    y_forward(1, 0)
    kids_of = dict(TREE)
    for dist in (2, 5, 1, 4, 3, 6, 7, 8):
        for way in (1, -1):
            if dist <= far[way]:
                z_copy(z, 0, (way * dist) % nz).wait_recv()
                if dist in kids_of:
                    z_forward(way, dist, kids_of[dist])
                y_forward(way, dist)
        if dist == 1:
            lax.fori_loop(1, 4, lambda k, _: (wy_copy(k).wait_recv(), 0)[1], 0)
            lax.fori_loop(1, 4, lambda k, _: (wx_copy(k).start(), 0)[1], 0)

    e_lane = iota((FB, 128), 1)
    e_first = onehot((e_lane == 0) | (e_lane == 2))
    e_second = onehot((e_lane == 1) | (e_lane == 3))

    def project(block, res):
        x0 = xall[0, block].reshape(nz * CONT, FB)
        x1 = xall[1, block].reshape(nz * CONT, FB)
        h1 = dot_nt(x1, w_second)
        hs[block, :, :256] = (dot_nt(x0, w_first) + h1[:, :256]).astype(BF16)
        hs[block, :, 256:384] = h1[:, 256:].astype(BF16)
        sq0 = (x0.astype(F32) * x0.astype(F32)).astype(BF16)
        sq1 = (x1.astype(F32) * x1.astype(F32)).astype(BF16)
        squares = dot(sq0, e_first) + dot(sq1, e_second)
        high = squares.astype(BF16).astype(F32)
        hs[block, :, 384:] = jnp.where(iota((nz * CONT, 128), 1) < 2, high, squares - high).astype(BF16)
        return res + dot(sel[0, block], x0) + dot(sel[1, block], x1)

    c_copy(y).start()
    res = project(yc, jnp.zeros((128, FB), F32))
    c_copy(y).wait_recv()
    res = project(2 * y + 1 - c, res)

    half = 2 * nz * CONT

    def share(pair, side):
        cols = pl.ds(pl.multiple_of(side * half, half), half)
        lhs = jnp.concatenate([perm[2 * pair, :, cols], perm[2 * pair + 1, :, cols]], 0)
        return dot(lhs, hs[pl.ds(2 * side, 2)].reshape(half, 512))

    def first_share(pair, _):
        served[pair] = share(pair, y)
        return 0

    lax.fori_loop(0, NB // 4, first_share, 0)
    for copy in y_waits:
        copy.wait_recv()
    c_copy(1 - y).start()
    res = project(2 * (1 - y) + c, res)
    lax.fori_loop(NB // 4, NB // 2, first_share, 0)

    c_copy(1 - y).wait_recv()
    res = project(2 * (1 - y) + 1 - c, res)

    fg = fg_ref[...].astype(F32)
    sw = sw_ref[...].astype(F32)
    a_row = iota((128, 128), 0) % 16
    aux = jnp.where(a_row < 8, res[:, :128], res[:, 128:])
    for i, line in enumerate((fg[0:1], fg[1:2], sw[0:1], sw[1:2])):
        aux = jnp.where(a_row == 12 + i, line, aux)
    for i in range(NB):
        auxb[i] = aux[i * 16 : (i + 1) * 16]
    four = onehot((iota((16, 128), 0) == iota((16, 128), 1)) & (iota((16, 128), 0) < 4))

    def s4_copy(i, j):
        ob, oyc = lax.rem(b + i, NB), lax.rem(yc + j, 4)
        return remote(
            gs.at[ob, oyc],
            r4.at[yc, b],
            s4_ssem.at[i * 4 + j],
            s4_rsem.at[i * 4 + j],
            dev(lax.div(oyc, 2), z, lax.rem(oyc, 2), ob),
        )

    def s5_copy(i):
        ob = lax.rem(b + i, NB)
        return remote(auxs.at[ob], r5.at[b], s5_ssem.at[i], s5_rsem.at[i], dev(y, z, c, ob))

    def serve(pair):
        g = (served[pair] + share(pair, 1 - y)).astype(BF16)
        for u in range(2):
            quads = g[u * 4 * rows : (u + 1) * 4 * rows]
            ob = 2 * pair + u
            gs[ob] = quads[:, :384].reshape(4, rows, 384)
            squares4 = quads[:, 384:]
            if 4 * rows < 128:
                squares4 = jnp.concatenate([squares4, jnp.zeros((128 - 4 * rows, 128), BF16)], 0)
            auxs[ob] = (auxb[ob] + dot_nt(four, squares4)).astype(BF16)

    def serve_send(step, _):
        pair = lax.rem(lax.div(b, 2) + step, NB // 2)
        serve(pair)
        for u in range(2):
            away = lax.rem(2 * pair + u - b + NB, NB)
            s5_copy(away).start()
            s4_copy(away, 1).start()
            s4_copy(away, 2).start()
        return 0

    lax.fori_loop(1, NB // 2, serve_send, 0)
    serve(lax.div(b, 2))
    sibling = lax.rem(1 - 2 * lax.rem(b, 2) + NB, NB)
    s5_copy(sibling).start()
    for j in (1, 2):
        s4_copy(sibling, j).start()
        s4_copy(0, j).start()
    lax.fori_loop(1, 4, lambda k, _: (wx_copy(k).wait_recv(), 0)[1], 0)
    wc_copy().start()
    for j in (3, 0):
        lax.fori_loop(0, NB - 1, lambda k, _: (s4_copy(lax.rem(k + 3, NB - 1) + 1, j).start(), 0)[1], 0)
        if j:
            s4_copy(0, j).start()
    r4[yc, b] = gs[b, yc]
    r5[b] = auxs[b]

    lax.fori_loop(1, NB, lambda k, _: (s5_copy(k).wait_recv(), 0)[1], 0)
    stats = r5[0].astype(F32)
    for i in range(1, NB):
        stats = stats + r5[i].astype(F32)
    l128 = iota((rows, 128), 1)
    mine = l128 == yc * rows + iota((rows, 128), 0)

    def inverse_rms(n):
        line = stats[n : n + 1] + stats[n + 2 : n + 3]
        column = jnp.sum(jnp.where(mine, jnp.broadcast_to(line, (rows, 128)), 0.0), -1, keepdims=True)
        return lax.rsqrt(column / D + EPS)

    scale0, scale1 = inverse_rms(0), inverse_rms(1)
    scale_ab = jnp.where(l128 < 96, scale0, scale1)


    def silu(v):
        return v / (1.0 + jnp.exp(-v))

    mr, mc = iota((nz * 16, 2 * rows), 0), iota((nz * 16, 2 * rows), 1)
    m_in = mr % 4
    m_src = (m_in % 2) * rows + (mr // 16) * 2 + m_in // 2
    spread = [onehot((mc == m_src) & ((mr // 4) % 4 == j)) for j in range(4)]

    def hidden(g):
        acc = r4[g, 0].astype(F32)
        for i in range(1, NB):
            acc = acc + r4[g, i].astype(F32)
        h_ab = silu(acc[:, :128] * scale_ab) * (acc[:, 128:256] * scale_ab)
        last = acc[:, 256:] * scale1
        h_c = silu(last) * pltpu.roll(last, 64, 1)
        h_one = jnp.where(l128 < 32, pltpu.roll(h_ab, 32, 1), pltpu.roll(h_c, 32, 1))
        return jnp.concatenate([h_ab, h_one], 0).astype(BF16)

    wc_copy().wait_recv()
    left = jnp.zeros((nz * 16, FB), F32)
    right = jnp.zeros((nz * 16, FB), F32)
    for j in (1, 2, 3, 0):
        lax.fori_loop(0 if j else 1, NB, lambda k, _: (s4_copy(k, j).wait_recv(), 0)[1], 0)
        g = lax.rem(yc - j + 4, 4)
        hid = hidden(g)
        for i in range(4):
            lhs = dot(spread[i], hid).astype(BF16)[:, :HOLD]
            left = left + dot(lhs, wbuf[lax.div(g, 2), lax.rem(g, 2), i // 2, 2 * (i % 2)])
            right = right + dot(lhs, wbuf[lax.div(g, 2), lax.rem(g, 2), i // 2, 2 * (i % 2) + 1])
    ms[:, :, :FB] = left.astype(BF16).reshape(nz, 16, FB)
    ms[:, :, FB:] = right.astype(BF16).reshape(nz, 16, FB)

    def s6_copy(src, step, slot):
        return remote(src, r6.at[slot], s6_ssem.at[slot], s6_rsem.at[slot], dev(y, lax.rem(z + step + nz, nz), c, b))

    s6_waits = []

    def s6_send(way, dist, step, src):
        copy = s6_copy(src, way * step, (way * dist) % nz)
        copy.start()
        s6_waits.append(copy)

    for parent, kids in reversed(TREE):
        for kid in kids:
            for way in (1, -1):
                if kid <= far[way] and kid not in kids_of:
                    s6_send(way, kid, kid - parent, ms.at[lax.rem(z + way * kid + nz, nz)])

    def gathered(pick):
        return jnp.concatenate(
            [jnp.concatenate([pick(2 * j), pick(2 * j + 1)], 1) for j in range(4)], 0
        )

    got = [r5[i].astype(F32) for i in range(NB)]
    resid4 = gathered(lambda i: jnp.concatenate([got[i][4:8], got[i][8:12]], 1))
    weight4 = gathered(
        lambda i: jnp.broadcast_to(
            jnp.concatenate([got[i][12:13] * got[i][14:15], got[i][13:14] * got[i][15:16]], 1), (4, FB)
        )
    )

    def s6_sum(way, kids, acc):
        for kid in kids:
            if kid <= far[way]:
                slot = (way * kid) % nz
                s6_copy(ms.at[z], 0, slot).wait_recv()
                acc = acc + r6[slot].astype(F32)
        return acc

    for at, (parent, kids) in reversed(list(enumerate(TREE[1:]))):
        for way in (1, -1):
            if parent <= far[way]:
                share = ms[lax.rem(z + way * parent + nz, nz)].astype(F32)
                ags[(1 - way) // 2, at] = s6_sum(way, kids, share).astype(BF16)
                s6_send(way, parent, parent, ags.at[(1 - way) // 2, at])
    moved = resid4 + ms[z].astype(F32)
    moved = s6_sum(-1, TREE[0][1][::-1], s6_sum(1, TREE[0][1][::-1], moved))
    ss = jnp.sum(moved * moved, -1, keepdims=True)
    st = jnp.sum(moved * weight4, -1, keepdims=True)
    ss = ss[0:4] + ss[4:8] + ss[8:12] + ss[12:16]
    st = st[0:4] + st[4:8] + st[8:12] + st[12:16]
    score = jnp.broadcast_to(st * lax.rsqrt(ss / D + EPS), (4, FB))
    for i in range(NB):
        j, half = i // 2, i % 2
        fs[i] = jnp.concatenate([moved[4 * j : 4 * j + 4, half * FB : (half + 1) * FB], score], 0)

    def s7_copy(k):
        other = lax.rem(b + k, NB)
        return remote(fs.at[other], r7.at[b], s7_ssem.at[k], s7_rsem.at[k], dev(y, z, c, other))

    lax.fori_loop(1, NB, lambda k, _: (s7_copy(k).start(), 0)[1], 0)
    r7[b] = fs[b]

    lax.fori_loop(1, 4, lambda k, _: (wy_copy(k).wait_send(), 0)[1], 0)
    lax.fori_loop(1, 4, lambda k, _: (wx_copy(k).wait_send(), 0)[1], 0)
    wc_copy().wait_send()
    lax.fori_loop(1, NB, lambda k, _: (s2_copy(k).wait_send(), 0)[1], 0)
    for copy in z_waits + y_waits:
        copy.wait_send()
    c_copy(0).wait_send()
    c_copy(1).wait_send()
    lax.fori_loop(1, 32, lambda k, _: (s4_copy(lax.div(k, 4), lax.rem(k, 4)).wait_send(), 0)[1], 0)
    lax.fori_loop(1, NB, lambda k, _: (s5_copy(k).wait_send(), 0)[1], 0)
    for copy in s6_waits:
        copy.wait_send()

    lax.fori_loop(1, NB, lambda k, _: (s7_copy(k).wait_recv(), 0)[1], 0)
    out_ref[...] = r7[...]
    lax.fori_loop(1, NB, lambda k, _: (s7_copy(k).wait_send(), 0)[1], 0)


def finish(parts_ref, out_ref, score_ref):
    out_ref[...] = jnp.concatenate([parts_ref[i, :4, :] for i in range(NB)], 0).astype(BF16)
    col = jnp.concatenate([parts_ref[i, 4:, :32] for i in range(NB)], 0)
    score_ref[...] = jnp.sum(jnp.where(iota((32, 32), 0) == iota((32, 32), 1), col, 0.0), 0, keepdims=True)


def shards(
    nz,
    resid,
    queries,
    new_kv,
    prefix_pool,
    page_table,
    prompt_len,
    tail_pool,
    tail_len,
    migration,
    out_w,
    mlp_gain,
    gate_w,
    up_w,
    down_w,
    final_gain,
    score_w,
):
    conts = 4 * nz * CONT
    rows = 2 * nz
    vmem = pl.BlockSpec(memory_space=pltpu.VMEM)
    hbm = pl.BlockSpec(memory_space=pl.ANY)
    dma = pltpu.SemaphoreType.DMA
    parts = pl.pallas_call(
        functools.partial(kernel, nz),
        out_shape=jax.ShapeDtypeStruct((NB, 8, FB), F32),
        in_specs=[hbm] * 16,
        out_specs=vmem,
        scratch_shapes=[
            pltpu.VMEM((PAGES * 256, HD), BF16),
            pltpu.VMEM((CONT * 256, HD), BF16),
            pltpu.VMEM((64, HD), BF16),
            pltpu.VMEM((64, HD), BF16),
            pltpu.VMEM((1, PAGES), jnp.int32),
            pltpu.SMEM((1, 1), jnp.int32),
            pltpu.SMEM((1, CONT), jnp.int32),
            pltpu.VMEM((HOLD, FB), BF16),
            pltpu.VMEM((2 * HD, D), BF16),
            pltpu.VMEM((32, D), BF16),
            pltpu.VMEM((conts // 128, 128), jnp.int32),
            pltpu.VMEM((HOLD, FB), BF16),
            pltpu.VMEM((HOLD, FB), BF16),
            pltpu.VMEM((16, 128), BF16),
            pltpu.VMEM((2, 128), BF16),
            pltpu.VMEM((2, 128), BF16),
            pltpu.VMEM((PAGES, 256), F32),
            pltpu.VMEM((64, PAGES * 256), F32),
            pltpu.VMEM((2, 2, 2, 4, HOLD, FB), BF16),
            pltpu.VMEM((NB, 32, FB), BF16),
            pltpu.VMEM((NB - 1, 32, FB), BF16),
            pltpu.VMEM((2, 4, nz, CONT, FB), BF16),
            pltpu.VMEM((NB, 4 * rows, conts), BF16),
            pltpu.VMEM((2, 4, 128, nz * CONT), BF16),
            pltpu.VMEM((4, nz * CONT, 512), BF16),
            pltpu.VMEM((NB // 2, 8 * rows, 512), F32),
            pltpu.VMEM((NB, 4, rows, 384), BF16),
            pltpu.VMEM((4, NB, rows, 384), BF16),
            pltpu.VMEM((NB, 16, 128), F32),
            pltpu.VMEM((NB, 16, 128), BF16),
            pltpu.VMEM((NB, 16, 128), BF16),
            pltpu.VMEM((nz, 16, 512), BF16),
            pltpu.VMEM((2, len(TREE) - 1, 16, 512), BF16),
            pltpu.VMEM((nz, 16, 512), BF16),
            pltpu.VMEM((NB, 8, FB), F32),
            pltpu.VMEM((NB, 8, FB), F32),
            dma((20,)),
            dma((8,)),
            dma((8,)),
            dma((NB,)),
            dma((NB,)),
            dma((nz,)),
            dma((nz,)),
            dma((nz,)),
            dma((nz,)),
            dma((2,)),
            dma((2,)),
            dma((32,)),
            dma((32,)),
            dma((NB,)),
            dma((NB,)),
            dma((nz,)),
            dma((nz,)),
            dma((NB,)),
            dma((NB,)),
        ],
        compiler_params=pltpu.CompilerParams(
            collective_id=0, has_side_effects=True, vmem_limit_bytes=58 * 1024 * 1024
        ),
    )(
        prefix_pool.reshape(PAGES * 256, HD),
        tail_pool.reshape(CONT * 256, HD),
        queries.reshape(64, HD),
        new_kv.reshape(64, HD),
        page_table,
        prompt_len.reshape(1, 1),
        tail_len,
        down_w,
        out_w,
        resid,
        migration.reshape(conts // 128, 128),
        gate_w.T,
        up_w.T,
        mlp_gain.reshape(16, 128),
        final_gain.reshape(2, 128),
        score_w.reshape(2, 128),
    )
    out, score = pl.pallas_call(
        finish,
        out_shape=(
            jax.ShapeDtypeStruct((32, FB), BF16),
            jax.ShapeDtypeStruct((1, 32), F32),
        ),
        in_specs=[vmem],
        out_specs=(vmem, vmem),
    )(parts)
    return out, score.reshape(32)


def solution(mesh):
    nz = mesh.shape["dp"] // 4
    return jax.shard_map(
        functools.partial(shards, nz),
        mesh=mesh,
        in_specs=(
            P("dp", None),
            P("dp", "blk", None),
            P("dp", None, "blk", None),
            P("dp", None, None, "blk", None),
            P("dp", None),
            P("dp"),
            P("dp", None, None, "blk", None),
            P("dp", None),
            P(),
            P("blk", None),
            P(),
            P("blk", "dp"),
            P("blk", "dp"),
            P("dp", "blk"),
            P("blk"),
            P("blk"),
        ),
        out_specs=(P("dp", "blk"), P("dp")),
        check_vma=False,
    )
```
